32 devices in a mesh: fsdp: 4 (over y, core), ctx: 2 (over x), tp: 4 (over z).
Axes of the slice: x: 2, y: 2, z: 4, core: 2. Of those that a mesh axis runs over, the one named last changes fastest.
Arguments:
- hidden_in: bfloat16 [8, 2048, 768], P('fsdp', ('ctx', 'tp')), may hold values from -6 to 6
- encoder_states: bfloat16 [8, 1500, 768], P('fsdp', 'ctx'), may hold values from -6 to 6
- segment_ids: int32 [8, 2048], P('fsdp'), may hold values from 0 to 15, never falling along the last dimension, each value on 1 to 448 neighbouring positions
- out_grad: bfloat16 [8, 2048, 768], P('fsdp', ('ctx', 'tp')), may hold values from -6 to 6
- norm1_gain: bfloat16 [768], P(('fsdp', 'ctx')), may hold values from 0.5 to 1.5
- norm1_bias: bfloat16 [768], P(('fsdp', 'ctx')), may hold values from -1.75 to 1.75
- norm2_gain: bfloat16 [768], P(('fsdp', 'ctx')), may hold values from 0.5 to 1.5
- norm2_bias: bfloat16 [768], P(('fsdp', 'ctx')), may hold values from -1.75 to 1.75
- norm3_gain: bfloat16 [768], P(('fsdp', 'ctx')), may hold values from 0.5 to 1.5
- norm3_bias: bfloat16 [768], P(('fsdp', 'ctx')), may hold values from -1.75 to 1.75
- self_query: bfloat16 [768, 768], P(('fsdp', 'ctx'), 'tp'), may hold values from -0.21875 to 0.21875
- self_key: bfloat16 [768, 768], P(('fsdp', 'ctx'), 'tp'), may hold values from -0.21875 to 0.21875
- self_value: bfloat16 [768, 768], P(('fsdp', 'ctx'), 'tp'), may hold values from -0.21875 to 0.21875
- self_output: bfloat16 [768, 768], P('tp', ('fsdp', 'ctx')), may hold values from -0.875 to 0.875
- cross_query: bfloat16 [768, 768], P(('fsdp', 'ctx'), 'tp'), may hold values from -0.21875 to 0.21875
- cross_key: bfloat16 [768, 768], P(('fsdp', 'ctx'), 'tp'), may hold values from -0.21875 to 0.21875
- cross_value: bfloat16 [768, 768], P(('fsdp', 'ctx'), 'tp'), may hold values from -0.21875 to 0.21875
- cross_output: bfloat16 [768, 768], P('tp', ('fsdp', 'ctx')), may hold values from -2 to 2
- fc_up: bfloat16 [768, 3072], P(('fsdp', 'ctx'), 'tp'), may hold values from -0.21875 to 0.21875
- fc_down: bfloat16 [3072, 768], P('tp', ('fsdp', 'ctx')), may hold values from -0.109375 to 0.109375
- self_query_bias: bfloat16 [12, 64], P('tp', ('fsdp', 'ctx')), may hold values from -3 to 3
- self_value_bias: bfloat16 [12, 64], P('tp', ('fsdp', 'ctx')), may hold values from -3 to 3
- cross_query_bias: bfloat16 [12, 64], P('tp', ('fsdp', 'ctx')), may hold values from -3 to 3
- cross_value_bias: bfloat16 [12, 64], P('tp', ('fsdp', 'ctx')), may hold values from -3 to 3
- up_bias: bfloat16 [12, 256], P('tp', ('fsdp', 'ctx')), may hold values from -3 to 3
- self_output_bias: bfloat16 [768], P(('fsdp', 'ctx')), may hold values from -1.75 to 1.75
- cross_output_bias: bfloat16 [768], P(('fsdp', 'ctx')), may hold values from -1.75 to 1.75
- down_bias: bfloat16 [768], P(('fsdp', 'ctx')), may hold values from -1.75 to 1.75
Outputs:
- hidden_out: bfloat16 [8, 2048, 768], P('fsdp', ('ctx', 'tp'))
- grad_hidden: float32 [8, 2048, 768], P('fsdp', ('ctx', 'tp'))
- grad_encoder: float32 [8, 1500, 768], P('fsdp', 'ctx', 'tp')
- grad_norm1_gain: float32 [768], P(('fsdp', 'ctx', 'tp'))
- grad_norm1_bias: float32 [768], P(('fsdp', 'ctx', 'tp'))
- grad_norm2_gain: float32 [768], P(('fsdp', 'ctx', 'tp'))
- grad_norm2_bias: float32 [768], P(('fsdp', 'ctx', 'tp'))
- grad_norm3_gain: float32 [768], P(('fsdp', 'ctx', 'tp'))
- grad_norm3_bias: float32 [768], P(('fsdp', 'ctx', 'tp'))
- grad_self_query: float32 [768, 768], P(('fsdp', 'ctx'), 'tp')
- grad_self_key: float32 [768, 768], P(('fsdp', 'ctx'), 'tp')
- grad_self_value: float32 [768, 768], P(('fsdp', 'ctx'), 'tp')
- grad_self_output: float32 [768, 768], P('tp', ('fsdp', 'ctx'))
- grad_cross_query: float32 [768, 768], P(('fsdp', 'ctx'), 'tp')
- grad_cross_key: float32 [768, 768], P(('fsdp', 'ctx'), 'tp')
- grad_cross_value: float32 [768, 768], P(('fsdp', 'ctx'), 'tp')
- grad_cross_output: float32 [768, 768], P('tp', ('fsdp', 'ctx'))
- grad_fc_up: float32 [768, 3072], P(('fsdp', 'ctx'), 'tp')
- grad_fc_down: float32 [3072, 768], P('tp', ('fsdp', 'ctx'))
- grad_self_query_bias: float32 [12, 64], P('tp', ('fsdp', 'ctx'))
- grad_self_value_bias: float32 [12, 64], P('tp', ('fsdp', 'ctx'))
- grad_cross_query_bias: float32 [12, 64], P('tp', ('fsdp', 'ctx'))
- grad_cross_value_bias: float32 [12, 64], P('tp', ('fsdp', 'ctx'))
- grad_up_bias: float32 [12, 256], P('tp', ('fsdp', 'ctx'))
- grad_self_output_bias: float32 [768], P(('fsdp', 'ctx', 'tp'))
- grad_cross_output_bias: float32 [768], P(('fsdp', 'ctx', 'tp'))
- grad_down_bias: float32 [768], P(('fsdp', 'ctx', 'tp'))
The draws below stay inside these ranges and needn't reach their ends.
Inputs may be any that keep to these rules, and one draw needn't show every extreme that they name: `segment_ids`: in each sequence the document numbers never fall; every one of the 16 documents holds 1 to min(448, 1024) tokens, and one holds exactly that many.
All inputs are finite; a program needn't handle non-finite values.
Results may differ from the reference program's by a relative error of at most 0.018.
Values may be sent and summed in bfloat16 or wider, within the bound.
A program may use at most 256 MiB of HBM per device.

```python
import math
import jax
import jax.numpy as jnp
import numpy as np
from jax import lax

D = 768
HEADS = 12
HEAD_DIM = 64
FF = 3072
DOC_MAX = 448
FRAMES = 1500
LEN = 2048
DOCS = 16
SEQS = 8


def strengthened(array, own_key, source, target, parts, factor):
    owner, partner = [(jnp.arange(array.shape[dim]) // (array.shape[dim] // parts)).reshape([-1 if axis == dim else 1 for axis in range(array.ndim)]) for dim in (source, target)]
    chosen = jax.random.permutation(own_key, parts)[partner]
    strong = (owner == chosen) | (owner == (partner + parts // 2) % parts)
    return jnp.where(strong, factor * array, array)


def level_of(stream_key, shape, shards, least, high):
    def one(axis_at, shards_of):
        heights = jax.random.uniform(jax.random.fold_in(jax.random.fold_in(stream_key, 6), axis_at), (shards_of,), jnp.float32, least / len(shards), high / len(shards))
        return jnp.repeat(jnp.exp(heights), shape[axis_at] // shards_of).reshape((-1,) + (1,) * (len(shape) - axis_at - 1))

    loudness = one(*shards[0])
    for cut in shards[1:]:
        loudness = loudness * one(*cut)
    return loudness


def split_up(count, total, most, slope):
    portions = [(1 << 20) // math.isqrt(grade ** slope) + 1 for grade in range(2, count + 1)]
    rest, holding = total - most - (count - 1), [1] * (count - 1)
    while rest > 0:
        candidates = [i for i in range(count - 1) if holding[i] < most]
        whole, left = sum([portions[i] for i in candidates]), rest
        for i in candidates:
            addition = min(most - holding[i], max(1, left * portions[i] // whole), rest)
            holding[i] = holding[i] + addition
            rest = rest - addition
    return np.array([most] + holding)


def ragged_sizes(key, number_of, total, reach, lean):
    if number_of == 2:
        one = jax.random.randint(key, (), max(1, total - reach), min(reach, total - 1) + 1)
        return jnp.stack([one, total - one])
    tallies = jnp.asarray(split_up(number_of, total, reach, lean), jnp.int32)
    pairs = (number_of - 1) // 2
    donor, receiver = tallies[1:1 + 2 * pairs:2], tallies[2:2 + 2 * pairs:2]
    margin = jnp.minimum(donor - 1, reach - receiver)
    moved = jax.random.randint(jax.random.fold_in(key, 1), (pairs,), 0, 1 << 20) % (margin + 1)
    tallies = tallies.at[1:1 + 2 * pairs:2].set(donor - moved).at[2:2 + 2 * pairs:2].set(receiver + moved)
    return tallies[jax.random.permutation(jax.random.fold_in(key, 2), number_of)]


def bell_draw(own_key, dims, deviation, limit, pieces=(), held_as=jnp.bfloat16):
    values = jax.random.normal(own_key, dims, jnp.float32) * deviation
    if len(pieces) > 0:
        values = level_of(own_key, dims, pieces, -0.22, 0.18) * values
    return jnp.clip(values, min=-limit, max=limit).astype(held_as)


def bell_draw_with(own_key, dims, scale, reach, cuts, heavy, kind=jnp.bfloat16):
    values = scale * jax.random.normal(own_key, dims, jnp.float32)
    if cuts:
        values = values * level_of(own_key, dims, cuts, -0.22, 0.18)
    return jnp.clip(strengthened(values, jax.random.fold_in(own_key, 3), *heavy), -reach, reach).astype(kind)


def setup_inputs(seed: int = 0) -> dict:
    key_list = jax.random.split(jax.random.key(seed), 29)
    hidden_in = bell_draw_with(key_list[0], (SEQS, LEN, D), 1.0, 6.0, ((0, 4), (1, 8)), (0, 2, 4, 2.0))
    encoder_states = bell_draw(key_list[1], (SEQS, FRAMES, D), 1.0, 6.0, ((0, 4), (1, 2)))
    segment_ids = jax.vmap(lambda own: jnp.searchsorted(jnp.cumsum(ragged_sizes(own, DOCS, LEN, min(DOC_MAX, LEN // 2), 2)), jnp.arange(LEN), side="right"))(jax.random.split(key_list[2], SEQS)).reshape((SEQS, LEN)).astype(jnp.int32)
    out_grad = bell_draw_with(key_list[3], (SEQS, LEN, D), 1.0, 6.0, ((0, 4), (1, 8)), (0, 2, 4, 2.0))
    norm1_gain = jnp.clip(1.0 + 0.1 * jax.random.normal(key_list[4], (D,), jnp.float32), 0.5, 1.5).astype(jnp.bfloat16)
    norm1_bias = bell_draw(key_list[5], (D,), 0.3, 1.75, ((0, 8),))
    norm2_gain = jnp.clip(1.0 + 0.1 * jax.random.normal(key_list[6], (D,), jnp.float32), 0.5, 1.5).astype(jnp.bfloat16)
    norm2_bias = bell_draw(key_list[7], (D,), 0.3, 1.75, ((0, 8),))
    norm3_gain = jnp.clip(1.0 + 0.1 * jax.random.normal(key_list[8], (D,), jnp.float32), 0.5, 1.5).astype(jnp.bfloat16)
    norm3_bias = bell_draw(key_list[9], (D,), 0.3, 1.75, ((0, 8),))
    self_query = bell_draw(key_list[10], (D, D), D ** -0.5, 0.21875, ((0, 8), (1, 4)))
    self_key = bell_draw(key_list[11], (D, D), D ** -0.5, 0.21875, ((0, 8), (1, 4)))
    self_value = bell_draw(key_list[12], (D, D), D ** -0.5, 0.21875, ((0, 8), (1, 4)))
    self_output = bell_draw(key_list[13], (D, D), (D // 16) ** -0.5, 0.875, ((0, 4), (1, 8)))
    cross_query = bell_draw(key_list[14], (D, D), D ** -0.5, 0.21875, ((0, 8), (1, 4)))
    cross_key = bell_draw(key_list[15], (D, D), D ** -0.5, 0.21875, ((0, 8), (1, 4)))
    cross_value = bell_draw(key_list[16], (D, D), D ** -0.5, 0.21875, ((0, 8), (1, 4)))
    cross_output = bell_draw(key_list[17], (D, D), (max(8, D // 128)) ** -0.5, 2.0, ((0, 4), (1, 8)))
    fc_up = bell_draw(key_list[18], (D, FF), D ** -0.5, 0.21875, ((0, 8), (1, 4)))
    fc_down = bell_draw(key_list[19], (FF, D), FF ** -0.5, 0.109375, ((0, 4), (1, 8)))
    self_query_bias = bell_draw(key_list[20], (HEADS, HEAD_DIM), 0.5, 3.0, ((0, 4), (1, 8)))
    self_value_bias = bell_draw(key_list[21], (HEADS, HEAD_DIM), 0.5, 3.0, ((0, 4), (1, 8)))
    cross_query_bias = bell_draw(key_list[22], (HEADS, HEAD_DIM), 0.5, 3.0, ((0, 4), (1, 8)))
    cross_value_bias = bell_draw(key_list[23], (HEADS, HEAD_DIM), 0.5, 3.0, ((0, 4), (1, 8)))
    up_bias = bell_draw(key_list[24], (HEADS, FF // HEADS), 0.5, 3.0, ((0, 4), (1, 8)))
    self_output_bias = bell_draw(key_list[25], (D,), 0.3, 1.75, ((0, 8),))
    cross_output_bias = bell_draw(key_list[26], (D,), 0.3, 1.75, ((0, 8),))
    down_bias = bell_draw(key_list[27], (D,), 0.3, 1.75, ((0, 8),))
    return {"hidden_in": hidden_in, "encoder_states": encoder_states, "segment_ids": segment_ids, "out_grad": out_grad, "norm1_gain": norm1_gain, "norm1_bias": norm1_bias, "norm2_gain": norm2_gain, "norm2_bias": norm2_bias, "norm3_gain": norm3_gain, "norm3_bias": norm3_bias, "self_query": self_query, "self_key": self_key, "self_value": self_value, "self_output": self_output, "cross_query": cross_query, "cross_key": cross_key, "cross_value": cross_value, "cross_output": cross_output, "fc_up": fc_up, "fc_down": fc_down, "self_query_bias": self_query_bias, "self_value_bias": self_value_bias, "cross_query_bias": cross_query_bias, "cross_value_bias": cross_value_bias, "up_bias": up_bias, "self_output_bias": self_output_bias, "cross_output_bias": cross_output_bias, "down_bias": down_bias}


@jax.custom_vjp
def low(v):
    return lax.optimization_barrier(v.astype(jnp.bfloat16)).astype(jnp.float32)

@jax.custom_vjp
def low_back(v):
    return v

def low_keep(v):
    return (low(v), None)

def low_pass(kept, grad):
    return (grad,)

def back_keep(v):
    return (v, None)

def back_low(kept, grad):
    return (low(grad),)
low.defvjp(low_keep, low_pass)
low_back.defvjp(back_keep, back_low)
highest = lax.Precision.HIGHEST

def layer_norm(values, gain_row, offset_row):
    centred = values - lax.optimization_barrier(jnp.mean(values, axis=-1, keepdims=True))
    spread = lax.optimization_barrier(jnp.mean(centred * centred, axis=-1, keepdims=True))
    return centred * lax.rsqrt(spread + 1e-05) * gain_row + offset_row

def gelu_exact(values):
    return 0.5 * values * (1.0 + lax.erf(values / math.sqrt(2.0)))

def matmul(left_rows, weight_matrix):
    return jnp.dot(left_rows, weight_matrix, precision=highest)

def paired(values):
    return low(low_back(values))

def attend(queries, keys_all, values_all, allowed):
    query_heads = queries.reshape(queries.shape[0], HEADS, HEAD_DIM)
    key_heads = keys_all.reshape(keys_all.shape[0], HEADS, HEAD_DIM)
    value_heads = values_all.reshape(values_all.shape[0], HEADS, HEAD_DIM)
    scores = low_back(jnp.einsum('qhe,khe->hqk', query_heads, key_heads, precision=highest) * HEAD_DIM ** (-0.5))
    scores = jnp.where(allowed[None], scores, -1e+30)
    largest = lax.optimization_barrier(jnp.max(scores, axis=-1, keepdims=True))
    weights = jnp.exp(scores - largest)
    probs = weights / lax.optimization_barrier(jnp.sum(weights, axis=-1, keepdims=True))
    mixed = jnp.einsum('hqk,khe->qhe', low(probs), value_heads, precision=highest)
    return paired(mixed.reshape(queries.shape[0], HEADS * HEAD_DIM))

def forward(inputs, frames, segments, params):
    gain_one, bias_one, gain_two, bias_two, gain_three, bias_three, w_query, w_key, w_value, w_output, w_cross_query, w_cross_key, w_cross_value, w_cross_output, w_up, w_down, bias_query, bias_value, bias_cross_query, bias_cross_value, bias_up, bias_output, bias_cross_output, bias_down = params
    places = jnp.arange(segments.shape[0], dtype=jnp.int32)
    allowed = (segments[:, None] == segments[None, :]) & (places[None, :] <= places[:, None])
    frame_docs = jnp.arange(frames.shape[0], dtype=jnp.int32) % DOCS
    cross_allowed = segments[:, None] == frame_docs[None, :]
    tokens_one = low(layer_norm(inputs, gain_one, bias_one))
    queries = paired(matmul(tokens_one, w_query) + bias_query.reshape(-1))
    keys_own = paired(matmul(tokens_one, w_key))
    values_own = paired(matmul(tokens_one, w_value) + bias_value.reshape(-1))
    self_mixed = attend(queries, keys_own, values_own, allowed)
    first_sum = inputs + low_back(matmul(self_mixed, w_output) + bias_output)
    tokens_two = low(layer_norm(first_sum, gain_two, bias_two))
    cross_queries = paired(matmul(tokens_two, w_cross_query) + bias_cross_query.reshape(-1))
    cross_keys = paired(matmul(frames, w_cross_key))
    cross_values = paired(matmul(frames, w_cross_value) + bias_cross_value.reshape(-1))
    cross_mixed = attend(cross_queries, cross_keys, cross_values, cross_allowed)
    second_sum = first_sum + low_back(matmul(cross_mixed, w_cross_output) + bias_cross_output)
    tokens_three = low(layer_norm(second_sum, gain_three, bias_three))
    hidden_pre = low_back(matmul(tokens_three, w_up) + bias_up.reshape(-1))
    activated = low(gelu_exact(hidden_pre))
    return second_sum + low_back(matmul(activated, w_down) + bias_down)

def add_pair(first_term, second_term):
    return first_term + second_term

def reference(hidden_in, encoder_states, segment_ids, out_grad, norm1_gain, norm1_bias, norm2_gain, norm2_bias, norm3_gain, norm3_bias, self_query, self_key, self_value, self_output, cross_query, cross_key, cross_value, cross_output, fc_up, fc_down, self_query_bias, self_value_bias, cross_query_bias, cross_value_bias, up_bias, self_output_bias, cross_output_bias, down_bias):
    params = tuple((argument.astype(jnp.float32) for argument in (norm1_gain, norm1_bias, norm2_gain, norm2_bias, norm3_gain, norm3_bias, self_query, self_key, self_value, self_output, cross_query, cross_key, cross_value, cross_output, fc_up, fc_down, self_query_bias, self_value_bias, cross_query_bias, cross_value_bias, up_bias, self_output_bias, cross_output_bias, down_bias)))

    def one_sequence(totals, item):
        inputs, frames, segments, cotangent = item

        def forward_of(input_rows, frame_rows, weights_all):
            return forward(input_rows, frame_rows, segments, weights_all)
        result, pull = jax.vjp(forward_of, inputs, frames, params)
        input_grad, frame_grad, param_grads = pull(cotangent)
        totals = jax.tree.map(add_pair, totals, param_grads)
        return (totals, (result.astype(jnp.bfloat16), input_grad, frame_grad))
    zeros = jax.tree.map(jnp.zeros_like, params)
    totals, results = lax.scan(one_sequence, zeros, (hidden_in.astype(jnp.float32), encoder_states.astype(jnp.float32), segment_ids, out_grad.astype(jnp.float32)))
    return (results[0], results[1], results[2], totals[0], totals[1], totals[2], totals[3], totals[4], totals[5], totals[6], totals[7], totals[8], totals[9], totals[10], totals[11], totals[12], totals[13], totals[14], totals[15], totals[16], totals[17], totals[18], totals[19], totals[20], totals[21], totals[22], totals[23])
```

```python
import functools
import math

import jax
import jax.numpy as jnp
from jax import lax
from jax.experimental import pallas as pl
from jax.experimental.pallas import tpu as pltpu
from jax.sharding import PartitionSpec as P

HEAD_DIM = 64
DOCS = 16
EPSILON = 1e-05
MASKED = -1e30
SCALE = HEAD_DIM ** (-0.5)
QT = 128

f32 = jnp.float32
bf16 = jnp.bfloat16

VMEM_LIMIT = 62 * 1024 * 1024


def nn(a, b):
    return lax.dot_general(a, b, (((1,), (0,)), ((), ())), preferred_element_type=f32)


def nt(a, b):
    return lax.dot_general(a, b, (((1,), (1,)), ((), ())), preferred_element_type=f32)


def tn(a, b):
    return lax.dot_general(a, b, (((0,), (0,)), ((), ())), preferred_element_type=f32)


def norm_parts(values):
    centred = values - jnp.mean(values, axis=-1, keepdims=True)
    rate = lax.rsqrt(jnp.mean(centred * centred, axis=-1, keepdims=True) + EPSILON)
    return centred * rate, rate


def norm_back(z, rate, gain, grad):
    scaled = gain * grad
    return rate * (
        scaled
        - jnp.mean(scaled, axis=-1, keepdims=True)
        - z * jnp.mean(scaled * z, axis=-1, keepdims=True)
    )


def row_sum(values):
    return jnp.sum(values, axis=0, keepdims=True)


def self_scores(kw, qn, masked_add):
    return nt(kw, qn) + masked_add


def window_mask(segk_ref, segq_ref, n, halo, window):
    keys = segk_ref[pl.ds(n * QT, window), :]
    same = keys == segq_ref[n]
    ahead = lax.broadcasted_iota(jnp.int32, (window, QT), 0) - lax.broadcasted_iota(
        jnp.int32, (window, QT), 1
    )
    return jnp.where(same & (ahead <= halo), 0.0, MASKED)


def fwd1_kernel(
    xa_ref, g1_ref, gain_ref, bias_ref, pb_ref, segk_ref, segq_ref, a1_ref, qkv_ref, o_ref, lse_ref
):
    rows = xa_ref.shape[0]
    own = segq_ref.shape[0] * QT
    halo = rows - own
    window = halo + QT
    hw = o_ref.shape[2]
    tile = 256

    @pl.when(pl.program_id(0) == 0)
    def _():
        def body(i, _):
            at = pl.ds(i * tile, tile)
            z, _ = norm_parts(xa_ref[at, :].astype(f32))
            a1_ref[at, :] = (z * gain_ref[...] + bias_ref[...]).astype(bf16)
            return 0

        lax.fori_loop(0, rows // tile, body, 0)

    w = g1_ref[0, :, : 3 * hw]

    def project(i, _):
        at = pl.ds(i * tile, tile)
        qkv_ref[0, at, :] = (nn(a1_ref[at, :], w) + pb_ref[0]).astype(bf16)
        return 0

    lax.fori_loop(0, rows // tile, project, 0)

    def attend(n, _):
        add = window_mask(segk_ref, segq_ref, n, halo, window)
        block = qkv_ref[0, pl.ds(n * QT, window), :]
        outs = []
        for i in range(hw // HEAD_DIM):
            kw = block[:, hw + i * HEAD_DIM : hw + (i + 1) * HEAD_DIM]
            vw = block[:, 2 * hw + i * HEAD_DIM : 2 * hw + (i + 1) * HEAD_DIM]
            qn = block[halo:, i * HEAD_DIM : (i + 1) * HEAD_DIM] * bf16(SCALE)
            scores = self_scores(kw, qn, add)
            top = jnp.max(scores, axis=0, keepdims=True)
            weights = jnp.exp(scores - top)
            total = jnp.sum(weights, axis=0, keepdims=True)
            mixed = tn(vw, weights.astype(bf16)) / total
            outs.append(mixed)
            lse_ref[0, n, i : i + 1, :] = top + jnp.log(total)
        o_ref[0, pl.ds(n * QT, QT), :] = jnp.concatenate(outs, axis=0).T.astype(bf16)
        return 0

    lax.fori_loop(0, own // QT, attend, 0)


def fwd2_kernel(
    span_ref, g2_ref, ep_ref, xo_ref, o_ref, vec_ref, cb_ref, kb_ref, segq_ref, count_ref,
    ckv_ref, r1_ref, a2_ref, cq_ref, co_ref, lse_ref, r2_ref, a3_ref, acc_ref,
):
    groups = g2_ref.shape[0]
    own = xo_ref.shape[0]
    hw = o_ref.shape[2]
    slots = ep_ref.shape[0]
    per_doc = slots // DOCS
    heads = hw // HEAD_DIM
    tile = 256

    for t in range(groups):

        def frames(i, _):
            at = pl.ds(i * tile, tile)
            y = nn(ep_ref[at, :], g2_ref[t, :, 2 * hw : 4 * hw]) + kb_ref[t]
            ckv_ref[t, at, :] = y.astype(bf16)
            return 0

        lax.fori_loop(0, slots // tile, frames, 0)

    def middle(i, _):
        at = pl.ds(i * tile, tile)
        r1 = xo_ref[at, :].astype(f32) + vec_ref[0:1, :]
        for t in range(groups):
            r1 = r1 + nt(o_ref[t, at, :], g2_ref[t, :, 0:hw])
        r1_ref[at, :] = r1
        z, _ = norm_parts(r1)
        a2 = (z * vec_ref[1:2, :] + vec_ref[2:3, :]).astype(bf16)
        a2_ref[at, :] = a2
        for t in range(groups):
            cq_ref[t, at, :] = (nn(a2, g2_ref[t, :, 4 * hw : 5 * hw]) + cb_ref[t]).astype(bf16)
        return 0

    lax.fori_loop(0, own // tile, middle, 0)

    acc_ref[...] = jnp.zeros_like(acc_ref)
    lse_ref[...] = jnp.zeros_like(lse_ref)
    place = lax.broadcasted_iota(jnp.int32, (per_doc, QT), 0).astype(f32)

    def attend(n, _):
        segs = segq_ref[n]

        def document(d, _):
            mine = segs == d.astype(f32)
            col = jnp.where(mine, 1.0, 0.0)
            add = jnp.where(place < count_ref[d], 0.0, MASKED)
            for t in range(groups):
                kv = ckv_ref[t, pl.ds(d * per_doc, per_doc), :]
                qs = cq_ref[t, pl.ds(n * QT, QT), :] * bf16(SCALE)
                for i in range(heads):
                    lane = slice(i * HEAD_DIM, (i + 1) * HEAD_DIM)
                    vlane = slice(hw + i * HEAD_DIM, hw + (i + 1) * HEAD_DIM)
                    scores = nt(kv[:, lane], qs[:, lane]) + add
                    top = jnp.max(scores, axis=0, keepdims=True)
                    weights = jnp.exp(scores - top)
                    total = jnp.sum(weights, axis=0, keepdims=True)
                    mixed = tn(kv[:, vlane], weights.astype(bf16)) * (col / total)
                    acc_ref[n, t, lane, :] += mixed
                    lse_ref[t, n, i : i + 1, :] += col * (top + jnp.log(total))
            return 0

        lax.fori_loop(span_ref[2 * n], span_ref[2 * n + 1] + 1, document, 0)
        for t in range(groups):
            co_ref[t, pl.ds(n * QT, QT), :] = acc_ref[n, t].T.astype(bf16)
        return 0

    lax.fori_loop(0, own // QT, attend, 0)

    def final(i, _):
        at = pl.ds(i * tile, tile)
        r2 = r1_ref[at, :] + vec_ref[3:4, :]
        for t in range(groups):
            r2 = r2 + nt(co_ref[t, at, :], g2_ref[t, :, hw : 2 * hw])
        r2_ref[at, :] = r2
        z, _ = norm_parts(r2)
        a3_ref[at, :] = (z * vec_ref[4:5, :] + vec_ref[5:6, :]).astype(bf16)
        return 0

    lax.fori_loop(0, own // tile, final, 0)


def ff_kernel(
    a3_ref, r2_ref, dy_ref, g3_ref, ub_ref, vec_ref,
    out_ref, dr2_ref, gr3_ref, ubg_ref, vecg_ref,
    a3t_ref, dmt_ref, acc_ref, acd_ref, gs_ref, dus_ref,
):
    t = pl.program_id(0)
    own, width = a3_ref.shape
    units = ub_ref.shape[2]
    tile = 256

    @pl.when(t == 0)
    def _():
        a3t_ref[...] = a3_ref[...].T
        dmt_ref[...] = dy_ref[...].T
        acc_ref[...] = jnp.zeros_like(acc_ref)
        acd_ref[...] = jnp.zeros_like(acd_ref)

    ubg_ref[...] = jnp.zeros_like(ubg_ref)
    up = g3_ref[0, :, :units]
    down = g3_ref[0, :, units:]

    def rows(i, _):
        at = pl.ds(i * tile, tile)
        u = nn(a3_ref[at, :], up) + ub_ref[0]
        phi = 0.5 + 0.5 * lax.erf(u * (1.0 / math.sqrt(2.0)))
        g = (u * phi).astype(bf16)
        gs_ref[at, :] = g
        slope = phi + u * (jnp.exp(-0.5 * u * u) * (1.0 / math.sqrt(2.0 * math.pi)))
        du = (nn(dy_ref[at, :], down) * slope).astype(bf16)
        dus_ref[at, :] = du
        ubg_ref[0] += row_sum(du.astype(f32))
        acc_ref[at, :] += nt(g, down)
        acd_ref[at, :] += nt(du, up)
        return 0

    lax.fori_loop(0, own // tile, rows, 0)

    def grads(i, _):
        at = pl.ds(i * tile, tile)
        gr3_ref[0, at, :units] = nn(a3t_ref[at, :], dus_ref[...]).astype(bf16)
        gr3_ref[0, at, units:] = nn(dmt_ref[at, :], gs_ref[...]).astype(bf16)
        return 0

    lax.fori_loop(0, width // tile, grads, 0)

    @pl.when(t == pl.num_programs(0) - 1)
    def _():
        vecg_ref[...] = jnp.zeros_like(vecg_ref)

        def finish(i, _):
            at = pl.ds(i * tile, tile)
            r2 = r2_ref[at, :]
            dy = dy_ref[at, :].astype(f32)
            out_ref[at, :] = (r2 + (acc_ref[at, :] + vec_ref[1:2, :])).astype(bf16)
            z, rate = norm_parts(r2)
            da = acd_ref[at, :]
            dr2_ref[at, :] = dy + norm_back(z, rate, vec_ref[0:1, :], da)
            vecg_ref[0:1, :] += row_sum(da * z)
            vecg_ref[1:2, :] += row_sum(da)
            vecg_ref[2:3, :] += row_sum(dy)
            return 0

        lax.fori_loop(0, own // tile, finish, 0)


def bwd2_kernel(
    span_ref, g2_ref, ep_ref, dr2_ref, cq_ref, ckv_ref, co_ref, lse_ref, a2_ref, r1_ref, o_ref,
    vec_ref, segq_ref, count_ref,
    dr1_ref, do_ref, gr2_ref, de_ref, vecg_ref, hbg_ref,
    dco_ref, dcq_ref, dkv_ref, low_ref, rowt_ref, ept_ref, acc_ref,
):
    groups, width = g2_ref.shape[0], g2_ref.shape[1]
    own = dr2_ref.shape[0]
    hw = o_ref.shape[2]
    slots = ep_ref.shape[0]
    per_doc = slots // DOCS
    heads = hw // HEAD_DIM
    tile = 256

    vecg_ref[...] = jnp.zeros_like(vecg_ref)
    hbg_ref[...] = jnp.zeros_like(hbg_ref)

    for i in range(own // tile):
        at = slice(i * tile, (i + 1) * tile)
        dc = dr2_ref[at, :].astype(bf16)
        vecg_ref[2:3, :] += row_sum(dc.astype(f32))
        rowt_ref[:, at] = dc.T
        for t in range(groups):
            dco_ref[t, at, :] = nn(dc, g2_ref[t, :, hw : 2 * hw]).astype(bf16)

    for t in range(groups):
        gr2_ref[t, :, hw : 2 * hw] = nn(rowt_ref[...], co_ref[t]).astype(bf16)

    dkv_ref[...] = jnp.zeros_like(dkv_ref)
    place = lax.broadcasted_iota(jnp.int32, (per_doc, QT), 0).astype(f32)

    def attend(n, _):
        segs = segq_ref[n]
        acc_ref[...] = jnp.zeros_like(acc_ref)

        def document(d, _):
            keep = (segs == d.astype(f32)) & (place < count_ref[d])
            add = jnp.where(keep, 0.0, MASKED)
            for t in range(groups):
                kv = ckv_ref[t, pl.ds(d * per_doc, per_doc), :]
                qs = cq_ref[t, pl.ds(n * QT, QT), :] * bf16(SCALE)
                dos = dco_ref[t, pl.ds(n * QT, QT), :]
                inner = (dos.astype(f32) * co_ref[t, pl.ds(n * QT, QT), :].astype(f32)).T
                dks, dvs = [], []
                for i in range(heads):
                    lane = slice(i * HEAD_DIM, (i + 1) * HEAD_DIM)
                    vlane = slice(hw + i * HEAD_DIM, hw + (i + 1) * HEAD_DIM)
                    scores = nt(kv[:, lane], qs[:, lane]) + add
                    probs = jnp.exp(scores - lse_ref[t, n, i : i + 1, :])
                    delta = row_sum(inner[lane, :])
                    grad = nt(kv[:, vlane], dos[:, lane])
                    ds = (probs * (grad - delta)).astype(bf16)
                    dvs.append(nn(probs.astype(bf16), dos[:, lane]))
                    dks.append(nn(ds, qs[:, lane]))
                    acc_ref[t, lane, :] += tn(kv[:, lane], ds)
                dkv_ref[t, pl.ds(d * per_doc, per_doc), :] += jnp.concatenate(dks + dvs, axis=1)
            return 0

        lax.fori_loop(span_ref[2 * n], span_ref[2 * n + 1] + 1, document, 0)
        for t in range(groups):
            dcq_ref[t, pl.ds(n * QT, QT), :] = (acc_ref[t].T * SCALE).astype(bf16)
        return 0

    lax.fori_loop(0, own // QT, attend, 0)

    for i in range(own // tile):
        at = slice(i * tile, (i + 1) * tile)
        da = jnp.zeros((tile, width), f32)
        for t in range(groups):
            da = da + nt(dcq_ref[t, at, :], g2_ref[t, :, 4 * hw : 5 * hw])
        z, rate = norm_parts(r1_ref[at, :])
        dr1 = dr2_ref[at, :] + norm_back(z, rate, vec_ref[0:1, :], da)
        dr1_ref[at, :] = dr1
        vecg_ref[0:1, :] += row_sum(da * z)
        vecg_ref[1:2, :] += row_sum(da)
        rowt_ref[:, at] = a2_ref[at, :].T

    for t in range(groups):
        gr2_ref[t, :, 4 * hw : 5 * hw] = nn(rowt_ref[...], dcq_ref[t]).astype(bf16)
        hbg_ref[t, 0:1, :] = row_sum(dcq_ref[t].astype(f32))

    for i in range(own // tile):
        at = slice(i * tile, (i + 1) * tile)
        ds = dr1_ref[at, :].astype(bf16)
        vecg_ref[3:4, :] += row_sum(ds.astype(f32))
        rowt_ref[:, at] = ds.T
        for t in range(groups):
            do_ref[t, at, :] = nn(ds, g2_ref[t, :, 0:hw]).astype(bf16)

    for t in range(groups):
        gr2_ref[t, :, 0:hw] = nn(rowt_ref[...], o_ref[t]).astype(bf16)

    for i in range(slots // tile):
        at = slice(i * tile, (i + 1) * tile)
        ept_ref[:, at] = ep_ref[at, :].T

    for t in range(groups):

        def lower(i, _):
            at = pl.ds(i * tile, tile)
            low = dkv_ref[t, at, :].astype(bf16)
            low_ref[t, at, :] = low
            hbg_ref[t, 1:2, :] += row_sum(low[:, hw:].astype(f32))
            return 0

        lax.fori_loop(0, slots // tile, lower, 0)

    def frame_grads(i, _):
        at = pl.ds(i * tile, tile)
        total = jnp.zeros((tile, width), f32)
        for t in range(groups):
            total = total + nt(low_ref[t, at, :], g2_ref[t, :, 2 * hw : 4 * hw])
        de_ref[at, :] = total.astype(bf16)
        return 0

    lax.fori_loop(0, slots // tile, frame_grads, 0)

    def key_grads(t, _):
        gr2_ref[t, :, 2 * hw : 4 * hw] = nn(ept_ref[...], low_ref[t]).astype(bf16)
        return 0

    lax.fori_loop(0, groups, key_grads, 0)


def bwd1_kernel(
    xa_ref, a1_ref, g1_ref, qkv_ref, o_ref, do_ref, lse_ref, segk_ref, segq_ref,
    da_ref, dh_ref, gr1_ref, vecg_ref, hbg_ref,
    a1t_ref, acc_ref, dk_ref, dv_ref, dq_ref, low_ref,
):
    t = pl.program_id(0)
    rows, width = xa_ref.shape
    own = segq_ref.shape[0] * QT
    halo = rows - own
    window = halo + QT
    hw = o_ref.shape[2]
    tile = 256

    @pl.when(t == 0)
    def _():
        for i in range(rows // tile):
            at = slice(i * tile, (i + 1) * tile)
            a1t_ref[:, at] = a1_ref[at, :].T
        acc_ref[...] = jnp.zeros_like(acc_ref)
        low_ref[0:halo, 0:hw] = jnp.zeros((halo, hw), bf16)

    dk_ref[...] = jnp.zeros_like(dk_ref)
    dv_ref[...] = jnp.zeros_like(dv_ref)

    def attend(n, _):
        add = window_mask(segk_ref, segq_ref, n, halo, window)
        at = pl.ds(n * QT, window)
        mine = pl.ds(n * QT, QT)
        block = qkv_ref[0, at, :]
        dos = do_ref[0, mine, :]
        inner = (dos.astype(f32) * o_ref[0, mine, :].astype(f32)).T
        dks, dvs, dqs = [], [], []
        for i in range(hw // HEAD_DIM):
            lane = slice(i * HEAD_DIM, (i + 1) * HEAD_DIM)
            kw = block[:, hw + i * HEAD_DIM : hw + (i + 1) * HEAD_DIM]
            vw = block[:, 2 * hw + i * HEAD_DIM : 2 * hw + (i + 1) * HEAD_DIM]
            qn = block[halo:, lane] * bf16(SCALE)
            scores = self_scores(kw, qn, add)
            probs = jnp.exp(scores - lse_ref[0, n, i : i + 1, :])
            delta = row_sum(inner[lane, :])
            grad = nt(vw, dos[:, lane])
            ds = (probs * (grad - delta)).astype(bf16)
            dvs.append(nn(probs.astype(bf16), dos[:, lane]))
            dks.append(nn(ds, qn))
            dqs.append(tn(kw, ds))
        dk_ref[at, :] += jnp.concatenate(dks, axis=1)
        dv_ref[at, :] += jnp.concatenate(dvs, axis=1)
        dq_ref[mine, :] = (jnp.concatenate(dqs, axis=0).T * SCALE).astype(bf16)
        return 0

    lax.fori_loop(0, own // QT, attend, 0)
    low_ref[halo:, 0:hw] = dq_ref[...]
    low_ref[:, hw : 2 * hw] = dk_ref[...].astype(bf16)
    low_ref[:, 2 * hw : 3 * hw] = dv_ref[...].astype(bf16)
    hbg_ref[...] = jnp.zeros_like(hbg_ref)
    hbg_ref[0, 0:1, :] = row_sum(dq_ref[...].astype(f32))
    hbg_ref[0, 1:2, :] = row_sum(dv_ref[...].astype(bf16).astype(f32))
    w = g1_ref[0, :, : 3 * hw]

    def back(i, _):
        at = pl.ds(i * tile, tile)
        acc_ref[at, :] += nt(low_ref[at, :], w)
        return 0

    lax.fori_loop(0, rows // tile, back, 0)

    def grads(i, _):
        at = pl.ds(i * tile, tile)
        gr1_ref[0, at, 0 : 3 * hw] = nn(a1t_ref[at, :], low_ref[...]).astype(bf16)
        return 0

    lax.fori_loop(0, width // tile, grads, 0)

    @pl.when(t == pl.num_programs(0) - 1)
    def _():
        vecg_ref[...] = jnp.zeros_like(vecg_ref)
        dh_ref[...] = acc_ref[0:halo, :].astype(bf16)
        da_ref[...] = acc_ref[halo:, :]

        def sums(i, _):
            at = pl.ds(i * tile, tile)
            z, _ = norm_parts(xa_ref[at, :].astype(f32))
            vecg_ref[0:1, :] += row_sum(acc_ref[at, :] * z)
            vecg_ref[1:2, :] += row_sum(acc_ref[at, :])
            return 0

        lax.fori_loop(0, rows // tile, sums, 0)


def bwd0_kernel(xo_ref, da_ref, dn_ref, dr1_ref, gain_ref, out_ref):
    z, rate = norm_parts(xo_ref[...].astype(f32))
    da = da_ref[...] + dn_ref[...].astype(f32)
    out_ref[...] = (dr1_ref[...] + norm_back(z, rate, gain_ref[...], da)).astype(bf16)


def whole(shape):
    return pl.BlockSpec(shape, lambda *_: (0,) * len(shape))


def step_of(shape):
    return pl.BlockSpec((1,) + shape[1:], lambda t: (t,) + (0,) * (len(shape) - 1))


def params(dims=0):
    return pltpu.CompilerParams(
        vmem_limit_bytes=VMEM_LIMIT,
        dimension_semantics=("arbitrary",) * dims if dims else None,
    )


def cost(flops, exps, size):
    return pl.CostEstimate(flops=int(flops), transcendentals=int(exps), bytes_accessed=int(size))


def sds(shape, dtype):
    return jax.ShapeDtypeStruct(shape, dtype)


def on_device(
    hidden_in, encoder_states, segment_ids, out_grad,
    norm1_gain, norm1_bias, norm2_gain, norm2_bias, norm3_gain, norm3_bias,
    self_query, self_key, self_value, self_output,
    cross_query, cross_key, cross_value, cross_output,
    fc_up, fc_down,
    self_query_bias, self_value_bias, cross_query_bias, cross_value_bias, up_bias,
    self_output_bias, cross_output_bias, down_bias,
):
    F, C, T = lax.axis_size("fsdp"), lax.axis_size("ctx"), lax.axis_size("tp")
    batches, sub, width = hidden_in.shape
    length = segment_ids.shape[1]
    frames_own = encoder_states.shape[1]
    assert T == 2 * batches and T == 4 and F % 2 == 0 and C == 2
    own = 2 * sub
    part = width // (F * C)
    hw = self_query.shape[1]
    units = fc_up.shape[1]
    heads = self_query_bias.shape[0]
    f, x, z = lax.axis_index("fsdp"), lax.axis_index("ctx"), lax.axis_index("tp")
    core = lax.rem(f, 2)
    odd = lax.rem(z, 2)
    owner = lax.div(z, 2)
    tfc = ("tp", "fsdp", "ctx")

    def round_pairs(r):
        pairs = []
        for m in range(F // 2):
            for c in range(2):
                for zz in range(T):
                    b = (r + zz) % 2
                    pairs.append(((2 * m + c) * T + zz, (2 * m + zz // 2) * T + 2 * c + b))
        return pairs

    rounds = [round_pairs(0), round_pairs(1)]
    backs = [[(d, s) for s, d in pairs] for pairs in rounds]
    cores = [(i, i ^ 1) for i in range(F)]
    axes = ("fsdp", "tp")

    def pick(values, index):
        return lax.dynamic_index_in_dim(values, index, 0, keepdims=False)

    def spread(values):
        first = lax.ppermute(pick(values, odd), axes, rounds[0])
        second = lax.ppermute(pick(values, 1 - odd), axes, rounds[1])
        even = odd == 0
        return jnp.concatenate(
            [jnp.where(even, first, second), jnp.where(even, second, first)], axis=0
        )

    def collect(values):
        first = lax.ppermute(pick(values, odd), axes, backs[0])
        second = lax.ppermute(pick(values, 1 - odd), axes, backs[1])
        even = odd == 0
        return jnp.stack([jnp.where(even, first, second), jnp.where(even, second, first)])

    chain, chain_back = [], []
    for m in range(F // 2):
        for piece in range(2 * C - 1):
            src = (2 * m + piece % 2) * C + piece // 2
            dst = (2 * m + (piece + 1) % 2) * C + (piece + 1) // 2
            chain.append((src, dst))
            chain_back.append((dst, src))

    vecs = (
        norm1_gain, norm1_bias, norm2_gain, norm2_bias, norm3_gain, norm3_bias,
        self_output_bias, cross_output_bias, down_bias,
    )
    hbs = (self_query_bias, self_value_bias, cross_query_bias, cross_value_bias)
    flat = jnp.concatenate(
        [v for v in vecs] + [v.reshape(-1) for v in hbs] + [up_bias.reshape(-1)]
    )
    small = jnp.pad(flat, (0, part * 64 - flat.shape[0])).reshape(part, 64)
    pack1 = jnp.concatenate([self_query, self_key, self_value, small], axis=1)
    pack2 = jnp.concatenate(
        [
            self_output.T, cross_output.T, cross_key, cross_value, cross_query,
            jnp.zeros((part, 64), bf16),
        ],
        axis=1,
    )
    pack3 = jnp.concatenate([fc_up, fc_down.T], axis=1)

    def gather(block):
        full = lax.all_gather(block, tfc, axis=0, tiled=True)
        return full.reshape(T, width, block.shape[1])

    xo = spread(hidden_in)
    g1 = gather(pack1)
    halo_x = lax.ppermute(xo, ("fsdp", "ctx"), chain)
    xa = jnp.concatenate([halo_x, xo], axis=0)

    seg_mine = pick(segment_ids.astype(f32), odd)
    swap_src = []
    for m in range(F // 2):
        for zz in range(T):
            swap_src.append(((2 * m + zz // 2) * T + zz, (2 * m + 1 - zz // 2) * T + zz))
    seg_row = jnp.where(
        core == owner, seg_mine, lax.ppermute(seg_mine, axes, swap_src)
    )
    piece = x * 2 + core
    seg_own = lax.dynamic_slice_in_dim(seg_row, piece * own, own)
    seg_halo = lax.dynamic_slice_in_dim(seg_row, jnp.maximum(piece - 1, 0) * own, own)
    seg_halo = jnp.where(piece == 0, -1.0, seg_halo)
    segk = jnp.concatenate([seg_halo, seg_own]).reshape(2 * own, 1)
    segq = seg_own.reshape(own // QT, 1, QT)
    ends = seg_own.reshape(own // QT, QT)
    span = jnp.stack([ends[:, 0], ends[:, -1]], axis=1).reshape(-1).astype(jnp.int32)

    e_mine = pick(encoder_states, odd)
    e_half = jnp.where(core == owner, e_mine, lax.ppermute(e_mine, axes, swap_src))
    e_other = lax.ppermute(e_half, "ctx", [(0, 1), (1, 0)])
    frames_all = 2 * frames_own
    per_doc = -(-frames_all // (DOCS * 32)) * 32
    slots = DOCS * per_doc
    left = x == 0
    e_all = jnp.concatenate(
        [
            jnp.where(left, e_half, e_other),
            jnp.where(left, e_other, e_half),
            jnp.zeros((slots - frames_all, width), bf16),
        ],
        axis=0,
    )
    ep = e_all.reshape(per_doc, DOCS, width).transpose(1, 0, 2).reshape(slots, width)
    counts = jnp.asarray([float(-(-(frames_all - d) // DOCS)) for d in range(DOCS)], f32)

    g2 = gather(pack2)
    dy = spread(out_grad)
    g3 = gather(pack3)

    flat_all = g1[:, :, 3 * hw :].reshape(T, F * C, part * 64)
    nv = len(vecs) * part
    vec_all = flat_all[0, :, :nv].reshape(F * C, len(vecs), part)
    vec_all = vec_all.transpose(1, 0, 2).reshape(len(vecs), width).astype(f32)
    per = self_query_bias.shape[1]
    nb = heads * per
    hb_all = flat_all[:, :, nv : nv + 4 * nb].reshape(T, F * C, 4, heads, per)
    hb_all = hb_all.transpose(2, 0, 3, 1, 4).reshape(4, T, 1, hw).astype(f32)
    ub_all = flat_all[:, :, nv + 4 * nb : nv + 4 * nb + up_bias.size]
    ub_all = ub_all.reshape(T, F * C, heads, up_bias.shape[1])
    ub_all = ub_all.transpose(0, 2, 1, 3).reshape(T, 1, units).astype(f32)

    zeros_hb = jnp.zeros((T, 1, hw), f32)
    pb = jnp.concatenate([hb_all[0], zeros_hb, hb_all[1]], axis=2)
    kb = jnp.concatenate([zeros_hb, hb_all[3]], axis=2)

    nq = own // QT
    a1, qkv, o, lse1 = pl.pallas_call(
        fwd1_kernel,
        grid=(T,),
        in_specs=[
            whole((2 * own, width)),
            step_of(g1.shape),
            whole((1, width)),
            whole((1, width)),
            step_of((T, 1, 3 * hw)),
            whole((2 * own, 1)),
            whole((nq, 1, QT)),
        ],
        out_specs=[
            whole((2 * own, width)),
            step_of((T, 2 * own, 3 * hw)),
            step_of((T, own, hw)),
            step_of((T, nq, 8, QT)),
        ],
        out_shape=[
            sds((2 * own, width), bf16),
            sds((T, 2 * own, 3 * hw), bf16),
            sds((T, own, hw), bf16),
            sds((T, nq, 8, QT), f32),
        ],
        compiler_params=params(1),
        cost_estimate=cost(2 * 2 * own * width * 3 * hw * T + 4 * own * (own + QT) * hw * T, own * (own + QT) * heads * T, 2 * g1.size + 12 * own * width),
        name="fwd1",
    )(xa, g1, vec_all[0:1], vec_all[1:2], pb, segk, segq)

    smem = pl.BlockSpec(memory_space=pltpu.SMEM)
    vm = pl.BlockSpec(memory_space=pltpu.VMEM)
    ckv, r1, a2, cq, co, lse2, r2, a3 = pl.pallas_call(
        fwd2_kernel,
        in_specs=[smem] + [vm] * 8 + [smem],
        out_specs=[vm] * 8,
        out_shape=[
            sds((T, slots, 2 * hw), bf16),
            sds((own, width), f32),
            sds((own, width), bf16),
            sds((T, own, hw), bf16),
            sds((T, own, hw), bf16),
            sds((T, nq, 8, QT), f32),
            sds((own, width), f32),
            sds((own, width), bf16),
        ],
        scratch_shapes=[pltpu.VMEM((nq, T, hw, QT), f32)],
        compiler_params=params(),
        cost_estimate=cost(2 * (2 * slots + 3 * own) * width * hw * T + 4 * own * slots * hw, own * per_doc * heads * T, 2 * g2.size + 20 * own * width),
        name="fwd2",
    )(
        span, g2, ep, xo, o,
        jnp.concatenate(
            [vec_all[6:7], vec_all[2:4], vec_all[7:8], vec_all[4:6], vec_all[8:9], vec_all[8:9]]
        ),
        hb_all[2], kb, segq, counts,
    )

    out_rows, dr2, gr3, ubg, vecg3 = pl.pallas_call(
        ff_kernel,
        grid=(T,),
        in_specs=[
            whole((own, width)),
            whole((own, width)),
            whole((own, width)),
            step_of(g3.shape),
            step_of((T, 1, units)),
            whole((2, width)),
        ],
        out_specs=[
            whole((own, width)),
            whole((own, width)),
            step_of(g3.shape),
            step_of((T, 1, units)),
            whole((8, width)),
        ],
        out_shape=[
            sds((own, width), bf16),
            sds((own, width), f32),
            sds(g3.shape, bf16),
            sds((T, 1, units), f32),
            sds((8, width), f32),
        ],
        scratch_shapes=[
            pltpu.VMEM((width, own), bf16),
            pltpu.VMEM((width, own), bf16),
            pltpu.VMEM((own, width), f32),
            pltpu.VMEM((own, width), f32),
            pltpu.VMEM((own, units), bf16),
            pltpu.VMEM((own, units), bf16),
        ],
        compiler_params=params(1),
        cost_estimate=cost(12 * own * width * units * T, 2 * own * units * T, 4 * g3.size + 12 * own * width),
        name="ff",
    )(a3, r2, dy, g3, ub_all, jnp.concatenate([vec_all[4:5], vec_all[8:9]]))

    def scatter(block):
        return lax.psum_scatter(
            block.reshape(T * width, block.shape[2]), tfc, scatter_dimension=0, tiled=True
        )

    sum3 = scatter(gr3)
    out_final = collect(out_rows.reshape(2, sub, width))

    dr1, do, gr2, de, vecg2, hbg2 = pl.pallas_call(
        bwd2_kernel,
        in_specs=[smem] + [vm] * 12 + [smem],
        out_specs=[vm] * 6,
        out_shape=[
            sds((own, width), f32),
            sds((T, own, hw), bf16),
            sds(g2.shape, bf16),
            sds((slots, width), bf16),
            sds((8, width), f32),
            sds((T, 8, hw), f32),
        ],
        scratch_shapes=[
            pltpu.VMEM((T, own, hw), bf16),
            pltpu.VMEM((T, own, hw), bf16),
            pltpu.VMEM((T, slots, 2 * hw), f32),
            pltpu.VMEM((T, slots, 2 * hw), bf16),
            pltpu.VMEM((width, own), bf16),
            pltpu.VMEM((width, slots), bf16),
            pltpu.VMEM((T, hw, QT), f32),
        ],
        compiler_params=params(),
        cost_estimate=cost(2 * (4 * slots + 6 * own) * width * hw * T + 10 * own * slots * hw, own * per_doc * heads * T, 4 * g2.size + 30 * own * width),
        name="bwd2",
    )(span, g2, ep, dr2, cq, ckv, co, lse2, a2, r1, o, vec_all[2:3], segq, counts)
    gr2, sum3 = lax.optimization_barrier((gr2, sum3))
    sum2 = scatter(gr2)

    da, dh, gr1, vecg1, hbg1 = pl.pallas_call(
        bwd1_kernel,
        grid=(T,),
        in_specs=[
            whole((2 * own, width)),
            whole((2 * own, width)),
            step_of(g1.shape),
            step_of(qkv.shape),
            step_of(o.shape),
            step_of(do.shape),
            step_of(lse1.shape),
            whole((2 * own, 1)),
            whole((nq, 1, QT)),
        ],
        out_specs=[
            whole((own, width)),
            whole((own, width)),
            step_of(g1.shape),
            whole((8, width)),
            step_of((T, 8, hw)),
        ],
        out_shape=[
            sds((own, width), f32),
            sds((own, width), bf16),
            sds(g1.shape, bf16),
            sds((8, width), f32),
            sds((T, 8, hw), f32),
        ],
        scratch_shapes=[
            pltpu.VMEM((width, 2 * own), bf16),
            pltpu.VMEM((2 * own, width), f32),
            pltpu.VMEM((2 * own, hw), f32),
            pltpu.VMEM((2 * own, hw), f32),
            pltpu.VMEM((own, hw), bf16),
            pltpu.VMEM((2 * own, 3 * hw), bf16),
        ],
        compiler_params=params(1),
        cost_estimate=cost(2 * 4 * own * width * 3 * hw * T + 10 * own * (own + QT) * hw * T, own * (own + QT) * heads * T, 4 * g1.size + 30 * own * width),
        name="bwd1",
    )(xa, a1, g1, qkv, o, do, lse1, segk, segq)

    d_next = lax.ppermute(dh, ("fsdp", "ctx"), chain_back)

    vec_g = jnp.concatenate(
        [vecg1[0:2], vecg2[0:2], vecg3[0:2], vecg2[3:4], vecg2[2:3], vecg3[2:3]]
    )
    third = part // T
    vg = vec_g.reshape(len(vecs), F * C, T, third).transpose(2, 1, 0, 3)
    vg = vg.reshape(T, F * C, len(vecs) * third)
    hg = jnp.stack([hbg1[:, 0], hbg1[:, 1], hbg2[:, 0], hbg2[:, 1]])
    hg = hg.reshape(4, T, heads, F * C, per).transpose(1, 3, 0, 2, 4).reshape(T, F * C, 4 * nb)
    ug = ubg.reshape(T, heads, F * C, up_bias.shape[1]).transpose(0, 2, 1, 3)
    ug = ug.reshape(T, F * C, up_bias.size)
    sg = jnp.concatenate([vg, hg, ug], axis=2)
    sg = jnp.pad(sg, ((0, 0), (0, 0), (0, part * 64 - sg.shape[2])))
    sg = sg.reshape(T, width, 64).astype(bf16)
    gr1 = lax.dynamic_update_slice(gr1, sg, (0, 0, 3 * hw))
    gr1, sum2 = lax.optimization_barrier((gr1, sum2))
    sum1 = scatter(gr1).astype(f32)

    grad_rows = pl.pallas_call(
        bwd0_kernel,
        grid=(2,),
        in_specs=[pl.BlockSpec((sub, width), lambda i: (i, 0))] * 4 + [whole((1, width))],
        out_specs=pl.BlockSpec((sub, width), lambda i: (i, 0)),
        out_shape=sds((own, width), bf16),
        compiler_params=params(1),
        cost_estimate=cost(20 * own * width, own, 14 * own * width),
        name="bwd0",
    )(xo, da, d_next, dr1, vec_all[0:1])
    grad_hidden = collect(grad_rows.reshape(2, sub, width)).astype(f32)

    de = de.reshape(DOCS, per_doc, width).transpose(1, 0, 2).reshape(slots, width)[:frames_all]
    halves = de.reshape(frames_all, 2, width // 2).transpose(1, 0, 2)
    got = lax.ppermute(pick(halves, 1 - core), "fsdp", cores)
    half = (pick(halves, core).astype(f32) + got.astype(f32)).astype(bf16)
    half = half.reshape(2, frames_own, width // 2)
    got = lax.ppermute(pick(half, 1 - x), "ctx", [(0, 1), (1, 0)])
    half = (pick(half, x).astype(f32) + got.astype(f32)).astype(bf16)
    half = half.reshape(frames_own, 2, width // 4).transpose(1, 0, 2)
    grad_encoder = collect(half).astype(f32)

    sum2 = sum2.astype(f32)
    sum3 = sum3.astype(f32)
    small_sum = sum1[:, 3 * hw :].reshape(-1)
    ng = len(vecs) * third
    vout = small_sum[:ng].reshape(len(vecs), third)
    hout = small_sum[ng : ng + 4 * nb].reshape(4, heads, per)
    uout = small_sum[ng + 4 * nb : ng + 4 * nb + up_bias.size].reshape(up_bias.shape)

    def cut(array, k):
        return array[:, k * hw : (k + 1) * hw]

    return (
        out_final,
        grad_hidden,
        grad_encoder,
        vout[0], vout[1], vout[2], vout[3], vout[4], vout[5],
        cut(sum1, 0), cut(sum1, 1), cut(sum1, 2), cut(sum2, 0).T,
        cut(sum2, 4), cut(sum2, 2), cut(sum2, 3), cut(sum2, 1).T,
        sum3[:, :units], sum3[:, units:].T,
        hout[0], hout[1], hout[2], hout[3], uout,
        vout[6], vout[7], vout[8],
    )


def solution(mesh):
    column = P(("fsdp", "ctx"), "tp")
    row = P("tp", ("fsdp", "ctx"))
    vector = P(("fsdp", "ctx"))
    vector_out = P(("fsdp", "ctx", "tp"))
    tokens = P("fsdp", ("ctx", "tp"), None)
    return jax.shard_map(
        on_device,
        mesh=mesh,
        in_specs=(tokens, P("fsdp", "ctx", None), P("fsdp", None), tokens)
        + (vector,) * 6
        + (column, column, column, row)
        + (column, column, column, row)
        + (column, row)
        + (row,) * 5
        + (vector,) * 3,
        out_specs=(tokens, tokens, P("fsdp", "ctx", "tp"))
        + (vector_out,) * 6
        + (column, column, column, row)
        + (column, column, column, row)
        + (column, row)
        + (row,) * 5
        + (vector_out,) * 3,
        check_vma=False,
    )
```

```python
import functools
import math

import jax
import jax.numpy as jnp
from jax import lax
from jax.experimental import pallas as pl
from jax.experimental.pallas import tpu as pltpu
from jax.sharding import PartitionSpec as P

HEAD_DIM = 64
DOCS = 16
EPSILON = 1e-05
MASKED = -1e30
SCALE = HEAD_DIM ** (-0.5)
QT = 128

f32 = jnp.float32
bf16 = jnp.bfloat16

VMEM_LIMIT = 62 * 1024 * 1024


def nn(a, b):
    return lax.dot_general(a, b, (((1,), (0,)), ((), ())), preferred_element_type=f32)


def nt(a, b):
    return lax.dot_general(a, b, (((1,), (1,)), ((), ())), preferred_element_type=f32)


def tn(a, b):
    return lax.dot_general(a, b, (((0,), (0,)), ((), ())), preferred_element_type=f32)


def norm_parts(values):
    centred = values - jnp.mean(values, axis=-1, keepdims=True)
    rate = lax.rsqrt(jnp.mean(centred * centred, axis=-1, keepdims=True) + EPSILON)
    return centred * rate, rate


def norm_back(z, rate, gain, grad):
    scaled = gain * grad
    return rate * (
        scaled
        - jnp.mean(scaled, axis=-1, keepdims=True)
        - z * jnp.mean(scaled * z, axis=-1, keepdims=True)
    )


def row_sum(values):
    return jnp.sum(values, axis=0, keepdims=True)


def self_scores(kw, qn, masked_add):
    return nt(kw, qn) + masked_add


def window_mask(segk_ref, segq_ref, n, halo, window):
    keys = segk_ref[pl.ds(n * QT, window), :]
    same = keys == segq_ref[n]
    ahead = lax.broadcasted_iota(jnp.int32, (window, QT), 0) - lax.broadcasted_iota(
        jnp.int32, (window, QT), 1
    )
    return jnp.where(same & (ahead <= halo), 0.0, MASKED)


def fwd1_kernel(
    xa_ref, g1_ref, gain_ref, bias_ref, pb_ref, segk_ref, segq_ref, a1_ref, qkv_ref, o_ref, lse_ref
):
    rows = xa_ref.shape[0]
    own = segq_ref.shape[0] * QT
    halo = rows - own
    window = halo + QT
    hw = o_ref.shape[2]
    tile = 256

    @pl.when(pl.program_id(0) == 0)
    def _():
        def body(i, _):
            at = pl.ds(i * tile, tile)
            z, _ = norm_parts(xa_ref[at, :].astype(f32))
            a1_ref[at, :] = (z * gain_ref[...] + bias_ref[...]).astype(bf16)
            return 0

        lax.fori_loop(0, rows // tile, body, 0)

    w = g1_ref[0, :, : 3 * hw]

    def project(i, _):
        at = pl.ds(i * tile, tile)
        qkv_ref[0, at, :] = (nn(a1_ref[at, :], w) + pb_ref[0]).astype(bf16)
        return 0

    lax.fori_loop(0, rows // tile, project, 0)

    def attend(n, _):
        add = window_mask(segk_ref, segq_ref, n, halo, window)
        block = qkv_ref[0, pl.ds(n * QT, window), :]
        outs = []
        for i in range(hw // HEAD_DIM):
            kw = block[:, hw + i * HEAD_DIM : hw + (i + 1) * HEAD_DIM]
            vw = block[:, 2 * hw + i * HEAD_DIM : 2 * hw + (i + 1) * HEAD_DIM]
            qn = block[halo:, i * HEAD_DIM : (i + 1) * HEAD_DIM] * bf16(SCALE)
            scores = self_scores(kw, qn, add)
            top = jnp.max(scores, axis=0, keepdims=True)
            weights = jnp.exp(scores - top)
            total = jnp.sum(weights, axis=0, keepdims=True)
            mixed = tn(vw, weights.astype(bf16)) / total
            outs.append(mixed)
            lse_ref[0, n, i : i + 1, :] = top + jnp.log(total)
        o_ref[0, pl.ds(n * QT, QT), :] = jnp.concatenate(outs, axis=0).T.astype(bf16)
        return 0

    lax.fori_loop(0, own // QT, attend, 0)


def fwd2_kernel(
    span_ref, g2_ref, e_ref, xo_ref, o_ref, vec_ref, cb_ref, kb_ref, segq_ref, count_ref,
    ckv_ref, r1_ref, a2_ref, cq_ref, co_ref, lse_ref, r2_ref, a3_ref, ep_ref, acc_ref, wide_ref,
):
    groups = g2_ref.shape[0]
    half = e_ref.shape[1]
    own = xo_ref.shape[0]
    hw = o_ref.shape[2]
    slots = ep_ref.shape[0]
    per_doc = slots // DOCS
    heads = hw // HEAD_DIM
    tile = 256

    for i in range(ep_ref.shape[1] // 128):
        lane = slice(i * 128, (i + 1) * 128)
        wide_ref[i, 0:half, :] = e_ref[0, :, lane].astype(f32)
        wide_ref[i, half : 2 * half, :] = e_ref[1, :, lane].astype(f32)
        wide_ref[i, 2 * half :, :] = jnp.zeros((slots - 2 * half, 128), f32)
        for d in range(DOCS):
            ep_ref[d * per_doc : (d + 1) * per_doc, lane] = wide_ref[
                i, pl.ds(d, per_doc, stride=DOCS), :
            ].astype(bf16)

    for t in range(groups):

        def frames(i, _):
            at = pl.ds(i * tile, tile)
            y = nn(ep_ref[at, :], g2_ref[t, :, 2 * hw : 4 * hw]) + kb_ref[t]
            ckv_ref[t, at, :] = y.astype(bf16)
            return 0

        lax.fori_loop(0, slots // tile, frames, 0)

    def middle(i, _):
        at = pl.ds(i * tile, tile)
        r1 = xo_ref[at, :].astype(f32) + vec_ref[0:1, :]
        for t in range(groups):
            r1 = r1 + nt(o_ref[t, at, :], g2_ref[t, :, 0:hw])
        r1_ref[at, :] = r1
        z, _ = norm_parts(r1)
        a2 = (z * vec_ref[1:2, :] + vec_ref[2:3, :]).astype(bf16)
        a2_ref[at, :] = a2
        for t in range(groups):
            cq_ref[t, at, :] = (nn(a2, g2_ref[t, :, 4 * hw : 5 * hw]) + cb_ref[t]).astype(bf16)
        return 0

    lax.fori_loop(0, own // tile, middle, 0)

    acc_ref[...] = jnp.zeros_like(acc_ref)
    lse_ref[...] = jnp.zeros_like(lse_ref)
    place = lax.broadcasted_iota(jnp.int32, (per_doc, QT), 0).astype(f32)

    def attend(n, _):
        segs = segq_ref[n]

        def document(d, _):
            mine = segs == d.astype(f32)
            col = jnp.where(mine, 1.0, 0.0)
            add = jnp.where(place < count_ref[d], 0.0, MASKED)
            for t in range(groups):
                kv = ckv_ref[t, pl.ds(d * per_doc, per_doc), :]
                qs = cq_ref[t, pl.ds(n * QT, QT), :] * bf16(SCALE)
                for i in range(heads):
                    lane = slice(i * HEAD_DIM, (i + 1) * HEAD_DIM)
                    vlane = slice(hw + i * HEAD_DIM, hw + (i + 1) * HEAD_DIM)
                    scores = nt(kv[:, lane], qs[:, lane]) + add
                    top = jnp.max(scores, axis=0, keepdims=True)
                    weights = jnp.exp(scores - top)
                    total = jnp.sum(weights, axis=0, keepdims=True)
                    mixed = tn(kv[:, vlane], weights.astype(bf16)) * (col / total)
                    acc_ref[n, t, lane, :] += mixed
                    lse_ref[t, n, i : i + 1, :] += col * (top + jnp.log(total))
            return 0

        lax.fori_loop(span_ref[2 * n], span_ref[2 * n + 1] + 1, document, 0)
        for t in range(groups):
            co_ref[t, pl.ds(n * QT, QT), :] = acc_ref[n, t].T.astype(bf16)
        return 0

    lax.fori_loop(0, own // QT, attend, 0)

    def final(i, _):
        at = pl.ds(i * tile, tile)
        r2 = r1_ref[at, :] + vec_ref[3:4, :]
        for t in range(groups):
            r2 = r2 + nt(co_ref[t, at, :], g2_ref[t, :, hw : 2 * hw])
        r2_ref[at, :] = r2
        z, _ = norm_parts(r2)
        a3_ref[at, :] = (z * vec_ref[4:5, :] + vec_ref[5:6, :]).astype(bf16)
        return 0

    lax.fori_loop(0, own // tile, final, 0)


def ff_kernel(
    a3_ref, r2_ref, dy_ref, g3_ref, ub_ref, vec_ref,
    out_ref, dr2_ref, gr3_ref, ubg_ref, vecg_ref,
    a3t_ref, dmt_ref, acc_ref, acd_ref, gs_ref, dus_ref,
):
    t = pl.program_id(0)
    own, width = a3_ref.shape
    units = ub_ref.shape[2]
    tile = 256

    @pl.when(t == 0)
    def _():
        a3t_ref[...] = a3_ref[...].T
        dmt_ref[...] = dy_ref[...].T
        acc_ref[...] = jnp.zeros_like(acc_ref)
        acd_ref[...] = jnp.zeros_like(acd_ref)

    ubg_ref[...] = jnp.zeros_like(ubg_ref)
    up = g3_ref[0, :, :units]
    down = g3_ref[0, :, units:]

    def rows(i, _):
        at = pl.ds(i * tile, tile)
        u = nn(a3_ref[at, :], up) + ub_ref[0]
        phi = 0.5 + 0.5 * lax.erf(u * (1.0 / math.sqrt(2.0)))
        g = (u * phi).astype(bf16)
        gs_ref[at, :] = g
        slope = phi + u * (jnp.exp(-0.5 * u * u) * (1.0 / math.sqrt(2.0 * math.pi)))
        du = (nn(dy_ref[at, :], down) * slope).astype(bf16)
        dus_ref[at, :] = du
        ubg_ref[0] += row_sum(du.astype(f32))
        acc_ref[at, :] += nt(g, down)
        acd_ref[at, :] += nt(du, up)
        return 0

    lax.fori_loop(0, own // tile, rows, 0)

    def grads(i, _):
        at = pl.ds(i * tile, tile)
        gr3_ref[0, at, :units] = nn(a3t_ref[at, :], dus_ref[...]).astype(bf16)
        gr3_ref[0, at, units:] = nn(dmt_ref[at, :], gs_ref[...]).astype(bf16)
        return 0

    lax.fori_loop(0, width // tile, grads, 0)

    @pl.when(t == pl.num_programs(0) - 1)
    def _():
        vecg_ref[...] = jnp.zeros_like(vecg_ref)

        def finish(i, _):
            at = pl.ds(i * tile, tile)
            r2 = r2_ref[at, :]
            dy = dy_ref[at, :].astype(f32)
            out_ref[at, :] = (r2 + (acc_ref[at, :] + vec_ref[1:2, :])).astype(bf16)
            z, rate = norm_parts(r2)
            da = acd_ref[at, :]
            dr2_ref[at, :] = dy + norm_back(z, rate, vec_ref[0:1, :], da)
            vecg_ref[0:1, :] += row_sum(da * z)
            vecg_ref[1:2, :] += row_sum(da)
            vecg_ref[2:3, :] += row_sum(dy)
            return 0

        lax.fori_loop(0, own // tile, finish, 0)


def bwd2_kernel(
    span_ref, g2_ref, ep_ref, dr2_ref, cq_ref, ckv_ref, co_ref, lse_ref, a2_ref, r1_ref, o_ref,
    vec_ref, segq_ref, count_ref,
    dr1_ref, do_ref, gr2_ref, de_ref, vecg_ref, hbg_ref,
    dco_ref, dcq_ref, dkv_ref, low_ref, rowt_ref, ept_ref, acc_ref, wide_ref,
):
    groups, width = g2_ref.shape[0], g2_ref.shape[1]
    own = dr2_ref.shape[0]
    hw = o_ref.shape[2]
    slots = ep_ref.shape[0]
    per_doc = slots // DOCS
    heads = hw // HEAD_DIM
    tile = 256

    vecg_ref[...] = jnp.zeros_like(vecg_ref)
    hbg_ref[...] = jnp.zeros_like(hbg_ref)

    for i in range(own // tile):
        at = slice(i * tile, (i + 1) * tile)
        dc = dr2_ref[at, :].astype(bf16)
        vecg_ref[2:3, :] += row_sum(dc.astype(f32))
        rowt_ref[:, at] = dc.T
        for t in range(groups):
            dco_ref[t, at, :] = nn(dc, g2_ref[t, :, hw : 2 * hw]).astype(bf16)

    for t in range(groups):
        gr2_ref[t, :, hw : 2 * hw] = nn(rowt_ref[...], co_ref[t]).astype(bf16)

    dkv_ref[...] = jnp.zeros_like(dkv_ref)
    place = lax.broadcasted_iota(jnp.int32, (per_doc, QT), 0).astype(f32)

    def attend(n, _):
        segs = segq_ref[n]
        acc_ref[...] = jnp.zeros_like(acc_ref)

        def document(d, _):
            keep = (segs == d.astype(f32)) & (place < count_ref[d])
            add = jnp.where(keep, 0.0, MASKED)
            for t in range(groups):
                kv = ckv_ref[t, pl.ds(d * per_doc, per_doc), :]
                qs = cq_ref[t, pl.ds(n * QT, QT), :] * bf16(SCALE)
                dos = dco_ref[t, pl.ds(n * QT, QT), :]
                inner = (dos.astype(f32) * co_ref[t, pl.ds(n * QT, QT), :].astype(f32)).T
                dks, dvs = [], []
                for i in range(heads):
                    lane = slice(i * HEAD_DIM, (i + 1) * HEAD_DIM)
                    vlane = slice(hw + i * HEAD_DIM, hw + (i + 1) * HEAD_DIM)
                    scores = nt(kv[:, lane], qs[:, lane]) + add
                    probs = jnp.exp(scores - lse_ref[t, n, i : i + 1, :])
                    delta = row_sum(inner[lane, :])
                    grad = nt(kv[:, vlane], dos[:, lane])
                    ds = (probs * (grad - delta)).astype(bf16)
                    dvs.append(nn(probs.astype(bf16), dos[:, lane]))
                    dks.append(nn(ds, qs[:, lane]))
                    acc_ref[t, lane, :] += tn(kv[:, lane], ds)
                dkv_ref[t, pl.ds(d * per_doc, per_doc), :] += jnp.concatenate(dks + dvs, axis=1)
            return 0

        lax.fori_loop(span_ref[2 * n], span_ref[2 * n + 1] + 1, document, 0)
        for t in range(groups):
            dcq_ref[t, pl.ds(n * QT, QT), :] = (acc_ref[t].T * SCALE).astype(bf16)
        return 0

    lax.fori_loop(0, own // QT, attend, 0)

    for i in range(own // tile):
        at = slice(i * tile, (i + 1) * tile)
        da = jnp.zeros((tile, width), f32)
        for t in range(groups):
            da = da + nt(dcq_ref[t, at, :], g2_ref[t, :, 4 * hw : 5 * hw])
        z, rate = norm_parts(r1_ref[at, :])
        dr1 = dr2_ref[at, :] + norm_back(z, rate, vec_ref[0:1, :], da)
        dr1_ref[at, :] = dr1
        vecg_ref[0:1, :] += row_sum(da * z)
        vecg_ref[1:2, :] += row_sum(da)
        rowt_ref[:, at] = a2_ref[at, :].T

    for t in range(groups):
        gr2_ref[t, :, 4 * hw : 5 * hw] = nn(rowt_ref[...], dcq_ref[t]).astype(bf16)
        hbg_ref[t, 0:1, :] = row_sum(dcq_ref[t].astype(f32))

    for i in range(own // tile):
        at = slice(i * tile, (i + 1) * tile)
        ds = dr1_ref[at, :].astype(bf16)
        vecg_ref[3:4, :] += row_sum(ds.astype(f32))
        rowt_ref[:, at] = ds.T
        for t in range(groups):
            do_ref[t, at, :] = nn(ds, g2_ref[t, :, 0:hw]).astype(bf16)

    for t in range(groups):
        gr2_ref[t, :, 0:hw] = nn(rowt_ref[...], o_ref[t]).astype(bf16)

    for i in range(slots // tile):
        at = slice(i * tile, (i + 1) * tile)
        ept_ref[:, at] = ep_ref[at, :].T

    for t in range(groups):

        def lower(i, _):
            at = pl.ds(i * tile, tile)
            low = dkv_ref[t, at, :].astype(bf16)
            low_ref[t, at, :] = low
            hbg_ref[t, 1:2, :] += row_sum(low[:, hw:].astype(f32))
            return 0

        lax.fori_loop(0, slots // tile, lower, 0)

    half = width // 2
    for i in range(DOCS // 4):
        at = slice(4 * i * per_doc, 4 * (i + 1) * per_doc)
        total = jnp.zeros((4 * per_doc, width), f32)
        for t in range(groups):
            total = total + nt(low_ref[t, at, :], g2_ref[t, :, 2 * hw : 4 * hw])
        for d in range(4):
            block = total[d * per_doc : (d + 1) * per_doc]
            for j in range(width // 128):
                wide_ref[j, pl.ds(4 * i + d, per_doc, stride=DOCS), :] = block[
                    :, j * 128 : (j + 1) * 128
                ]
    per_half = half // 128
    for j in range(width // 128):
        lane = slice((j % per_half) * 128, (j % per_half + 1) * 128)
        held = de_ref.shape[2]
        for h in range(de_ref.shape[1]):
            at = slice(h * held, (h + 1) * held)
            de_ref[j // per_half, h, :, lane] = wide_ref[j, at, :].astype(bf16)

    def key_grads(t, _):
        gr2_ref[t, :, 2 * hw : 4 * hw] = nn(ept_ref[...], low_ref[t]).astype(bf16)
        return 0

    lax.fori_loop(0, groups, key_grads, 0)


def bwd1_kernel(
    xa_ref, a1_ref, g1_ref, qkv_ref, o_ref, do_ref, lse_ref, segk_ref, segq_ref,
    da_ref, dh_ref, gr1_ref, vecg_ref, hbg_ref,
    a1t_ref, acc_ref, dk_ref, dv_ref, dq_ref, low_ref,
):
    t = pl.program_id(0)
    rows, width = xa_ref.shape
    own = segq_ref.shape[0] * QT
    halo = rows - own
    window = halo + QT
    hw = o_ref.shape[2]
    tile = 256

    @pl.when(t == 0)
    def _():
        for i in range(rows // tile):
            at = slice(i * tile, (i + 1) * tile)
            a1t_ref[:, at] = a1_ref[at, :].T
        acc_ref[...] = jnp.zeros_like(acc_ref)
        low_ref[0:halo, 0:hw] = jnp.zeros((halo, hw), bf16)

    dk_ref[...] = jnp.zeros_like(dk_ref)
    dv_ref[...] = jnp.zeros_like(dv_ref)

    def attend(n, _):
        add = window_mask(segk_ref, segq_ref, n, halo, window)
        at = pl.ds(n * QT, window)
        mine = pl.ds(n * QT, QT)
        block = qkv_ref[0, at, :]
        dos = do_ref[0, mine, :]
        inner = (dos.astype(f32) * o_ref[0, mine, :].astype(f32)).T
        dks, dvs, dqs = [], [], []
        for i in range(hw // HEAD_DIM):
            lane = slice(i * HEAD_DIM, (i + 1) * HEAD_DIM)
            kw = block[:, hw + i * HEAD_DIM : hw + (i + 1) * HEAD_DIM]
            vw = block[:, 2 * hw + i * HEAD_DIM : 2 * hw + (i + 1) * HEAD_DIM]
            qn = block[halo:, lane] * bf16(SCALE)
            scores = self_scores(kw, qn, add)
            probs = jnp.exp(scores - lse_ref[0, n, i : i + 1, :])
            delta = row_sum(inner[lane, :])
            grad = nt(vw, dos[:, lane])
            ds = (probs * (grad - delta)).astype(bf16)
            dvs.append(nn(probs.astype(bf16), dos[:, lane]))
            dks.append(nn(ds, qn))
            dqs.append(tn(kw, ds))
        dk_ref[at, :] += jnp.concatenate(dks, axis=1)
        dv_ref[at, :] += jnp.concatenate(dvs, axis=1)
        dq_ref[mine, :] = (jnp.concatenate(dqs, axis=0).T * SCALE).astype(bf16)
        return 0

    lax.fori_loop(0, own // QT, attend, 0)
    low_ref[halo:, 0:hw] = dq_ref[...]
    low_ref[:, hw : 2 * hw] = dk_ref[...].astype(bf16)
    low_ref[:, 2 * hw : 3 * hw] = dv_ref[...].astype(bf16)
    hbg_ref[...] = jnp.zeros_like(hbg_ref)
    hbg_ref[0, 0:1, :] = row_sum(dq_ref[...].astype(f32))
    hbg_ref[0, 1:2, :] = row_sum(dv_ref[...].astype(bf16).astype(f32))
    w = g1_ref[0, :, : 3 * hw]

    def back(i, _):
        at = pl.ds(i * tile, tile)
        acc_ref[at, :] += nt(low_ref[at, :], w)
        return 0

    lax.fori_loop(0, rows // tile, back, 0)

    def grads(i, _):
        at = pl.ds(i * tile, tile)
        gr1_ref[0, at, 0 : 3 * hw] = nn(a1t_ref[at, :], low_ref[...]).astype(bf16)
        return 0

    lax.fori_loop(0, width // tile, grads, 0)

    @pl.when(t == pl.num_programs(0) - 1)
    def _():
        vecg_ref[...] = jnp.zeros_like(vecg_ref)
        dh_ref[...] = acc_ref[0:halo, :].astype(bf16)
        da_ref[...] = acc_ref[halo:, :]

        def sums(i, _):
            at = pl.ds(i * tile, tile)
            z, _ = norm_parts(xa_ref[at, :].astype(f32))
            vecg_ref[0:1, :] += row_sum(acc_ref[at, :] * z)
            vecg_ref[1:2, :] += row_sum(acc_ref[at, :])
            return 0

        lax.fori_loop(0, rows // tile, sums, 0)


def whole(shape):
    return pl.BlockSpec(shape, lambda *_: (0,) * len(shape))


def step_of(shape):
    return pl.BlockSpec((1,) + shape[1:], lambda t: (t,) + (0,) * (len(shape) - 1))


def params(dims=0):
    return pltpu.CompilerParams(
        vmem_limit_bytes=VMEM_LIMIT,
        dimension_semantics=("arbitrary",) * dims if dims else None,
    )


def cost(flops, exps, size):
    return pl.CostEstimate(flops=int(flops), transcendentals=int(exps), bytes_accessed=int(size))


def sds(shape, dtype):
    return jax.ShapeDtypeStruct(shape, dtype)

MESH_ID = pl.DeviceIdType.MESH


def place_of(chips, ctx, groups):
    f, x, z = lax.axis_index("fsdp"), lax.axis_index("ctx"), lax.axis_index("tp")
    return lax.div(f, 2), lax.rem(f, 2), x, z


def greet(chips, ctx, groups, y, c, x, z):
    barrier = pltpu.get_barrier_semaphore()
    peers = [(2 * lax.rem(y + j, chips) + c, x, z) for j in range(1, chips)]
    for dc in range(2):
        for dx in range(ctx):
            for dz in range(groups):
                if dc + dx + dz > 0:
                    other = (2 * y + lax.rem(c + dc, 2), lax.rem(x + dx, ctx), lax.rem(z + dz, groups))
                    peers.append(other)
    for peer in peers:
        pl.semaphore_signal(barrier, inc=1, device_id=peer, device_id_type=MESH_ID)
    pl.semaphore_wait(barrier, len(peers))


def gather_kernel(paths, chips, ctx, groups, *refs):
    count = len(paths)
    packs, (rows_in, frames_in, seg_in) = refs[:count], refs[count : count + 3]
    refs = refs[count + 3 :]
    fulls, (rows_out, frames_out, seg_out) = refs[:count], refs[count : count + 3]
    blank, local, zs, zr, fs, fr, ss, sr, cs, cr, xs, xr, xl, es, er, el = refs[count + 3 :]
    y, c, x, z = place_of(chips, ctx, groups)
    greet(chips, ctx, groups, y, c, x, z)
    sent = []

    def sizes(a):
        return (ctx, chips) if paths[a] == "xy" else (chips, ctx)

    def spot(a, k, i, j, core):
        t = lax.rem(z + groups - k, groups)
        dx, dy = (i, j) if paths[a] == "xy" else (j, i)
        return fulls[a].at[t, lax.rem(y + chips - dy, chips), core, lax.rem(x + ctx - dx, ctx)]

    def peer(a, first, hop):
        along_x = (paths[a] == "xy") == first
        if along_x:
            return (2 * y + c, lax.rem(x + hop, ctx), z)
        return (2 * lax.rem(y + hop, chips) + c, x, z)

    def flat(a, i, j):
        return i * sizes(a)[1] + j

    def send(src, dst, ssem, rsem, device):
        copy = pltpu.make_async_remote_copy(
            src_ref=src, dst_ref=dst, send_sem=ssem, recv_sem=rsem,
            device_id=device, device_id_type=MESH_ID,
        )
        copy.start()
        sent.append(copy)

    def arrived(dst, ssem, rsem):
        pltpu.make_async_remote_copy(
            src_ref=dst, dst_ref=dst, send_sem=ssem, recv_sem=rsem,
            device_id=(2 * y + 1 - c, x, z), device_id_type=MESH_ID,
        ).wait_recv()

    def to_core(a, k, i, j, src):
        send(src, spot(a, k, i, j, c), cs.at[a, k, flat(a, i, j)], cr.at[a, k, flat(a, i, j)], (2 * y + 1 - c, x, z))

    def second(a, k, i, src):
        for j in range(1, sizes(a)[1]):
            send(src, spot(a, k, i, 0, c), ss.at[a, k, flat(a, i, j)], sr.at[a, k, flat(a, i, j)], peer(a, False, j))

    half, low = lax.div(z, 2), lax.rem(z, 2)
    me = (2 * y + c, x, z)
    core_peer = (2 * y + 1 - c, x, z)

    def remote(src, dst, ssem, rsem, device):
        return pltpu.make_async_remote_copy(
            src_ref=src, dst_ref=dst, send_sem=ssem, recv_sem=rsem,
            device_id=device, device_id_type=MESH_ID,
        )

    blank[...] = jnp.zeros_like(blank)
    next_piece = 2 * x + half + 1
    for b in range(2):
        stays = (half == c) & (2 * c + b == z)
        away = remote(
            rows_in.at[b], rows_out.at[2 + low], xs.at[b], xr.at[2 + low], (2 * y + half, x, 2 * c + b)
        )
        here = pltpu.make_async_copy(rows_in.at[b], rows_out.at[2 + low], xl.at[2])
        pl.when(jnp.logical_not(stays))(away.start)
        pl.when(stays)(here.start)
        core_to, x_to = lax.rem(next_piece, 2), lax.div(next_piece, 2)
        exists = x_to < ctx
        stays = (core_to == c) & (x_to == x) & (2 * c + b == z)
        away = remote(
            rows_in.at[b], rows_out.at[low], xs.at[2 + b], xr.at[low],
            (2 * y + core_to, lax.rem(x_to, ctx), 2 * c + b),
        )
        here = pltpu.make_async_copy(rows_in.at[b], rows_out.at[low], xl.at[3])
        pl.when(exists & jnp.logical_not(stays))(away.start)
        pl.when(exists & stays)(here.start)
    first = (x == 0) & (c == 0)

    @pl.when(first)
    def _():
        for s in range(2):
            pltpu.make_async_copy(blank, rows_out.at[s], xl.at[s]).start()

    holds = half == c

    @pl.when(holds)
    def _():
        pltpu.make_async_copy(frames_in.at[low], frames_out.at[x], el.at[0]).start()
        pltpu.make_async_copy(seg_in.at[low], seg_out, el.at[1]).start()
        remote(
            frames_in.at[low], frames_out.at[x], es.at[0], er.at[0], (2 * y + c, 1 - x, z)
        ).start()
        remote(frames_in.at[low], frames_out.at[x], es.at[1], er.at[1], core_peer).start()
        remote(seg_in.at[low], seg_out, es.at[2], er.at[2], core_peer).start()

    mine = []
    for a in range(count):
        copy = pltpu.make_async_copy(packs[a], spot(a, 0, 0, 0, c), local.at[a])
        copy.start()
        mine.append(copy)
        for k in range(1, groups):
            send(
                packs[a], spot(a, 0, 0, 0, c), zs.at[a, k], zr.at[a, k],
                (2 * y + c, x, lax.rem(z + k, groups)),
            )
    for step in range(groups + 2):
        for a in range(count):
            n1, n2 = sizes(a)
            k = step
            if k < groups:
                src = packs[a] if k == 0 else spot(a, k, 0, 0, c)
                if k > 0:
                    arrived(src, zs.at[a, k], zr.at[a, k])
                for i in range(1, n1):
                    send(src, spot(a, k, 0, 0, c), fs.at[a, k, i], fr.at[a, k, i], peer(a, True, i))
                second(a, k, 0, src)
                to_core(a, k, 0, 0, src)
            k = step - 1
            if 0 <= k < groups:
                for i in range(1, n1):
                    src = spot(a, k, i, 0, c)
                    arrived(src, fs.at[a, k, i], fr.at[a, k, i])
                    second(a, k, i, src)
                    to_core(a, k, i, 0, src)
            k = step - 2
            if 0 <= k < groups:
                for i in range(n1):
                    for j in range(1, n2):
                        src = spot(a, k, i, j, c)
                        arrived(src, ss.at[a, k, flat(a, i, j)], sr.at[a, k, flat(a, i, j)])
                        to_core(a, k, i, j, src)
    far = 1 - x

    @pl.when(holds)
    def _():
        remote(frames_in.at[low], frames_out.at[far], es.at[0], er.at[0], (2 * y + c, far, z)).wait_recv()
        remote(frames_out.at[far], frames_out.at[far], es.at[3], er.at[3], core_peer).start()

    for a in range(count):
        n1, n2 = sizes(a)
        for k in range(groups):
            for i in range(n1):
                for j in range(n2):
                    arrived(spot(a, k, i, j, 1 - c), cs.at[a, k, flat(a, i, j)], cr.at[a, k, flat(a, i, j)])
    @pl.when(holds)
    def _():
        relay = remote(frames_out.at[far], frames_out.at[far], es.at[3], er.at[3], core_peer)
        remote(frames_in.at[low], frames_out.at[x], es.at[0], er.at[0], (2 * y + c, far, z)).wait_send()
        remote(frames_in.at[low], frames_out.at[x], es.at[1], er.at[1], core_peer).wait_send()
        remote(seg_in.at[low], seg_out, es.at[2], er.at[2], core_peer).wait_send()
        relay.wait_send()
        pltpu.make_async_copy(frames_in.at[low], frames_out.at[x], el.at[0]).wait()
        pltpu.make_async_copy(seg_in.at[low], seg_out, el.at[1]).wait()

    @pl.when(jnp.logical_not(holds))
    def _():
        remote(frames_in.at[low], frames_out.at[x], es.at[1], er.at[1], core_peer).wait_recv()
        remote(seg_in.at[low], seg_out, es.at[2], er.at[2], core_peer).wait_recv()
        remote(frames_out.at[far], frames_out.at[far], es.at[3], er.at[3], core_peer).wait_recv()

    for b in range(2):
        stays = (half == c) & (2 * c + b == z)
        away = remote(
            rows_in.at[b], rows_out.at[2 + low], xs.at[b], xr.at[2 + low], (2 * y + half, x, 2 * c + b)
        )
        here = pltpu.make_async_copy(rows_in.at[b], rows_out.at[2 + low], xl.at[2])
        pl.when(jnp.logical_not(stays))(away.wait_send)
        pl.when(stays)(here.wait)
        core_to, x_to = lax.rem(next_piece, 2), lax.div(next_piece, 2)
        exists = x_to < ctx
        stays = (core_to == c) & (x_to == x) & (2 * c + b == z)
        away = remote(
            rows_in.at[b], rows_out.at[low], xs.at[2 + b], xr.at[low],
            (2 * y + core_to, lax.rem(x_to, ctx), 2 * c + b),
        )
        here = pltpu.make_async_copy(rows_in.at[b], rows_out.at[low], xl.at[3])
        pl.when(exists & jnp.logical_not(stays))(away.wait_send)
        pl.when(exists & stays)(here.wait)

    @pl.when(first)
    def _():
        for s in range(2):
            pltpu.make_async_copy(blank, rows_out.at[s], xl.at[s]).wait()

    for s in range(2):
        came = jnp.logical_not((half == c) & (2 * c + s == z))
        pl.when(came)(remote(rows_in.at[0], rows_out.at[2 + s], xs.at[0], xr.at[2 + s], core_peer).wait_recv)
        came = (c == 1) & jnp.logical_not((half == c) & (s == z)) | (c == 0) & (x > 0)
        pl.when(came)(remote(rows_in.at[0], rows_out.at[s], xs.at[0], xr.at[s], core_peer).wait_recv)

    for copy in sent:
        copy.wait_send()
    for copy in mine:
        copy.wait()


def gather_packs(packs, rows, frames, segs, paths, chips, ctx, groups, collective_id):
    count = len(packs)
    side = max(chips, ctx)
    dma = pltpu.SemaphoreType.DMA
    moved = sum(p.size for p in packs) * 2 * (2 * chips * ctx * groups)
    return pl.pallas_call(
        functools.partial(gather_kernel, paths, chips, ctx, groups),
        in_specs=[pl.BlockSpec(memory_space=pltpu.VMEM)] * count
        + [pl.BlockSpec(memory_space=pl.ANY)] * 3,
        out_specs=[pl.BlockSpec(memory_space=pl.ANY)] * (count + 3),
        out_shape=[sds((groups, chips, 2, ctx) + p.shape, p.dtype) for p in packs]
        + [
            sds((4,) + rows.shape[1:], bf16),
            sds((ctx,) + frames.shape[1:], bf16),
            sds(segs.shape[1:], f32),
        ],
        scratch_shapes=[
            pltpu.VMEM(rows.shape[1:], bf16),
            dma((count,)),
            dma((count, groups)),
            dma((count, groups)),
            dma((count, groups, side)),
            dma((count, groups, side)),
            dma((count, groups, chips * ctx)),
            dma((count, groups, chips * ctx)),
            dma((count, groups, chips * ctx)),
            dma((count, groups, chips * ctx)),
            dma((4,)),
            dma((4,)),
            dma((4,)),
            dma((4,)),
            dma((4,)),
            dma((2,)),
        ],
        compiler_params=pltpu.CompilerParams(
            collective_id=collective_id, has_side_effects=True, vmem_limit_bytes=8 * 1024 * 1024
        ),
        cost_estimate=cost(0, 0, 10 * moved),
        name="gather_packs",
    )(*packs, rows, frames, segs)


def reduce_kernel(paths, chips, ctx, groups, *refs):
    count = len(paths)
    grads, (de, dh, da, dr1, xo, gain) = refs[:count], refs[count : count + 6]
    refs = refs[count + 6 :]
    outs, (gx, ge) = refs[:count], refs[count : count + 2]
    at = count + 2
    bufs = [refs[at + 7 * a : at + 7 * a + 7] for a in range(count)]
    at = at + 7 * count
    hbuf, gbuf, rce, se, rxe, qe = refs[at : at + 6]
    cs, cr, s1, r1, s2, r2, zs, zr, hs, hr, es, er, gs, gr, gl = refs[at + 6 :]
    y, c, x, z = place_of(chips, ctx, groups)
    half, low = lax.div(z, 2), lax.rem(z, 2)
    core_peer = (2 * y + 1 - c, x, z)
    greet(chips, ctx, groups, y, c, x, z)
    sent = []

    def sizes(a):
        return (ctx, chips) if paths[a] == "xy" else (chips, ctx)

    def mine(a):
        return (x, y) if paths[a] == "xy" else (y, x)

    def peer(a, first, index):
        if (paths[a] == "xy") == first:
            return (2 * y + c, index, z)
        return (2 * index + c, x, z)

    def send(src, dst, ssem, rsem, device):
        copy = pltpu.make_async_remote_copy(
            src_ref=src, dst_ref=dst, send_sem=ssem, recv_sem=rsem,
            device_id=device, device_id_type=MESH_ID,
        )
        copy.start()
        sent.append(copy)

    def arrived(dst, ssem, rsem):
        pltpu.make_async_remote_copy(
            src_ref=dst, dst_ref=dst, send_sem=ssem, recv_sem=rsem,
            device_id=(2 * y + 1 - c, x, z), device_id_type=MESH_ID,
        ).wait_recv()

    def group(g):
        return lax.rem(z + 1 + g, groups)

    def remote(src, dst, ssem, rsem, device):
        return pltpu.make_async_remote_copy(
            src_ref=src, dst_ref=dst, send_sem=ssem, recv_sem=rsem,
            device_id=device, device_id_type=MESH_ID,
        )

    piece = 2 * x + c
    prev = lax.rem(piece + 2 * ctx - 1, 2 * ctx)
    prev_core, prev_x = lax.rem(prev, 2), lax.div(prev, 2)
    to_prev = remote(dh, hbuf, hs, hr, (2 * y + prev_core, prev_x, z))
    pl.when(piece > 0)(to_prev.start)

    send(de.at[1 - c], rce, es.at[0], er.at[0], core_peer)

    for g in range(groups):
        for a in range(count):
            send(
                grads[a].at[group(g), :, 1 - c], bufs[a][0].at[group(g)], cs.at[a, g], cr.at[a, g],
                (2 * y + 1 - c, x, z),
            )

    def stage1(g):
        t = group(g)
        for a in range(count):
            rc, p1, b1 = bufs[a][0], bufs[a][1], bufs[a][2]
            arrived(rc.at[t], cs.at[a, g], cr.at[a, g])
            for yy in range(chips):
                for xx in range(ctx):
                    i, j = (xx, yy) if paths[a] == "xy" else (yy, xx)
                    total = grads[a][t, yy, c, xx].astype(f32) + rc[t, yy, xx].astype(f32)
                    p1[t, i, j] = total.astype(bf16)
            n1, _ = sizes(a)
            for i in range(1, n1):
                index = lax.rem(mine(a)[0] + i, n1)
                send(
                    p1.at[t, index], b1.at[t, i - 1], s1.at[a, g, i], r1.at[a, g, i],
                    peer(a, True, index),
                )

    def stage2(g):
        t = group(g)
        for a in range(count):
            p1, b1, p2, b2 = bufs[a][1:5]
            n1, n2 = sizes(a)
            for i in range(1, n1):
                arrived(b1.at[t, i - 1], s1.at[a, g, i], r1.at[a, g, i])
            for j in range(n2):
                total = p1[t, mine(a)[0], j].astype(f32)
                for i in range(1, n1):
                    total = total + b1[t, i - 1, j].astype(f32)
                p2[t, j] = total.astype(bf16)
            for j in range(1, n2):
                index = lax.rem(mine(a)[1] + j, n2)
                send(
                    p2.at[t, index], b2.at[t, j - 1], s2.at[a, g, j], r2.at[a, g, j],
                    peer(a, False, index),
                )

    def stage3(g):
        t = group(g)
        for a in range(count):
            p2, b2, p3, b3 = bufs[a][3:7]
            _, n2 = sizes(a)
            for j in range(1, n2):
                arrived(b2.at[t, j - 1], s2.at[a, g, j], r2.at[a, g, j])
            total = p2[t, mine(a)[1]].astype(f32)
            for j in range(1, n2):
                total = total + b2[t, j - 1].astype(f32)
            if g == groups - 1:
                outs[a][...] = total
            else:
                p3[g] = total.astype(bf16)
                send(p3.at[g], b3.at[g], zs.at[a, g], zr.at[a, g], (2 * y + c, x, t))

    def home(src, dst, k, s):
        stays = (half == c) & (2 * c + s == z)
        away = remote(
            src.at[s], dst.at[low], gs.at[k, s], gr.at[k, low], (2 * y + half, x, 2 * c + s)
        )
        here = pltpu.make_async_copy(src.at[s], dst.at[low], gl.at[k])
        return stays, away, here

    def go_home(src, dst, k):
        for s in range(2):
            stays, away, here = home(src, dst, k, s)
            pl.when(jnp.logical_not(stays))(away.start)
            pl.when(stays)(here.start)

    def settle(src, dst, k):
        for s in range(2):
            stays, away, here = home(src, dst, k, s)
            pl.when(jnp.logical_not(stays))(away.wait_send)
            pl.when(stays)(here.wait)
        for b in range(2):
            came = jnp.logical_not((half == c) & (2 * c + b == z))
            pl.when(came)(remote(src.at[0], dst.at[b], gs.at[k, 0], gr.at[k, b], core_peer).wait_recv)

    def frames1():
        arrived(rce, es.at[0], er.at[0])
        for h in range(ctx):
            se[h] = (de[c, h].astype(f32) + rce[h].astype(f32)).astype(bf16)
        send(se.at[1 - x], rxe, es.at[1], er.at[1], (2 * y + c, 1 - x, z))

    def frames2():
        arrived(rxe, es.at[1], er.at[1])
        total = (se[x].astype(f32) + rxe[...].astype(f32)).astype(bf16)
        quarter = qe.shape[2]
        for s in range(2):
            qe[s] = total[:, s * quarter : (s + 1) * quarter]
        go_home(qe, ge, 1)

    def rows_back():
        last = piece == 2 * ctx - 1

        @pl.when(last)
        def _():
            hbuf[...] = jnp.zeros_like(hbuf)

        @pl.when(jnp.logical_not(last))
        def _():
            remote(dh, hbuf, hs, hr, core_peer).wait_recv()

        sub = gbuf.shape[1]
        for i in range(gbuf.shape[0]):
            at = slice(i * sub, (i + 1) * sub)
            zn, rate = norm_parts(xo[at, :].astype(f32))
            total = da[at, :] + hbuf[at, :].astype(f32)
            gbuf[i] = (dr1[at, :] + norm_back(zn, rate, gain[...], total)).astype(bf16)
        go_home(gbuf, gx, 0)

    for g in range(groups):
        stage1(g)
    frames1()
    rows_back()
    for g in range(groups + 1):
        if g < groups:
            stage2(g)
        if g > 0:
            stage3(g - 1)
        if g == 1:
            frames2()
    for a in range(count):
        b3 = bufs[a][6]
        for g in range(groups - 1):
            arrived(b3.at[g], zs.at[a, g], zr.at[a, g])
            outs[a][...] += b3[g].astype(f32)
    settle(gbuf, gx, 0)
    settle(qe, ge, 1)
    pl.when(piece > 0)(to_prev.wait_send)
    for copy in sent:
        copy.wait_send()


def reduce_packs(grads, de, dh, da, dr1, xo, gain, paths, chips, ctx, groups, collective_id):
    count = len(grads)
    side = max(chips, ctx)
    own, width = dr1.shape
    held = de.shape[2]
    dma = pltpu.SemaphoreType.DMA
    scratch = []
    for a in range(count):
        block = grads[a].shape[4:]
        n1, n2 = (ctx, chips) if paths[a] == "xy" else (chips, ctx)
        for lead in (
            (groups, chips, ctx), (groups, n1, n2), (groups, n1 - 1, n2), (groups, n2),
            (groups, n2 - 1), (groups - 1,), (groups - 1,),
        ):
            scratch.append(pltpu.VMEM(lead + block, bf16))
    return pl.pallas_call(
        functools.partial(reduce_kernel, paths, chips, ctx, groups),
        in_specs=[pl.BlockSpec(memory_space=pltpu.VMEM)] * (count + 6),
        out_specs=[pl.BlockSpec(memory_space=pltpu.VMEM)] * (count + 2),
        out_shape=[sds(g.shape[4:], f32) for g in grads]
        + [sds((2, own // 2, width), bf16), sds((2, held, width // 4), bf16)],
        scratch_shapes=scratch
        + [
            pltpu.VMEM((own, width), bf16),
            pltpu.VMEM((2, own // 2, width), bf16),
            pltpu.VMEM((ctx, held, width // 2), bf16),
            pltpu.VMEM((ctx, held, width // 2), bf16),
            pltpu.VMEM((held, width // 2), bf16),
            pltpu.VMEM((2, held, width // 4), bf16),
            dma((count, groups)),
            dma((count, groups)),
            dma((count, groups, side)),
            dma((count, groups, side)),
            dma((count, groups, side)),
            dma((count, groups, side)),
            dma((count, groups)),
            dma((count, groups)),
            dma(()),
            dma(()),
            dma((2,)),
            dma((2,)),
            dma((2, 2)),
            dma((2, 2)),
            dma((2,)),
        ],
        compiler_params=pltpu.CompilerParams(
            collective_id=collective_id, has_side_effects=True, vmem_limit_bytes=VMEM_LIMIT
        ),
        cost_estimate=cost(0, 0, 10 * sum(g.size for g in grads)),
        name="reduce_packs",
    )(*grads, de, dh, da, dr1, xo, gain)


def unpack_kernel(g1_ref, permh_ref, permu_ref, vec_ref, hb_ref, ub_ref):
    block = g1_ref[0, :, 64:]

    @pl.when(pl.program_id(0) == 0)
    def _():
        vec_ref[...] = block.astype(f32).T[0:16]

    hb_ref[0] = tn(block, permh_ref[...])[16:24]
    ub_ref[0] = tn(block, permu_ref[...])[24:25]


def pack_kernel(gr1_ref, vec_ref, h1_ref, h2_ref, ubg_ref, permh_ref, permu_ref, out_ref):
    width = vec_ref.shape[1]
    heads = jnp.concatenate([h1_ref[0, 0:2], h2_ref[0, 0:2], jnp.zeros((4, h1_ref.shape[2]), f32)])
    units = jnp.broadcast_to(ubg_ref[0], (8, width))
    small = jnp.concatenate(
        [
            vec_ref[...].T,
            nt(permh_ref[...], heads.astype(bf16)),
            nt(permu_ref[...], units.astype(bf16)),
            jnp.zeros((width, 32), f32),
        ],
        axis=1,
    )
    out_ref[0] = jnp.concatenate([gr1_ref[0, :, :64], small.astype(bf16)], axis=1)


def on_device(
    hidden_in, encoder_states, segment_ids, out_grad,
    norm1_gain, norm1_bias, norm2_gain, norm2_bias, norm3_gain, norm3_bias,
    self_query, self_key, self_value, self_output,
    cross_query, cross_key, cross_value, cross_output,
    fc_up, fc_down,
    self_query_bias, self_value_bias, cross_query_bias, cross_value_bias, up_bias,
    self_output_bias, cross_output_bias, down_bias,
):
    F, C, T = lax.axis_size("fsdp"), lax.axis_size("ctx"), lax.axis_size("tp")
    batches, sub, width = hidden_in.shape
    length = segment_ids.shape[1]
    frames_own = encoder_states.shape[1]
    assert T == 2 * batches and T == 4 and F % 2 == 0 and C == 2
    own = 2 * sub
    part = width // (F * C)
    hw = self_query.shape[1]
    units = fc_up.shape[1]
    heads = self_query_bias.shape[0]
    f, x, z = lax.axis_index("fsdp"), lax.axis_index("ctx"), lax.axis_index("tp")
    core = lax.rem(f, 2)
    odd = lax.rem(z, 2)
    tfc = ("tp", "fsdp", "ctx")

    def round_pairs(r):
        pairs = []
        for m in range(F // 2):
            for c in range(2):
                for zz in range(T):
                    b = (r + zz) % 2
                    pairs.append(((2 * m + c) * T + zz, (2 * m + zz // 2) * T + 2 * c + b))
        return pairs

    rounds = [round_pairs(0), round_pairs(1)]
    backs = [[(d, s) for s, d in pairs] for pairs in rounds]
    axes = ("fsdp", "tp")

    def pick(values, index):
        return lax.dynamic_index_in_dim(values, index, 0, keepdims=False)

    def spread(values):
        first = lax.ppermute(pick(values, odd), axes, rounds[0])
        second = lax.ppermute(pick(values, 1 - odd), axes, rounds[1])
        even = odd == 0
        return jnp.concatenate(
            [jnp.where(even, first, second), jnp.where(even, second, first)], axis=0
        )

    def collect(values):
        first = lax.ppermute(pick(values, odd), axes, backs[0])
        second = lax.ppermute(pick(values, 1 - odd), axes, backs[1])
        even = odd == 0
        return jnp.stack([jnp.where(even, first, second), jnp.where(even, second, first)])

    vecs = (
        norm1_gain, norm1_bias, norm2_gain, norm2_bias, norm3_gain, norm3_bias,
        self_output_bias, cross_output_bias, down_bias,
    )
    hbs = (self_query_bias, self_value_bias, cross_query_bias, cross_value_bias)
    def column_of(values):
        return jnp.pad(values.reshape(1, -1), ((0, 0), (0, part - values.size)))

    blank = jnp.zeros((1, part), bf16)
    small = jnp.concatenate(
        [v.reshape(1, part) for v in vecs] + [blank] * (16 - len(vecs))
        + [column_of(v) for v in hbs] + [blank] * 4
        + [up_bias.reshape(1, part)] + [blank] * 39
    ).T
    pack1 = jnp.concatenate([self_query, self_key, self_value, small], axis=1)
    pack2 = jnp.concatenate(
        [
            self_output.T, cross_output.T, cross_key, cross_value, cross_query,
            jnp.zeros((part, 64), bf16),
        ],
        axis=1,
    )
    pack3 = jnp.concatenate([fc_up, fc_down.T], axis=1)

    def gather(block):
        full = lax.all_gather(block, tfc, axis=0, tiled=True)
        return full.reshape(T, width, block.shape[1])

    chips = F // 2
    g1, g2, xa, frames, seg_row = gather_packs(
        (pack1, pack2), hidden_in, encoder_states, segment_ids.astype(f32)[:, None, :],
        ("yx", "xy"), chips, C, T, 0,
    )
    g1 = g1.reshape(T, width, pack1.shape[1])
    g2 = g2.reshape(T, width, pack2.shape[1])
    xa = xa.reshape(2 * own, width)
    xo = xa[own:]
    seg_row = seg_row.reshape(length)

    piece = x * 2 + core
    seg_own = lax.dynamic_slice_in_dim(seg_row, piece * own, own)
    seg_halo = lax.dynamic_slice_in_dim(seg_row, jnp.maximum(piece - 1, 0) * own, own)
    seg_halo = jnp.where(piece == 0, -1.0, seg_halo)
    segk = jnp.concatenate([seg_halo, seg_own]).reshape(2 * own, 1)
    segq = seg_own.reshape(own // QT, 1, QT)
    ends = seg_own.reshape(own // QT, QT)
    span = jnp.stack([ends[:, 0], ends[:, -1]], axis=1).reshape(-1).astype(jnp.int32)

    frames_all = 2 * frames_own
    per_doc = -(-frames_all // (DOCS * 32)) * 32
    slots = DOCS * per_doc
    counts = jnp.asarray([float(-(-(frames_all - d) // DOCS)) for d in range(DOCS)], f32)

    out_grad, pack3, g1 = lax.optimization_barrier((out_grad, pack3, g1))
    g3 = gather(pack3)
    dy = spread(out_grad)

    per = self_query_bias.shape[1]
    row_id = lax.broadcasted_iota(jnp.int32, (width, 1), 0)
    owner_id, local_id = row_id // part, row_id % part
    head_to = (local_id // per) * HEAD_DIM + owner_id * per + local_id % per
    head_to = jnp.where(local_id < heads * per, head_to, -1)
    permh = (head_to == lax.broadcasted_iota(jnp.int32, (1, hw), 1)).astype(bf16)
    wide = up_bias.shape[1]
    unit_to = (local_id // wide) * (units // heads) + owner_id * wide + local_id % wide
    permu = (unit_to == lax.broadcasted_iota(jnp.int32, (1, units), 1)).astype(bf16)
    spare = pl.BlockSpec((1, width, 128), lambda t: (t, 0, 3 * hw // 128))
    vec_all, hb_t, ub_all = pl.pallas_call(
        unpack_kernel,
        grid=(T,),
        in_specs=[spare, whole(permh.shape), whole(permu.shape)],
        out_specs=[whole((16, width)), step_of((T, 8, hw)), step_of((T, 1, units))],
        out_shape=[sds((16, width), f32), sds((T, 8, hw), f32), sds((T, 1, units), f32)],
        compiler_params=params(1),
        cost_estimate=cost(2 * 64 * width * (hw + units) * T, 0, 6 * width * width),
        name="unpack",
    )(g1, permh, permu)
    hb_all = hb_t[:, 0:4].transpose(1, 0, 2)[:, :, None, :]

    zeros_hb = jnp.zeros((T, 1, hw), f32)
    pb = jnp.concatenate([hb_all[0], zeros_hb, hb_all[1]], axis=2)
    kb = jnp.concatenate([zeros_hb, hb_all[3]], axis=2)

    nq = own // QT
    a1, qkv, o, lse1 = pl.pallas_call(
        fwd1_kernel,
        grid=(T,),
        in_specs=[
            whole((2 * own, width)),
            step_of(g1.shape),
            whole((1, width)),
            whole((1, width)),
            step_of((T, 1, 3 * hw)),
            whole((2 * own, 1)),
            whole((nq, 1, QT)),
        ],
        out_specs=[
            whole((2 * own, width)),
            step_of((T, 2 * own, 3 * hw)),
            step_of((T, own, hw)),
            step_of((T, nq, 8, QT)),
        ],
        out_shape=[
            sds((2 * own, width), bf16),
            sds((T, 2 * own, 3 * hw), bf16),
            sds((T, own, hw), bf16),
            sds((T, nq, 8, QT), f32),
        ],
        compiler_params=params(1),
        cost_estimate=cost(2 * 2 * own * width * 3 * hw * T + 4 * own * (own + QT) * hw * T, own * (own + QT) * heads * T, 2 * g1.size + 12 * own * width),
        name="fwd1",
    )(xa, g1, vec_all[0:1], vec_all[1:2], pb, segk, segq)

    smem = pl.BlockSpec(memory_space=pltpu.SMEM)
    vm = pl.BlockSpec(memory_space=pltpu.VMEM)
    ckv, r1, a2, cq, co, lse2, r2, a3, ep = pl.pallas_call(
        fwd2_kernel,
        in_specs=[smem] + [vm] * 8 + [smem],
        out_specs=[vm] * 9,
        out_shape=[
            sds((T, slots, 2 * hw), bf16),
            sds((own, width), f32),
            sds((own, width), bf16),
            sds((T, own, hw), bf16),
            sds((T, own, hw), bf16),
            sds((T, nq, 8, QT), f32),
            sds((own, width), f32),
            sds((own, width), bf16),
            sds((slots, width), bf16),
        ],
        scratch_shapes=[pltpu.VMEM((nq, T, hw, QT), f32), pltpu.VMEM((width // 128, slots, 128), f32)],
        compiler_params=params(),
        cost_estimate=cost(2 * (2 * slots + 3 * own) * width * hw * T + 4 * own * slots * hw, own * per_doc * heads * T, 2 * g2.size + 20 * own * width),
        name="fwd2",
    )(
        span, g2, frames, xo, o,
        jnp.concatenate(
            [vec_all[6:7], vec_all[2:4], vec_all[7:8], vec_all[4:6], vec_all[8:9], vec_all[8:9]]
        ),
        hb_all[2], kb, segq, counts,
    )

    out_rows, dr2, gr3, ubg, vecg3 = pl.pallas_call(
        ff_kernel,
        grid=(T,),
        in_specs=[
            whole((own, width)),
            whole((own, width)),
            whole((own, width)),
            step_of(g3.shape),
            step_of((T, 1, units)),
            whole((2, width)),
        ],
        out_specs=[
            whole((own, width)),
            whole((own, width)),
            step_of(g3.shape),
            step_of((T, 1, units)),
            whole((8, width)),
        ],
        out_shape=[
            sds((own, width), bf16),
            sds((own, width), f32),
            sds(g3.shape, bf16),
            sds((T, 1, units), f32),
            sds((8, width), f32),
        ],
        scratch_shapes=[
            pltpu.VMEM((width, own), bf16),
            pltpu.VMEM((width, own), bf16),
            pltpu.VMEM((own, width), f32),
            pltpu.VMEM((own, width), f32),
            pltpu.VMEM((own, units), bf16),
            pltpu.VMEM((own, units), bf16),
        ],
        compiler_params=params(1),
        cost_estimate=cost(12 * own * width * units * T, 2 * own * units * T, 4 * g3.size + 12 * own * width),
        name="ff",
    )(a3, r2, dy, g3, ub_all, jnp.concatenate([vec_all[4:5], vec_all[8:9]]))

    def scatter(block):
        return lax.psum_scatter(
            block.reshape(T * width, block.shape[2]), tfc, scatter_dimension=0, tiled=True
        )

    sum3 = scatter(gr3)
    out_final = collect(out_rows.reshape(2, sub, width))

    dr1, do, gr2, de, vecg2, hbg2 = pl.pallas_call(
        bwd2_kernel,
        in_specs=[smem] + [vm] * 12 + [smem],
        out_specs=[vm] * 6,
        out_shape=[
            sds((own, width), f32),
            sds((T, own, hw), bf16),
            sds(g2.shape, bf16),
            sds((2, C, frames_own, width // 2), bf16),
            sds((8, width), f32),
            sds((T, 8, hw), f32),
        ],
        scratch_shapes=[
            pltpu.VMEM((T, own, hw), bf16),
            pltpu.VMEM((T, own, hw), bf16),
            pltpu.VMEM((T, slots, 2 * hw), f32),
            pltpu.VMEM((T, slots, 2 * hw), bf16),
            pltpu.VMEM((width, own), bf16),
            pltpu.VMEM((width, slots), bf16),
            pltpu.VMEM((T, hw, QT), f32),
            pltpu.VMEM((width // 128, slots, 128), f32),
        ],
        compiler_params=params(),
        cost_estimate=cost(2 * (4 * slots + 6 * own) * width * hw * T + 10 * own * slots * hw, own * per_doc * heads * T, 4 * g2.size + 30 * own * width),
        name="bwd2",
    )(span, g2, ep, dr2, cq, ckv, co, lse2, a2, r1, o, vec_all[2:3], segq, counts)

    da, dh, gr1, vecg1, hbg1 = pl.pallas_call(
        bwd1_kernel,
        grid=(T,),
        in_specs=[
            whole((2 * own, width)),
            whole((2 * own, width)),
            step_of(g1.shape),
            step_of(qkv.shape),
            step_of(o.shape),
            step_of(do.shape),
            step_of(lse1.shape),
            whole((2 * own, 1)),
            whole((nq, 1, QT)),
        ],
        out_specs=[
            whole((own, width)),
            whole((own, width)),
            step_of(g1.shape),
            whole((8, width)),
            step_of((T, 8, hw)),
        ],
        out_shape=[
            sds((own, width), f32),
            sds((own, width), bf16),
            sds(g1.shape, bf16),
            sds((8, width), f32),
            sds((T, 8, hw), f32),
        ],
        scratch_shapes=[
            pltpu.VMEM((width, 2 * own), bf16),
            pltpu.VMEM((2 * own, width), f32),
            pltpu.VMEM((2 * own, hw), f32),
            pltpu.VMEM((2 * own, hw), f32),
            pltpu.VMEM((own, hw), bf16),
            pltpu.VMEM((2 * own, 3 * hw), bf16),
        ],
        compiler_params=params(1),
        cost_estimate=cost(2 * 4 * own * width * 3 * hw * T + 10 * own * (own + QT) * hw * T, own * (own + QT) * heads * T, 4 * g1.size + 30 * own * width),
        name="bwd1",
    )(xa, a1, g1, qkv, o, do, lse1, segk, segq)

    vec_g = jnp.concatenate(
        [vecg1[0:2], vecg2[0:2], vecg3[0:2], vecg2[3:4], vecg2[2:3], vecg3[2:3]]
    )
    third = part // T
    vec_g = jnp.pad(vec_g, ((0, 16 - len(vecs)), (0, 0)))
    gr1 = pl.pallas_call(
        pack_kernel,
        grid=(T,),
        in_specs=[
            spare, whole((16, width)), step_of(hbg1.shape), step_of(hbg2.shape),
            step_of(ubg.shape), whole(permh.shape), whole(permu.shape),
        ],
        out_specs=spare,
        out_shape=sds(gr1.shape, bf16),
        input_output_aliases={0: 0},
        compiler_params=params(1),
        cost_estimate=cost(2 * 16 * width * (hw + units) * T, 0, 6 * width * width),
        name="pack",
    )(gr1, vec_g, hbg1, hbg2, ubg, permh, permu)
    split = (T, chips, 2, C, part)
    sum1, sum2, grad_hidden, grad_encoder = reduce_packs(
        (gr1.reshape(split + gr1.shape[2:]), gr2.reshape(split + gr2.shape[2:])),
        de, dh, da, dr1, xo, vec_all[0:1], ("xy", "yx"), chips, C, T, 1,
    )
    grad_hidden = grad_hidden.astype(f32)
    grad_encoder = grad_encoder.astype(f32)

    sum3 = sum3.astype(f32)
    vout = lax.dynamic_slice_in_dim(sum1[:, 3 * hw : 3 * hw + 16], z * third, third).T
    hout = sum1[: heads * per, 3 * hw + 16 : 3 * hw + 20].T.reshape(4, heads, per)
    uout = sum1[:, 3 * hw + 24].reshape(up_bias.shape)

    def cut(array, k):
        return array[:, k * hw : (k + 1) * hw]

    return (
        out_final,
        grad_hidden,
        grad_encoder,
        vout[0], vout[1], vout[2], vout[3], vout[4], vout[5],
        cut(sum1, 0), cut(sum1, 1), cut(sum1, 2), cut(sum2, 0).T,
        cut(sum2, 4), cut(sum2, 2), cut(sum2, 3), cut(sum2, 1).T,
        sum3[:, :units], sum3[:, units:].T,
        hout[0], hout[1], hout[2], hout[3], uout,
        vout[6], vout[7], vout[8],
    )


def solution(mesh):
    column = P(("fsdp", "ctx"), "tp")
    row = P("tp", ("fsdp", "ctx"))
    vector = P(("fsdp", "ctx"))
    vector_out = P(("fsdp", "ctx", "tp"))
    tokens = P("fsdp", ("ctx", "tp"), None)
    return jax.shard_map(
        on_device,
        mesh=mesh,
        in_specs=(tokens, P("fsdp", "ctx", None), P("fsdp", None), tokens)
        + (vector,) * 6
        + (column, column, column, row)
        + (column, column, column, row)
        + (column, row)
        + (row,) * 5
        + (vector,) * 3,
        out_specs=(tokens, tokens, P("fsdp", "ctx", "tp"))
        + (vector_out,) * 6
        + (column, column, column, row)
        + (column, column, column, row)
        + (column, row)
        + (row,) * 5
        + (vector_out,) * 3,
        check_vma=False,
    )
```

```python
import functools
import math

import jax
import jax.numpy as jnp
from jax import lax
from jax.experimental import pallas as pl
from jax.experimental.pallas import tpu as pltpu
from jax.sharding import PartitionSpec as P

HEAD_DIM = 64
DOCS = 16
EPSILON = 1e-05
MASKED = -1e30
SCALE = HEAD_DIM ** (-0.5)
QT = 128

f32 = jnp.float32
bf16 = jnp.bfloat16

VMEM_LIMIT = 62 * 1024 * 1024


def nn(a, b):
    return lax.dot_general(a, b, (((1,), (0,)), ((), ())), preferred_element_type=f32)


def nt(a, b):
    return lax.dot_general(a, b, (((1,), (1,)), ((), ())), preferred_element_type=f32)


def tn(a, b):
    return lax.dot_general(a, b, (((0,), (0,)), ((), ())), preferred_element_type=f32)


def norm_parts(values):
    centred = values - jnp.mean(values, axis=-1, keepdims=True)
    rate = lax.rsqrt(jnp.mean(centred * centred, axis=-1, keepdims=True) + EPSILON)
    return centred * rate, rate


def norm_back(z, rate, gain, grad):
    scaled = gain * grad
    return rate * (
        scaled
        - jnp.mean(scaled, axis=-1, keepdims=True)
        - z * jnp.mean(scaled * z, axis=-1, keepdims=True)
    )


def row_sum(values):
    return jnp.sum(values, axis=0, keepdims=True)


def spread_heads(block):
    heads = block.shape[1] // HEAD_DIM
    lanes = lax.broadcasted_iota(jnp.int32, (1, block.shape[1]), 1)
    parts = []
    for i in range(heads):
        mine = (lanes >= i * HEAD_DIM) & (lanes < (i + 1) * HEAD_DIM)
        parts.append(block * jnp.where(mine, 1.0, 0.0).astype(block.dtype))
    return jnp.concatenate(parts, axis=0)


def own_blocks(matrix):
    heads = matrix.shape[0] // HEAD_DIM
    return jnp.concatenate(
        [
            matrix[i * HEAD_DIM : (i + 1) * HEAD_DIM, i * QT : (i + 1) * QT]
            for i in range(heads)
        ],
        axis=0,
    )


def head_row(matrix):
    heads = matrix.shape[0] // HEAD_DIM
    return jnp.concatenate(
        [row_sum(matrix[i * HEAD_DIM : (i + 1) * HEAD_DIM]) for i in range(heads)], axis=1
    )


def for_heads(block, heads):
    return jnp.concatenate([block] * heads, axis=1)


def window_mask(segk_ref, segq_ref, n, halo, window):
    keys = segk_ref[pl.ds(n * QT, window), :]
    same = keys == segq_ref[n]
    ahead = lax.broadcasted_iota(jnp.int32, (window, QT), 0) - lax.broadcasted_iota(
        jnp.int32, (window, QT), 1
    )
    return jnp.where(same & (ahead <= halo), 0.0, MASKED)


def fwd1_kernel(
    xa_ref, g1_ref, permh_ref, permu_ref, segk_ref, segq_ref,
    a1_ref, qkv_ref, o_ref, lse_ref, vec_ref, hb_ref, ub_ref,
):
    rows = xa_ref.shape[0]
    own = segq_ref.shape[0] * QT
    halo = rows - own
    window = halo + QT
    hw = o_ref.shape[2]
    tile = 256
    heads = hw // HEAD_DIM
    small = g1_ref[0, :, 3 * hw :]
    head_rows = tn(small, permh_ref[...])
    unit_rows = tn(small, permu_ref[...])
    biases = [row_parts(head_rows, 16 + heads * w, heads) for w in range(4)]
    hb_ref[0] = jnp.concatenate(biases + [jnp.zeros((4, hw), f32)], axis=0)
    ub_ref[0] = row_parts(unit_rows, 16 + 4 * heads, heads)
    bias = jnp.concatenate([biases[0], jnp.zeros((1, hw), f32), biases[1]], axis=1)

    @pl.when(pl.program_id(0) == 0)
    def _():
        vec_ref[...] = small.astype(f32).T[0:16]

        def body(i, _):
            at = pl.ds(i * tile, tile)
            z, _ = norm_parts(xa_ref[at, :].astype(f32))
            a1_ref[at, :] = (z * vec_ref[0:1, :] + vec_ref[1:2, :]).astype(bf16)
            return 0

        lax.fori_loop(0, rows // tile, body, 0)

    w = g1_ref[0, :, : 3 * hw]

    def project(i, _):
        at = pl.ds(i * tile, tile)
        qkv_ref[0, at, :] = (nn(a1_ref[at, :], w) + bias).astype(bf16)
        return 0

    lax.fori_loop(0, rows // tile, project, 0)

    def attend(n, _):
        add = window_mask(segk_ref, segq_ref, n, halo, window)
        block = qkv_ref[0, pl.ds(n * QT, window), :]
        spread = spread_heads(block[halo:, :hw] * bf16(SCALE))
        scores = nt(block[:, hw : 2 * hw], spread) + for_heads(add, heads)
        top = jnp.max(scores, axis=0, keepdims=True)
        weights = jnp.exp(scores - top)
        total = jnp.sum(weights, axis=0, keepdims=True)
        mixed = own_blocks(tn(block[:, 2 * hw :], weights.astype(bf16)) / total)
        lse_ref[0, n] = top + jnp.log(total)
        o_ref[0, pl.ds(n * QT, QT), :] = mixed.T.astype(bf16)
        return 0

    lax.fori_loop(0, own // QT, attend, 0)


def fwd2_kernel(
    span_ref, g2_ref, e_ref, xo_ref, o_ref, vec_ref, hb_ref, segq_ref, count_ref,
    ckv_ref, r1_ref, a2_ref, cq_ref, co_ref, lse_ref, r2_ref, a3_ref, ep_ref, acc_ref, wide_ref, spread_ref,
):
    groups = g2_ref.shape[0]
    half = e_ref.shape[1]
    own = xo_ref.shape[0]
    hw = o_ref.shape[2]
    slots = ep_ref.shape[0]
    per_doc = slots // DOCS
    heads = hw // HEAD_DIM
    tile = 256

    def regroup(i, _):
        lane = pl.ds(pl.multiple_of(i * 128, 128), 128)
        wide_ref[i, 0:half, :] = e_ref[0, :, lane].astype(f32)
        wide_ref[i, half : 2 * half, :] = e_ref[1, :, lane].astype(f32)
        wide_ref[i, 2 * half :, :] = jnp.zeros((slots - 2 * half, 128), f32)
        for d in range(DOCS):
            ep_ref[d * per_doc : (d + 1) * per_doc, lane] = wide_ref[
                i, pl.ds(d, per_doc, stride=DOCS), :
            ].astype(bf16)
        return 0

    lax.fori_loop(0, ep_ref.shape[1] // 128, regroup, 0)

    def frame_group(t, _):
        bias = jnp.concatenate([jnp.zeros((1, hw), f32), hb_ref[t, 3:4, :]], axis=1)

        def frames(i, _, bias=bias):
            at = pl.ds(i * tile, tile)
            y = nn(ep_ref[at, :], g2_ref[t, :, 2 * hw : 4 * hw]) + bias
            ckv_ref[t, at, :] = y.astype(bf16)
            return 0

        lax.fori_loop(0, slots // tile, frames, 0)
        return 0

    lax.fori_loop(0, groups, frame_group, 0)

    def middle(i, _):
        at = pl.ds(i * tile, tile)
        r1 = xo_ref[at, :].astype(f32) + vec_ref[6:7, :]
        for t in range(groups):
            r1 = r1 + nt(o_ref[t, at, :], g2_ref[t, :, 0:hw])
        r1_ref[at, :] = r1
        z, _ = norm_parts(r1)
        a2 = (z * vec_ref[2:3, :] + vec_ref[3:4, :]).astype(bf16)
        a2_ref[at, :] = a2
        for t in range(groups):
            cq_ref[t, at, :] = (nn(a2, g2_ref[t, :, 4 * hw : 5 * hw]) + hb_ref[t, 2:3, :]).astype(bf16)
        return 0

    lax.fori_loop(0, own // tile, middle, 0)

    acc_ref[...] = jnp.zeros_like(acc_ref)
    lse_ref[...] = jnp.zeros_like(lse_ref)
    place = lax.broadcasted_iota(jnp.int32, (per_doc, QT), 0).astype(f32)

    def attend(n, _):
        segs = segq_ref[n]
        for t in range(groups):
            spread_ref[t] = spread_heads(cq_ref[t, pl.ds(n * QT, QT), :] * bf16(SCALE))

        def document(d, _):
            col = for_heads(jnp.where(segs == d.astype(f32), 1.0, 0.0), heads)
            add = for_heads(jnp.where(place < count_ref[d], 0.0, MASKED), heads)
            for t in range(groups):
                kv = ckv_ref[t, pl.ds(d * per_doc, per_doc), :]
                scores = nt(kv[:, :hw], spread_ref[t]) + add
                top = jnp.max(scores, axis=0, keepdims=True)
                weights = jnp.exp(scores - top)
                total = jnp.sum(weights, axis=0, keepdims=True)
                mixed = tn(kv[:, hw:], weights.astype(bf16)) * (col / total)
                acc_ref[n, t] += own_blocks(mixed)
                lse_ref[t, n] += col * (top + jnp.log(total))
            return 0

        lax.fori_loop(span_ref[2 * n], span_ref[2 * n + 1] + 1, document, 0)
        for t in range(groups):
            co_ref[t, pl.ds(n * QT, QT), :] = acc_ref[n, t].T.astype(bf16)
        return 0

    lax.fori_loop(0, own // QT, attend, 0)

    def final(i, _):
        at = pl.ds(i * tile, tile)
        r2 = r1_ref[at, :] + vec_ref[7:8, :]
        for t in range(groups):
            r2 = r2 + nt(co_ref[t, at, :], g2_ref[t, :, hw : 2 * hw])
        r2_ref[at, :] = r2
        z, _ = norm_parts(r2)
        a3_ref[at, :] = (z * vec_ref[4:5, :] + vec_ref[5:6, :]).astype(bf16)
        return 0

    lax.fori_loop(0, own // tile, final, 0)


def ff_kernel(
    a3_ref, r2_ref, dy_ref, g3_ref, ub_ref, vec_ref,
    out_ref, dr2_ref, gr3_ref, ubg_ref, vecg_ref,
    a3t_ref, dmt_ref, acc_ref, acd_ref, gs_ref, dus_ref,
):
    t = pl.program_id(0)
    own, width = a3_ref.shape
    units = ub_ref.shape[2]
    tile = 256

    @pl.when(t == 0)
    def _():
        a3t_ref[...] = a3_ref[...].T
        dmt_ref[...] = dy_ref[...].T
        acc_ref[...] = jnp.zeros_like(acc_ref)
        acd_ref[...] = jnp.zeros_like(acd_ref)

    ubg_ref[...] = jnp.zeros_like(ubg_ref)
    up = g3_ref[0, :, :units]
    down = g3_ref[0, :, units:]

    def rows(i, _):
        at = pl.ds(i * tile, tile)
        u = nn(a3_ref[at, :], up) + ub_ref[0]
        phi = 0.5 + 0.5 * lax.erf(u * (1.0 / math.sqrt(2.0)))
        g = (u * phi).astype(bf16)
        gs_ref[at, :] = g
        slope = phi + u * (jnp.exp(-0.5 * u * u) * (1.0 / math.sqrt(2.0 * math.pi)))
        du = (nn(dy_ref[at, :], down) * slope).astype(bf16)
        dus_ref[at, :] = du
        ubg_ref[0] += row_sum(du.astype(f32))
        acc_ref[at, :] += nt(g, down)
        acd_ref[at, :] += nt(du, up)
        return 0

    lax.fori_loop(0, own // tile, rows, 0)

    def grads(i, _):
        at = pl.ds(i * tile, tile)
        gr3_ref[0, at, :units] = nn(a3t_ref[at, :], dus_ref[...]).astype(bf16)
        gr3_ref[0, at, units:] = nn(dmt_ref[at, :], gs_ref[...]).astype(bf16)
        return 0

    lax.fori_loop(0, width // tile, grads, 0)

    @pl.when(t == pl.num_programs(0) - 1)
    def _():
        vecg_ref[...] = jnp.zeros_like(vecg_ref)

        def finish(i, _):
            at = pl.ds(i * tile, tile)
            r2 = r2_ref[at, :]
            dy = dy_ref[at, :].astype(f32)
            out_ref[at, :] = (r2 + (acc_ref[at, :] + vec_ref[8:9, :])).astype(bf16)
            z, rate = norm_parts(r2)
            da = acd_ref[at, :]
            dr2_ref[at, :] = dy + norm_back(z, rate, vec_ref[4:5, :], da)
            vecg_ref[0:1, :] += row_sum(da * z)
            vecg_ref[1:2, :] += row_sum(da)
            vecg_ref[2:3, :] += row_sum(dy)
            return 0

        lax.fori_loop(0, own // tile, finish, 0)


def bwd2_kernel(
    span_ref, g2_ref, ep_ref, dr2_ref, cq_ref, ckv_ref, co_ref, lse_ref, a2_ref, r1_ref, o_ref,
    vec_ref, segq_ref, count_ref,
    dr1_ref, do_ref, gr2_ref, de_ref, vecg_ref, hbg_ref,
    dco_ref, dcq_ref, dkv_ref, low_ref, rowt_ref, ept_ref, acc_ref, wide_ref, qs_ref, dos_ref, delta_ref,
):
    groups, width = g2_ref.shape[0], g2_ref.shape[1]
    own = dr2_ref.shape[0]
    hw = o_ref.shape[2]
    slots = ep_ref.shape[0]
    per_doc = slots // DOCS
    heads = hw // HEAD_DIM
    tile = 256

    vecg_ref[...] = jnp.zeros_like(vecg_ref)
    hbg_ref[...] = jnp.zeros_like(hbg_ref)

    def tile_at(i):
        return pl.ds(pl.multiple_of(i * tile, tile), tile)

    def first(i, _):
        at = tile_at(i)
        dc = dr2_ref[at, :].astype(bf16)
        vecg_ref[2:3, :] += row_sum(dc.astype(f32))
        rowt_ref[:, at] = dc.T
        for t in range(groups):
            dco_ref[t, at, :] = nn(dc, g2_ref[t, :, hw : 2 * hw]).astype(bf16)
        return 0

    lax.fori_loop(0, own // tile, first, 0)

    def output_grads(t, _):
        gr2_ref[t, :, hw : 2 * hw] = nn(rowt_ref[...], co_ref[t]).astype(bf16)
        return 0

    lax.fori_loop(0, groups, output_grads, 0)

    dkv_ref[...] = jnp.zeros_like(dkv_ref)
    place = lax.broadcasted_iota(jnp.int32, (per_doc, QT), 0).astype(f32)

    def attend(n, _):
        segs = segq_ref[n]
        mine = pl.ds(n * QT, QT)
        acc_ref[...] = jnp.zeros_like(acc_ref)
        for t in range(groups):
            qs_ref[t] = spread_heads(cq_ref[t, mine, :] * bf16(SCALE))
            dos = dco_ref[t, mine, :]
            dos_ref[t] = spread_heads(dos)
            inner = (dos.astype(f32) * co_ref[t, mine, :].astype(f32)).T
            delta_ref[t] = head_row(inner)

        def document(d, _):
            keep = (segs == d.astype(f32)) & (place < count_ref[d])
            add = for_heads(jnp.where(keep, 0.0, MASKED), heads)
            at = pl.ds(d * per_doc, per_doc)
            for t in range(groups):
                kv = ckv_ref[t, at, :]
                scores = nt(kv[:, :hw], qs_ref[t]) + add
                probs = jnp.exp(scores - lse_ref[t, n])
                grad = nt(kv[:, hw:], dos_ref[t])
                ds = (probs * (grad - delta_ref[t])).astype(bf16)
                dkv_ref[t, at, :hw] += nn(ds, qs_ref[t])
                dkv_ref[t, at, hw:] += nn(probs.astype(bf16), dos_ref[t])
                acc_ref[t] += own_blocks(tn(kv[:, :hw], ds))
            return 0

        lax.fori_loop(span_ref[2 * n], span_ref[2 * n + 1] + 1, document, 0)
        for t in range(groups):
            dcq_ref[t, mine, :] = (acc_ref[t].T * SCALE).astype(bf16)
        return 0

    lax.fori_loop(0, own // QT, attend, 0)

    def queries_back(i, _):
        at = tile_at(i)
        da = jnp.zeros((tile, width), f32)
        for t in range(groups):
            da = da + nt(dcq_ref[t, at, :], g2_ref[t, :, 4 * hw : 5 * hw])
        z, rate = norm_parts(r1_ref[at, :])
        dr1 = dr2_ref[at, :] + norm_back(z, rate, vec_ref[2:3, :], da)
        dr1_ref[at, :] = dr1
        vecg_ref[0:1, :] += row_sum(da * z)
        vecg_ref[1:2, :] += row_sum(da)
        rowt_ref[:, at] = a2_ref[at, :].T
        return 0

    lax.fori_loop(0, own // tile, queries_back, 0)

    def query_grads(t, _):
        gr2_ref[t, :, 4 * hw : 5 * hw] = nn(rowt_ref[...], dcq_ref[t]).astype(bf16)
        hbg_ref[t, 0:1, :] = row_sum(dcq_ref[t].astype(f32))
        return 0

    lax.fori_loop(0, groups, query_grads, 0)

    def self_back(i, _):
        at = tile_at(i)
        ds = dr1_ref[at, :].astype(bf16)
        vecg_ref[3:4, :] += row_sum(ds.astype(f32))
        rowt_ref[:, at] = ds.T
        for t in range(groups):
            do_ref[t, at, :] = nn(ds, g2_ref[t, :, 0:hw]).astype(bf16)
        return 0

    lax.fori_loop(0, own // tile, self_back, 0)

    def self_grads(t, _):
        gr2_ref[t, :, 0:hw] = nn(rowt_ref[...], o_ref[t]).astype(bf16)
        return 0

    lax.fori_loop(0, groups, self_grads, 0)

    def turn(i, _):
        at = tile_at(i)
        ept_ref[:, at] = ep_ref[at, :].T
        for t in range(groups):
            low = dkv_ref[t, at, :].astype(bf16)
            low_ref[t, at, :] = low
            hbg_ref[t, 1:2, :] += row_sum(low[:, hw:].astype(f32))
        return 0

    lax.fori_loop(0, slots // tile, turn, 0)

    half = width // 2
    def frame_grads(i, _):
        at = pl.ds(pl.multiple_of(4 * i * per_doc, 4 * per_doc), 4 * per_doc)
        total = jnp.zeros((4 * per_doc, width), f32)
        for t in range(groups):
            total = total + nt(low_ref[t, at, :], g2_ref[t, :, 2 * hw : 4 * hw])
        for d in range(4):
            block = total[d * per_doc : (d + 1) * per_doc]
            for j in range(width // 128):
                wide_ref[j, pl.ds(4 * i + d, per_doc, stride=DOCS), :] = block[
                    :, j * 128 : (j + 1) * 128
                ]
        return 0

    lax.fori_loop(0, DOCS // 4, frame_grads, 0)
    per_half = half // 128
    for j in range(width // 128):
        lane = slice((j % per_half) * 128, (j % per_half + 1) * 128)
        held = de_ref.shape[2]
        for h in range(de_ref.shape[1]):
            at = slice(h * held, (h + 1) * held)
            de_ref[j // per_half, h, :, lane] = wide_ref[j, at, :].astype(bf16)

    def key_grads(t, _):
        gr2_ref[t, :, 2 * hw : 4 * hw] = nn(ept_ref[...], low_ref[t]).astype(bf16)
        return 0

    lax.fori_loop(0, groups, key_grads, 0)


def bwd1_kernel(
    xa_ref, a1_ref, g1_ref, qkv_ref, o_ref, do_ref, lse_ref, segk_ref, segq_ref,
    vecg2_ref, vecg3_ref, hbg2_ref, ubg_ref, permh_ref, permu_ref,
    da_ref, dh_ref, gr1_ref, sg_ref,
    a1t_ref, acc_ref, dk_ref, dv_ref, dq_ref, low_ref, vecg_ref, hbg_ref,
):
    t = pl.program_id(0)
    rows, width = xa_ref.shape
    own = segq_ref.shape[0] * QT
    halo = rows - own
    window = halo + QT
    hw = o_ref.shape[2]
    tile = 256

    @pl.when(t == 0)
    def _():
        for i in range(rows // tile):
            at = slice(i * tile, (i + 1) * tile)
            a1t_ref[:, at] = a1_ref[at, :].T
        acc_ref[...] = jnp.zeros_like(acc_ref)
        low_ref[0:halo, 0:hw] = jnp.zeros((halo, hw), bf16)

    dk_ref[...] = jnp.zeros_like(dk_ref)
    dv_ref[...] = jnp.zeros_like(dv_ref)

    def attend(n, _):
        add = window_mask(segk_ref, segq_ref, n, halo, window)
        at = pl.ds(n * QT, window)
        mine = pl.ds(n * QT, QT)
        block = qkv_ref[0, at, :]
        dos = do_ref[0, mine, :]
        heads = hw // HEAD_DIM
        delta = head_row((dos.astype(f32) * o_ref[0, mine, :].astype(f32)).T)
        dos = spread_heads(dos)
        qs = spread_heads(block[halo:, :hw] * bf16(SCALE))
        scores = nt(block[:, hw : 2 * hw], qs) + for_heads(add, heads)
        probs = jnp.exp(scores - lse_ref[0, n])
        grad = nt(block[:, 2 * hw :], dos)
        ds = (probs * (grad - delta)).astype(bf16)
        dv_ref[at, :] += nn(probs.astype(bf16), dos)
        dk_ref[at, :] += nn(ds, qs)
        dq = own_blocks(tn(block[:, hw : 2 * hw], ds))
        dq_ref[mine, :] = (dq.T * SCALE).astype(bf16)
        return 0

    lax.fori_loop(0, own // QT, attend, 0)
    low_ref[halo:, 0:hw] = dq_ref[...]
    low_ref[:, hw : 2 * hw] = dk_ref[...].astype(bf16)
    low_ref[:, 2 * hw : 3 * hw] = dv_ref[...].astype(bf16)
    hbg_ref[t, 0:1, :] = row_sum(dq_ref[...].astype(f32))
    hbg_ref[t, 1:2, :] = row_sum(dv_ref[...].astype(bf16).astype(f32))
    w = g1_ref[0, :, : 3 * hw]

    def back(i, _):
        at = pl.ds(i * tile, tile)
        acc_ref[at, :] += nt(low_ref[at, :], w)
        return 0

    lax.fori_loop(0, rows // tile, back, 0)

    def grads(i, _):
        at = pl.ds(i * tile, tile)
        gr1_ref[0, at, 0 : 3 * hw] = nn(a1t_ref[at, :], low_ref[...]).astype(bf16)
        return 0

    lax.fori_loop(0, width // tile, grads, 0)

    @pl.when(t == pl.num_programs(0) - 1)
    def _():
        vecg_ref[...] = jnp.zeros_like(vecg_ref)
        dh_ref[...] = acc_ref[0:halo, :].astype(bf16)
        da_ref[...] = acc_ref[halo:, :]

        def sums(i, _):
            at = pl.ds(i * tile, tile)
            z, _ = norm_parts(xa_ref[at, :].astype(f32))
            vecg_ref[0:1, :] += row_sum(acc_ref[at, :] * z)
            vecg_ref[1:2, :] += row_sum(acc_ref[at, :])
            return 0

        lax.fori_loop(0, rows // tile, sums, 0)
        heads = hw // HEAD_DIM
        vectors = jnp.concatenate(
            [
                vecg_ref[0:2, :], vecg2_ref[0:2, :], vecg3_ref[0:2, :],
                vecg2_ref[3:4, :], vecg2_ref[2:3, :], vecg3_ref[2:3, :], jnp.zeros((7, width), f32),
            ],
            axis=0,
        ).T
        for g in range(hbg2_ref.shape[0]):
            four = (hbg_ref[g, 0:1], hbg_ref[g, 1:2], hbg2_ref[g, 0:1], hbg2_ref[g, 1:2])
            by_head = [lane_parts(row, heads) for row in four]
            by_head = jnp.concatenate(by_head + [jnp.zeros((16 - 4 * heads, HEAD_DIM), f32)], axis=0)
            by_unit = lane_parts(ubg_ref[g], heads)
            edge = jnp.zeros((4 * heads, by_unit.shape[1]), f32)
            rest = jnp.zeros((16 - 5 * heads, by_unit.shape[1]), f32)
            by_unit = jnp.concatenate([edge, by_unit, rest], axis=0)
            biases = nt(permh_ref[...], by_head.astype(bf16)) + nt(permu_ref[...], by_unit.astype(bf16))
            sg_ref[g] = jnp.concatenate(
                [vectors, biases, jnp.zeros((width, 32), f32)], axis=1
            ).astype(bf16)


def whole(shape):
    return pl.BlockSpec(shape, lambda *_: (0,) * len(shape))


def step_of(shape):
    return pl.BlockSpec((1,) + shape[1:], lambda t: (t,) + (0,) * (len(shape) - 1))


def params(dims=0):
    return pltpu.CompilerParams(
        vmem_limit_bytes=VMEM_LIMIT,
        dimension_semantics=("arbitrary",) * dims if dims else None,
    )


def cost(flops, exps, size):
    return pl.CostEstimate(flops=int(flops), transcendentals=int(exps), bytes_accessed=int(size))


def sds(shape, dtype):
    return jax.ShapeDtypeStruct(shape, dtype)

MESH_ID = pl.DeviceIdType.MESH


def place_of(chips, ctx, groups):
    f, x, z = lax.axis_index("fsdp"), lax.axis_index("ctx"), lax.axis_index("tp")
    return lax.div(f, 2), lax.rem(f, 2), x, z


def greet(chips, ctx, groups, y, c, x, z):
    barrier = pltpu.get_barrier_semaphore()
    peers = [(2 * lax.rem(y + j, chips) + c, x, z) for j in range(1, chips)]
    for dc in range(2):
        for dx in range(ctx):
            for dz in range(groups):
                if dc + dx + dz > 0:
                    other = (2 * y + lax.rem(c + dc, 2), lax.rem(x + dx, ctx), lax.rem(z + dz, groups))
                    peers.append(other)
    for peer in peers:
        pl.semaphore_signal(barrier, inc=1, device_id=peer, device_id_type=MESH_ID)
    pl.semaphore_wait(barrier, len(peers))


def gather_kernel(paths, chips, ctx, groups, *refs):
    count = len(paths)
    packs, (rows_in, frames_in, seg_in) = refs[:count], refs[count : count + 3]
    refs = refs[count + 3 :]
    fulls, (rows_out, frames_out, seg_out) = refs[:count], refs[count : count + 3]
    blank, local, zs, zr, fs, fr, ss, sr, cs, cr, xs, xr, xl, es, er, el = refs[count + 3 :]
    y, c, x, z = place_of(chips, ctx, groups)
    greet(chips, ctx, groups, y, c, x, z)
    sent = []

    def sizes(a):
        return (ctx, chips) if paths[a] == "xy" else (chips, ctx)

    def spot(a, k, i, j, core):
        t = lax.rem(z + groups - k, groups)
        dx, dy = (i, j) if paths[a] == "xy" else (j, i)
        return fulls[a].at[t, lax.rem(y + chips - dy, chips), core, lax.rem(x + ctx - dx, ctx)]

    def peer(a, first, hop):
        along_x = (paths[a] == "xy") == first
        if along_x:
            return (2 * y + c, lax.rem(x + hop, ctx), z)
        return (2 * lax.rem(y + hop, chips) + c, x, z)

    def flat(a, i, j):
        return i * sizes(a)[1] + j

    def send(src, dst, ssem, rsem, device):
        copy = pltpu.make_async_remote_copy(
            src_ref=src, dst_ref=dst, send_sem=ssem, recv_sem=rsem,
            device_id=device, device_id_type=MESH_ID,
        )
        copy.start()
        sent.append(copy)

    def arrived(dst, ssem, rsem):
        pltpu.make_async_remote_copy(
            src_ref=dst, dst_ref=dst, send_sem=ssem, recv_sem=rsem,
            device_id=(2 * y + 1 - c, x, z), device_id_type=MESH_ID,
        ).wait_recv()

    def to_core(a, k, i, j, src):
        send(src, spot(a, k, i, j, c), cs.at[a, k, flat(a, i, j)], cr.at[a, k, flat(a, i, j)], (2 * y + 1 - c, x, z))

    def second(a, k, i, src):
        for j in range(1, sizes(a)[1]):
            send(src, spot(a, k, i, 0, c), ss.at[a, k, flat(a, i, j)], sr.at[a, k, flat(a, i, j)], peer(a, False, j))

    half, low = lax.div(z, 2), lax.rem(z, 2)
    me = (2 * y + c, x, z)
    core_peer = (2 * y + 1 - c, x, z)

    def remote(src, dst, ssem, rsem, device):
        return pltpu.make_async_remote_copy(
            src_ref=src, dst_ref=dst, send_sem=ssem, recv_sem=rsem,
            device_id=device, device_id_type=MESH_ID,
        )

    blank[...] = jnp.zeros_like(blank)
    next_piece = 2 * x + c + 1
    next_exists = next_piece < 2 * ctx
    next_device = (2 * y + lax.rem(next_piece, 2), lax.rem(lax.div(next_piece, 2), ctx), z)

    def stays(b):
        return (half == c) & (2 * c + b == z)

    def to_owner(b):
        return remote(
            rows_in.at[b], rows_out.at[2 + low], xs.at[b], xr.at[2 + low], (2 * y + half, x, 2 * c + b)
        )

    def to_self(b):
        return pltpu.make_async_copy(rows_in.at[b], rows_out.at[2 + low], xl.at[2])

    def to_next(s):
        return remote(rows_out.at[2 + s], rows_out.at[s], xs.at[2 + s], xr.at[s], next_device)

    first = (x == 0) & (c == 0)

    @pl.when(first)
    def _():
        for s in range(2):
            pltpu.make_async_copy(blank, rows_out.at[s], xl.at[s]).start()

    holds = half == c

    @pl.when(holds)
    def _():
        pltpu.make_async_copy(frames_in.at[low], frames_out.at[x], el.at[0]).start()
        pltpu.make_async_copy(seg_in, seg_out, el.at[1]).start()
        remote(
            frames_in.at[low], frames_out.at[x], es.at[0], er.at[0], (2 * y + c, 1 - x, z)
        ).start()
        remote(frames_in.at[low], frames_out.at[x], es.at[1], er.at[1], core_peer).start()
        remote(seg_in, seg_out, es.at[2], er.at[2], core_peer).start()

    mine = []
    for a in range(count):
        copy = pltpu.make_async_copy(packs[a], spot(a, 0, 0, 0, c), local.at[a])
        copy.start()
        mine.append(copy)
    for k in range(1, groups):
        for a in range(count):
            send(
                packs[a], spot(a, 0, 0, 0, c), zs.at[a, k], zr.at[a, k],
                (2 * y + c, x, lax.rem(z + k, groups)),
            )
    for b in range(2):
        pl.when(jnp.logical_not(stays(b)))(to_owner(b).start)
        pl.when(stays(b))(to_self(b).start)
    for step in range(groups + 2):
        for a in range(count):
            n1, n2 = sizes(a)
            k = step
            if k < groups:
                src = packs[a] if k == 0 else spot(a, k, 0, 0, c)
                if k > 0:
                    arrived(src, zs.at[a, k], zr.at[a, k])
                for i in range(1, n1):
                    send(src, spot(a, k, 0, 0, c), fs.at[a, k, i], fr.at[a, k, i], peer(a, True, i))
                second(a, k, 0, src)
                to_core(a, k, 0, 0, src)
            k = step - 1
            if 0 <= k < groups:
                for i in range(1, n1):
                    src = spot(a, k, i, 0, c)
                    arrived(src, fs.at[a, k, i], fr.at[a, k, i])
                    second(a, k, i, src)
                    to_core(a, k, i, 0, src)
            k = step - 2
            if 0 <= k < groups:
                for i in range(n1):
                    for j in range(1, n2):
                        src = spot(a, k, i, j, c)
                        arrived(src, ss.at[a, k, flat(a, i, j)], sr.at[a, k, flat(a, i, j)])
                        to_core(a, k, i, j, src)
    for s in range(2):
        pl.when(jnp.logical_not(stays(s)))(
            remote(rows_in.at[0], rows_out.at[2 + s], xs.at[0], xr.at[2 + s], core_peer).wait_recv
        )
        pl.when(stays(s))(to_self(s).wait)
    for s in range(2):
        pl.when(next_exists)(to_next(s).start)

    far = 1 - x

    @pl.when(holds)
    def _():
        remote(frames_in.at[low], frames_out.at[far], es.at[0], er.at[0], (2 * y + c, far, z)).wait_recv()
        remote(frames_out.at[far], frames_out.at[far], es.at[3], er.at[3], core_peer).start()

    for a in range(count):
        n1, n2 = sizes(a)
        for k in range(groups):
            for i in range(n1):
                for j in range(n2):
                    arrived(spot(a, k, i, j, 1 - c), cs.at[a, k, flat(a, i, j)], cr.at[a, k, flat(a, i, j)])
    @pl.when(holds)
    def _():
        relay = remote(frames_out.at[far], frames_out.at[far], es.at[3], er.at[3], core_peer)
        remote(frames_in.at[low], frames_out.at[x], es.at[0], er.at[0], (2 * y + c, far, z)).wait_send()
        remote(frames_in.at[low], frames_out.at[x], es.at[1], er.at[1], core_peer).wait_send()
        remote(seg_in, seg_out, es.at[2], er.at[2], core_peer).wait_send()
        relay.wait_send()
        pltpu.make_async_copy(frames_in.at[low], frames_out.at[x], el.at[0]).wait()
        pltpu.make_async_copy(seg_in, seg_out, el.at[1]).wait()

    @pl.when(jnp.logical_not(holds))
    def _():
        remote(frames_in.at[low], frames_out.at[x], es.at[1], er.at[1], core_peer).wait_recv()
        remote(seg_in, seg_out, es.at[2], er.at[2], core_peer).wait_recv()
        remote(frames_out.at[far], frames_out.at[far], es.at[3], er.at[3], core_peer).wait_recv()

    for b in range(2):
        pl.when(jnp.logical_not(stays(b)))(to_owner(b).wait_send)

    @pl.when(first)
    def _():
        for s in range(2):
            pltpu.make_async_copy(blank, rows_out.at[s], xl.at[s]).wait()

    for s in range(2):
        pl.when(next_exists)(to_next(s).wait_send)
        pl.when(jnp.logical_not(first))(to_next(s).wait_recv)

    for copy in sent:
        copy.wait_send()
    for copy in mine:
        copy.wait()


def gather_packs(packs, rows, frames, segs, paths, chips, ctx, groups, collective_id):
    count = len(packs)
    side = max(chips, ctx)
    dma = pltpu.SemaphoreType.DMA
    moved = sum(p.size for p in packs) * 2 * (2 * chips * ctx * groups)
    return pl.pallas_call(
        functools.partial(gather_kernel, paths, chips, ctx, groups),
        in_specs=[pl.BlockSpec(memory_space=pltpu.VMEM)] * count
        + [pl.BlockSpec(memory_space=pl.ANY)] * 3,
        out_specs=[pl.BlockSpec(memory_space=pl.ANY)] * (count + 3),
        out_shape=[sds((groups, chips, 2, ctx) + p.shape, p.dtype) for p in packs]
        + [
            sds((4,) + rows.shape[1:], bf16),
            sds((ctx,) + frames.shape[1:], bf16),
            sds(segs.shape, f32),
        ],
        scratch_shapes=[
            pltpu.VMEM(rows.shape[1:], bf16),
            dma((count,)),
            dma((count, groups)),
            dma((count, groups)),
            dma((count, groups, side)),
            dma((count, groups, side)),
            dma((count, groups, chips * ctx)),
            dma((count, groups, chips * ctx)),
            dma((count, groups, chips * ctx)),
            dma((count, groups, chips * ctx)),
            dma((4,)),
            dma((4,)),
            dma((4,)),
            dma((4,)),
            dma((4,)),
            dma((2,)),
        ],
        compiler_params=pltpu.CompilerParams(
            collective_id=collective_id, has_side_effects=True, vmem_limit_bytes=8 * 1024 * 1024
        ),
        cost_estimate=cost(0, 0, 10 * moved),
        name="gather_packs",
    )(*packs, rows, frames, segs)


def reduce_kernel(paths, chips, ctx, groups, *refs):
    count = len(paths)
    grads, (de, dh, da, dr1, xo, gain) = refs[:count], refs[count : count + 6]
    refs = refs[count + 6 :]
    outs, (gx, ge) = refs[:count], refs[count : count + 2]
    at = count + 2
    bufs = [refs[at + 7 * a : at + 7 * a + 7] for a in range(count)]
    at = at + 7 * count
    hbuf, gbuf, rce, se, rxe, qe = refs[at : at + 6]
    cs, cr, s1, r1, s2, r2, zs, zr, hs, hr, es, er, gs, gr, gl = refs[at + 6 :]
    y, c, x, z = place_of(chips, ctx, groups)
    half, low = lax.div(z, 2), lax.rem(z, 2)
    core_peer = (2 * y + 1 - c, x, z)
    greet(chips, ctx, groups, y, c, x, z)
    sent = []

    def sizes(a):
        return (ctx, chips) if paths[a] == "xy" else (chips, ctx)

    def mine(a):
        return (x, y) if paths[a] == "xy" else (y, x)

    def peer(a, first, index):
        if (paths[a] == "xy") == first:
            return (2 * y + c, index, z)
        return (2 * index + c, x, z)

    def send(src, dst, ssem, rsem, device):
        copy = pltpu.make_async_remote_copy(
            src_ref=src, dst_ref=dst, send_sem=ssem, recv_sem=rsem,
            device_id=device, device_id_type=MESH_ID,
        )
        copy.start()
        sent.append(copy)

    def arrived(dst, ssem, rsem):
        pltpu.make_async_remote_copy(
            src_ref=dst, dst_ref=dst, send_sem=ssem, recv_sem=rsem,
            device_id=(2 * y + 1 - c, x, z), device_id_type=MESH_ID,
        ).wait_recv()

    def group(g):
        return lax.rem(z + 1 + g, groups)

    def remote(src, dst, ssem, rsem, device):
        return pltpu.make_async_remote_copy(
            src_ref=src, dst_ref=dst, send_sem=ssem, recv_sem=rsem,
            device_id=device, device_id_type=MESH_ID,
        )

    piece = 2 * x + c
    prev = lax.rem(piece + 2 * ctx - 1, 2 * ctx)
    prev_core, prev_x = lax.rem(prev, 2), lax.div(prev, 2)
    to_prev = remote(dh, hbuf, hs, hr, (2 * y + prev_core, prev_x, z))
    pl.when(piece > 0)(to_prev.start)

    send(de.at[1 - c], rce, es.at[0], er.at[0], core_peer)

    for g in range(groups):
        for a in range(count):
            send(
                grads[a].at[group(g), :, 1 - c], bufs[a][0].at[group(g)], cs.at[a, g], cr.at[a, g],
                (2 * y + 1 - c, x, z),
            )

    def onward(a, g, i):
        n1, _ = sizes(a)
        t, index = group(g), lax.rem(mine(a)[0] + i, n1)
        p1, b1 = bufs[a][1], bufs[a][2]
        return remote(
            p1.at[t, index], b1.at[t, i - 1], s1.at[a, g, i], r1.at[a, g, i], peer(a, True, index)
        )

    def stage1(g, _):
        t = group(g)
        for a in range(count):
            rc, p1 = bufs[a][0], bufs[a][1]
            arrived(rc.at[t], cs.at[a, g], cr.at[a, g])
            for yy in range(chips):
                for xx in range(ctx):
                    i, j = (xx, yy) if paths[a] == "xy" else (yy, xx)
                    total = grads[a][t, yy, c, xx].astype(f32) + rc[t, yy, xx].astype(f32)
                    p1[t, i, j] = total.astype(bf16)
            for i in range(1, sizes(a)[0]):
                onward(a, g, i).start()
        return 0

    def stage2(g):
        t = group(g)
        for a in range(count):
            p1, b1, p2, b2 = bufs[a][1:5]
            n1, n2 = sizes(a)
            for i in range(1, n1):
                arrived(b1.at[t, i - 1], s1.at[a, g, i], r1.at[a, g, i])
            for j in range(n2):
                total = p1[t, mine(a)[0], j].astype(f32)
                for i in range(1, n1):
                    total = total + b1[t, i - 1, j].astype(f32)
                p2[t, j] = total.astype(bf16)
            for j in range(1, n2):
                index = lax.rem(mine(a)[1] + j, n2)
                send(
                    p2.at[t, index], b2.at[t, j - 1], s2.at[a, g, j], r2.at[a, g, j],
                    peer(a, False, index),
                )

    def stage3(g):
        t = group(g)
        for a in range(count):
            p2, b2, p3, b3 = bufs[a][3:7]
            _, n2 = sizes(a)
            for j in range(1, n2):
                arrived(b2.at[t, j - 1], s2.at[a, g, j], r2.at[a, g, j])
            total = p2[t, mine(a)[1]].astype(f32)
            for j in range(1, n2):
                total = total + b2[t, j - 1].astype(f32)
            if g == groups - 1:
                outs[a][...] = total
            else:
                p3[g] = total.astype(bf16)
                send(p3.at[g], b3.at[g], zs.at[a, g], zr.at[a, g], (2 * y + c, x, t))

    def home(src, dst, k, s):
        stays = (half == c) & (2 * c + s == z)
        away = remote(
            src.at[s], dst.at[low], gs.at[k, s], gr.at[k, low], (2 * y + half, x, 2 * c + s)
        )
        here = pltpu.make_async_copy(src.at[s], dst.at[low], gl.at[k])
        return stays, away, here

    def go_home(src, dst, k):
        for s in range(2):
            stays, away, here = home(src, dst, k, s)
            pl.when(jnp.logical_not(stays))(away.start)
            pl.when(stays)(here.start)

    def settle(src, dst, k):
        for s in range(2):
            stays, away, here = home(src, dst, k, s)
            pl.when(jnp.logical_not(stays))(away.wait_send)
            pl.when(stays)(here.wait)
        for b in range(2):
            came = jnp.logical_not((half == c) & (2 * c + b == z))
            pl.when(came)(remote(src.at[0], dst.at[b], gs.at[k, 0], gr.at[k, b], core_peer).wait_recv)

    def frames1():
        arrived(rce, es.at[0], er.at[0])
        for h in range(ctx):
            se[h] = (de[c, h].astype(f32) + rce[h].astype(f32)).astype(bf16)
        send(se.at[1 - x], rxe, es.at[1], er.at[1], (2 * y + c, 1 - x, z))

    def frames2():
        arrived(rxe, es.at[1], er.at[1])
        total = (se[x].astype(f32) + rxe[...].astype(f32)).astype(bf16)
        quarter = qe.shape[2]
        for s in range(2):
            qe[s] = total[:, s * quarter : (s + 1) * quarter]
        go_home(qe, ge, 1)

    def rows_back():
        last = piece == 2 * ctx - 1

        @pl.when(last)
        def _():
            hbuf[...] = jnp.zeros_like(hbuf)

        @pl.when(jnp.logical_not(last))
        def _():
            remote(dh, hbuf, hs, hr, core_peer).wait_recv()

        sub = gbuf.shape[1]
        for i in range(gbuf.shape[0]):
            at = slice(i * sub, (i + 1) * sub)
            zn, rate = norm_parts(xo[at, :].astype(f32))
            total = da[at, :] + hbuf[at, :].astype(f32)
            gbuf[i] = (dr1[at, :] + norm_back(zn, rate, gain[0:1, :], total)).astype(bf16)
        go_home(gbuf, gx, 0)

    lax.fori_loop(0, groups, stage1, 0)
    frames1()
    rows_back()
    for g in range(groups + 1):
        if g < groups:
            stage2(g)
        if g > 0:
            stage3(g - 1)
        if g == 1:
            frames2()
    for a in range(count):
        b3 = bufs[a][6]
        for g in range(groups - 1):
            arrived(b3.at[g], zs.at[a, g], zr.at[a, g])
            outs[a][...] += b3[g].astype(f32)
    settle(gbuf, gx, 0)
    settle(qe, ge, 1)
    pl.when(piece > 0)(to_prev.wait_send)
    for g in range(groups):
        for a in range(count):
            for i in range(1, sizes(a)[0]):
                onward(a, g, i).wait_send()
    for copy in sent:
        copy.wait_send()


def reduce_packs(grads, de, dh, da, dr1, xo, gain, paths, chips, ctx, groups, collective_id):
    count = len(grads)
    side = max(chips, ctx)
    own, width = dr1.shape
    held = de.shape[2]
    dma = pltpu.SemaphoreType.DMA
    scratch = []
    for a in range(count):
        block = grads[a].shape[4:]
        n1, n2 = (ctx, chips) if paths[a] == "xy" else (chips, ctx)
        for lead in (
            (groups, chips, ctx), (groups, n1, n2), (groups, n1 - 1, n2), (groups, n2),
            (groups, n2 - 1), (groups - 1,), (groups - 1,),
        ):
            scratch.append(pltpu.VMEM(lead + block, bf16))
    return pl.pallas_call(
        functools.partial(reduce_kernel, paths, chips, ctx, groups),
        in_specs=[pl.BlockSpec(memory_space=pltpu.VMEM)] * (count + 6),
        out_specs=[pl.BlockSpec(memory_space=pltpu.VMEM)] * (count + 2),
        out_shape=[sds(g.shape[4:], f32) for g in grads]
        + [
            sds((2, own // 2, width), bf16),
            sds((2, held, width // 4), bf16),
        ],
        scratch_shapes=scratch
        + [
            pltpu.VMEM((own, width), bf16),
            pltpu.VMEM((2, own // 2, width), bf16),
            pltpu.VMEM((ctx, held, width // 2), bf16),
            pltpu.VMEM((ctx, held, width // 2), bf16),
            pltpu.VMEM((held, width // 2), bf16),
            pltpu.VMEM((2, held, width // 4), bf16),
            dma((count, groups)),
            dma((count, groups)),
            dma((count, groups, side)),
            dma((count, groups, side)),
            dma((count, groups, side)),
            dma((count, groups, side)),
            dma((count, groups)),
            dma((count, groups)),
            dma(()),
            dma(()),
            dma((2,)),
            dma((2,)),
            dma((3, 2)),
            dma((3, 2)),
            dma((3,)),
        ],
        compiler_params=pltpu.CompilerParams(
            collective_id=collective_id, has_side_effects=True, vmem_limit_bytes=VMEM_LIMIT
        ),
        cost_estimate=cost(0, 0, 10 * sum(g.size for g in grads)),
        name="reduce_packs",
    )(*grads, de, dh, da, dr1, xo, gain)


def prep_kernel(
    vec_ref, qb_ref, vb_ref, cqb_ref, cvb_ref, ub_ref,
    sq_ref, sk_ref, sv_ref, so_ref, cq_ref, ck_ref, cv_ref, co_ref, up_ref, down_ref,
    p1_ref, p2_ref, p3_ref, permh_ref, permu_ref,
):
    part, hw = sq_ref.shape
    units = up_ref.shape[1]

    for table, size in ((permh_ref, qb_ref.shape[1]), (permu_ref, ub_ref.shape[1])):
        row = lax.broadcasted_iota(jnp.int32, table.shape, 0).astype(f32)
        column = lax.broadcasted_iota(jnp.int32, table.shape, 1).astype(f32)
        owner = jnp.floor((row + 0.5) * (1.0 / part))
        local = row - owner * part
        hit = (local < size) & (owner * size + local == column)
        table[...] = jnp.where(hit, 1.0, 0.0).astype(bf16)

    def padded(rows):
        rows = rows.astype(f32)
        return jnp.concatenate([rows, jnp.zeros((rows.shape[0], part - rows.shape[1]), f32)], axis=1)

    rows = [vec_ref[...], jnp.zeros((16 - vec_ref.shape[0], part), f32)]
    rows += [padded(r[...]) for r in (qb_ref, vb_ref, cqb_ref, cvb_ref, ub_ref)]
    rows.append(jnp.zeros((64 - sum(r.shape[0] for r in rows), part), f32))
    small = jnp.concatenate(rows, axis=0).T.astype(bf16)
    p1_ref[...] = jnp.concatenate([sq_ref[...], sk_ref[...], sv_ref[...], small], axis=1)
    p2_ref[...] = jnp.concatenate(
        [
            so_ref[...].T, co_ref[...].T, ck_ref[...], cv_ref[...], cq_ref[...],
            jnp.zeros((part, 64), bf16),
        ],
        axis=1,
    )
    p3_ref[:, :units] = up_ref[...]
    p3_ref[:, units:] = down_ref[...].T


def lane_parts(row, count):
    size = row.shape[1] // count
    return jnp.concatenate([row[:, i * size : (i + 1) * size] for i in range(count)], axis=0)


def row_parts(matrix, first, count):
    return jnp.concatenate([matrix[first + i : first + i + 1] for i in range(count)], axis=1)


def on_device(
    hidden_in, encoder_states, segment_ids, out_grad,
    norm1_gain, norm1_bias, norm2_gain, norm2_bias, norm3_gain, norm3_bias,
    self_query, self_key, self_value, self_output,
    cross_query, cross_key, cross_value, cross_output,
    fc_up, fc_down,
    self_query_bias, self_value_bias, cross_query_bias, cross_value_bias, up_bias,
    self_output_bias, cross_output_bias, down_bias,
):
    F, C, T = lax.axis_size("fsdp"), lax.axis_size("ctx"), lax.axis_size("tp")
    batches, sub, width = hidden_in.shape
    length = segment_ids.shape[1]
    frames_own = encoder_states.shape[1]
    assert T == 2 * batches and T == 4 and F % 2 == 0 and C == 2
    own = 2 * sub
    part = width // (F * C)
    hw = self_query.shape[1]
    units = fc_up.shape[1]
    heads = self_query_bias.shape[0]
    f, x, z = lax.axis_index("fsdp"), lax.axis_index("ctx"), lax.axis_index("tp")
    core = lax.rem(f, 2)
    odd = lax.rem(z, 2)
    tfc = ("tp", "fsdp", "ctx")

    def round_pairs(r):
        pairs = []
        for m in range(F // 2):
            for c in range(2):
                for zz in range(T):
                    b = (r + zz) % 2
                    pairs.append(((2 * m + c) * T + zz, (2 * m + zz // 2) * T + 2 * c + b))
        return pairs

    rounds = [round_pairs(0), round_pairs(1)]
    axes = ("fsdp", "tp")

    def pick(values, index):
        return lax.dynamic_index_in_dim(values, index, 0, keepdims=False)

    def spread(values):
        first = lax.ppermute(pick(values, odd), axes, rounds[0])
        second = lax.ppermute(pick(values, 1 - odd), axes, rounds[1])
        even = odd == 0
        return jnp.concatenate(
            [jnp.where(even, first, second), jnp.where(even, second, first)], axis=0
        )

    vecs = (
        norm1_gain, norm1_bias, norm2_gain, norm2_bias, norm3_gain, norm3_bias,
        self_output_bias, cross_output_bias, down_bias,
    )
    per, wide = self_query_bias.shape[1], up_bias.shape[1]
    vm = pl.BlockSpec(memory_space=pltpu.VMEM)
    pack1, pack2, pack3, permh, permu = pl.pallas_call(
        prep_kernel,
        in_specs=[vm] * 16,
        out_specs=[vm] * 5,
        out_shape=[
            sds((part, 3 * hw + 64), bf16),
            sds((part, 5 * hw + 64), bf16),
            sds((part, 2 * units), bf16),
            sds((width, F * C * per), bf16),
            sds((width, F * C * wide), bf16),
        ],
        compiler_params=params(),
        cost_estimate=cost(0, 0, 4 * part * (8 * hw + 2 * units)),
        name="prep",
    )(
        jnp.stack([v.astype(f32) for v in vecs]),
        self_query_bias, self_value_bias, cross_query_bias, cross_value_bias, up_bias,
        self_query, self_key, self_value, self_output,
        cross_query, cross_key, cross_value, cross_output, fc_up, fc_down,
    )

    def gather(block):
        full = lax.all_gather(block, tfc, axis=0, tiled=True)
        return full.reshape(T, width, block.shape[1])

    chips = F // 2
    g1, g2, xa, frames, seg_row = gather_packs(
        (pack1, pack2), hidden_in, encoder_states, segment_ids.astype(f32),
        ("yx", "xy"), chips, C, T, 0,
    )
    g1 = g1.reshape(T, width, pack1.shape[1])
    g2 = g2.reshape(T, width, pack2.shape[1])
    xa = xa.reshape(2 * own, width)
    xo = xa[own:]
    seg_row = pick(seg_row, odd)

    piece = x * 2 + core
    seg_own = lax.dynamic_slice_in_dim(seg_row, piece * own, own)
    seg_halo = lax.dynamic_slice_in_dim(seg_row, jnp.maximum(piece - 1, 0) * own, own)
    seg_halo = jnp.where(piece == 0, -1.0, seg_halo)
    segk = jnp.concatenate([seg_halo, seg_own]).reshape(2 * own, 1)
    segq = seg_own.reshape(own // QT, 1, QT)
    ends = seg_own.reshape(own // QT, QT)
    span = jnp.stack([ends[:, 0], ends[:, -1]], axis=1).reshape(-1).astype(jnp.int32)

    frames_all = 2 * frames_own
    per_doc = -(-frames_all // (DOCS * 32)) * 32
    slots = DOCS * per_doc
    counts = jnp.asarray([float(-(-(frames_all - d) // DOCS)) for d in range(DOCS)], f32)

    out_grad, pack3, g1 = lax.optimization_barrier((out_grad, pack3, g1))
    g3 = gather(pack3)
    dy = spread(out_grad)

    nq = own // QT
    a1, qkv, o, lse1, vec_all, hb_all, ub_all = pl.pallas_call(
        fwd1_kernel,
        grid=(T,),
        in_specs=[
            whole((2 * own, width)),
            step_of(g1.shape),
            whole(permh.shape),
            whole(permu.shape),
            whole((2 * own, 1)),
            whole((nq, 1, QT)),
        ],
        out_specs=[
            whole((2 * own, width)),
            step_of((T, 2 * own, 3 * hw)),
            step_of((T, own, hw)),
            step_of((T, nq, 1, heads * QT)),
            whole((16, width)),
            step_of((T, 8, hw)),
            step_of((T, 1, units)),
        ],
        out_shape=[
            sds((2 * own, width), bf16),
            sds((T, 2 * own, 3 * hw), bf16),
            sds((T, own, hw), bf16),
            sds((T, nq, 1, heads * QT), f32),
            sds((16, width), f32),
            sds((T, 8, hw), f32),
            sds((T, 1, units), f32),
        ],
        compiler_params=params(1),
        cost_estimate=cost(2 * 2 * own * width * 3 * hw * T + 4 * own * (own + QT) * hw * T, own * (own + QT) * heads * T, 2 * g1.size + 12 * own * width),
        name="fwd1",
    )(xa, g1, permh, permu, segk, segq)

    smem = pl.BlockSpec(memory_space=pltpu.SMEM)
    ckv, r1, a2, cq, co, lse2, r2, a3, ep = pl.pallas_call(
        fwd2_kernel,
        in_specs=[smem] + [vm] * 7 + [smem],
        out_specs=[vm] * 9,
        out_shape=[
            sds((T, slots, 2 * hw), bf16),
            sds((own, width), f32),
            sds((own, width), bf16),
            sds((T, own, hw), bf16),
            sds((T, own, hw), bf16),
            sds((T, nq, 1, heads * QT), f32),
            sds((own, width), f32),
            sds((own, width), bf16),
            sds((slots, width), bf16),
        ],
        scratch_shapes=[
            pltpu.VMEM((nq, T, hw, QT), f32),
            pltpu.VMEM((width // 128, slots, 128), f32),
            pltpu.VMEM((T, heads * QT, hw), bf16),
        ],
        compiler_params=params(),
        cost_estimate=cost(2 * (2 * slots + 3 * own) * width * hw * T + 4 * own * slots * hw, own * per_doc * heads * T, 2 * g2.size + 20 * own * width),
        name="fwd2",
    )(
        span, g2, frames, xo, o, vec_all, hb_all, segq, counts,
    )

    out_rows, dr2, gr3, ubg, vecg3 = pl.pallas_call(
        ff_kernel,
        grid=(T,),
        in_specs=[
            whole((own, width)),
            whole((own, width)),
            whole((own, width)),
            step_of(g3.shape),
            step_of((T, 1, units)),
            whole((16, width)),
        ],
        out_specs=[
            whole((own, width)),
            whole((own, width)),
            step_of(g3.shape),
            step_of((T, 1, units)),
            whole((8, width)),
        ],
        out_shape=[
            sds((own, width), bf16),
            sds((own, width), f32),
            sds(g3.shape, bf16),
            sds((T, 1, units), f32),
            sds((8, width), f32),
        ],
        scratch_shapes=[
            pltpu.VMEM((width, own), bf16),
            pltpu.VMEM((width, own), bf16),
            pltpu.VMEM((own, width), f32),
            pltpu.VMEM((own, width), f32),
            pltpu.VMEM((own, units), bf16),
            pltpu.VMEM((own, units), bf16),
        ],
        compiler_params=params(1),
        cost_estimate=cost(12 * own * width * units * T, 2 * own * units * T, 4 * g3.size + 12 * own * width),
        name="ff",
    )(a3, r2, dy, g3, ub_all, vec_all)

    def scatter(block):
        return lax.psum_scatter(
            block.reshape(T * width, block.shape[2]), tfc, scatter_dimension=0, tiled=True
        )

    sum3 = scatter(gr3)
    backs = [[(d, s) for s, d in pairs] for pairs in rounds]
    out_rows = out_rows.reshape(2, sub, width)
    back0 = lax.ppermute(pick(out_rows, odd), axes, backs[0])
    back1 = lax.ppermute(pick(out_rows, 1 - odd), axes, backs[1])

    dr1, do, gr2, de, vecg2, hbg2 = pl.pallas_call(
        bwd2_kernel,
        in_specs=[smem] + [vm] * 12 + [smem],
        out_specs=[vm] * 6,
        out_shape=[
            sds((own, width), f32),
            sds((T, own, hw), bf16),
            sds(g2.shape, bf16),
            sds((2, C, frames_own, width // 2), bf16),
            sds((8, width), f32),
            sds((T, 8, hw), f32),
        ],
        scratch_shapes=[
            pltpu.VMEM((T, own, hw), bf16),
            pltpu.VMEM((T, own, hw), bf16),
            pltpu.VMEM((T, slots, 2 * hw), f32),
            pltpu.VMEM((T, slots, 2 * hw), bf16),
            pltpu.VMEM((width, own), bf16),
            pltpu.VMEM((width, slots), bf16),
            pltpu.VMEM((T, hw, QT), f32),
            pltpu.VMEM((width // 128, slots, 128), f32),
            pltpu.VMEM((T, heads * QT, hw), bf16),
            pltpu.VMEM((T, heads * QT, hw), bf16),
            pltpu.VMEM((T, 1, heads * QT), f32),
        ],
        compiler_params=params(),
        cost_estimate=cost(2 * (4 * slots + 6 * own) * width * hw * T + 10 * own * slots * hw, own * per_doc * heads * T, 4 * g2.size + 30 * own * width),
        name="bwd2",
    )(span, g2, ep, dr2, cq, ckv, co, lse2, a2, r1, o, vec_all, segq, counts)

    do, back0, back1 = lax.optimization_barrier((do, back0, back1))
    even = odd == 0
    out_final = jnp.stack([jnp.where(even, back0, back1), jnp.where(even, back1, back0)])

    da, dh, gr1, sg = pl.pallas_call(
        bwd1_kernel,
        grid=(T,),
        in_specs=[
            whole((2 * own, width)),
            whole((2 * own, width)),
            step_of(g1.shape),
            step_of(qkv.shape),
            step_of(o.shape),
            step_of(do.shape),
            step_of(lse1.shape),
            whole((2 * own, 1)),
            whole((nq, 1, QT)),
            whole((8, width)),
            whole((8, width)),
            whole((T, 8, hw)),
            whole((T, 1, units)),
            whole(permh.shape),
            whole(permu.shape),
        ],
        out_specs=[
            whole((own, width)),
            whole((own, width)),
            step_of((T, width, 3 * hw)),
            whole((T, width, 64)),
        ],
        out_shape=[
            sds((own, width), f32),
            sds((own, width), bf16),
            sds((T, width, 3 * hw), bf16),
            sds((T, width, 64), bf16),
        ],
        scratch_shapes=[
            pltpu.VMEM((width, 2 * own), bf16),
            pltpu.VMEM((2 * own, width), f32),
            pltpu.VMEM((2 * own, hw), f32),
            pltpu.VMEM((2 * own, hw), f32),
            pltpu.VMEM((own, hw), bf16),
            pltpu.VMEM((2 * own, 3 * hw), bf16),
            pltpu.VMEM((8, width), f32),
            pltpu.VMEM((T, 8, hw), f32),
        ],
        compiler_params=params(1),
        cost_estimate=cost(2 * 4 * own * width * 3 * hw * T + 10 * own * (own + QT) * hw * T, own * (own + QT) * heads * T, 4 * g1.size + 30 * own * width),
        name="bwd1",
    )(
        xa, a1, g1, qkv, o, do, lse1, segk, segq, vecg2, vecg3, hbg2, ubg, permh, permu,
    )

    split = (T, chips, 2, C, part)
    sum1, sum2, sums, grad_hidden, grad_encoder = reduce_packs(
        tuple(g.reshape(split + g.shape[2:]) for g in (gr1, gr2, sg)),
        de, dh, da, dr1, xo, vec_all,
        ("xy", "yx", "xy"), chips, C, T, 1,
    )
    grad_hidden = grad_hidden.astype(f32)
    grad_encoder = grad_encoder.astype(f32)

    sum3 = sum3.astype(f32)
    third = part // T
    vout = lax.dynamic_slice_in_dim(sums[:, :16], z * third, third).T
    hout = sums[:per, 16 : 16 + 4 * heads].T.reshape(4, heads, per)
    uout = sums[:wide, 16 + 4 * heads : 16 + 5 * heads].T

    def cut(array, k):
        return array[:, k * hw : (k + 1) * hw]

    return (
        out_final,
        grad_hidden,
        grad_encoder,
        vout[0], vout[1], vout[2], vout[3], vout[4], vout[5],
        cut(sum1, 0), cut(sum1, 1), cut(sum1, 2), cut(sum2, 0).T,
        cut(sum2, 4), cut(sum2, 2), cut(sum2, 3), cut(sum2, 1).T,
        sum3[:, :units], sum3[:, units:].T,
        hout[0], hout[1], hout[2], hout[3], uout,
        vout[6], vout[7], vout[8],
    )


def solution(mesh):
    column = P(("fsdp", "ctx"), "tp")
    row = P("tp", ("fsdp", "ctx"))
    vector = P(("fsdp", "ctx"))
    vector_out = P(("fsdp", "ctx", "tp"))
    tokens = P("fsdp", ("ctx", "tp"), None)
    return jax.shard_map(
        on_device,
        mesh=mesh,
        in_specs=(tokens, P("fsdp", "ctx", None), P("fsdp", None), tokens)
        + (vector,) * 6
        + (column, column, column, row)
        + (column, column, column, row)
        + (column, row)
        + (row,) * 5
        + (vector,) * 3,
        out_specs=(tokens, tokens, P("fsdp", "ctx", "tp"))
        + (vector_out,) * 6
        + (column, column, column, row)
        + (column, column, column, row)
        + (column, row)
        + (row,) * 5
        + (vector_out,) * 3,
        check_vma=False,
    )
```

```python
import functools
import math

import jax
import jax.numpy as jnp
from jax import lax
from jax.experimental import pallas as pl
from jax.experimental.pallas import tpu as pltpu
from jax.sharding import PartitionSpec as P

HEAD_DIM = 64
DOCS = 16
EPSILON = 1e-05
MASKED = -1e30
SCALE = HEAD_DIM ** (-0.5)
QT = 128

f32 = jnp.float32
bf16 = jnp.bfloat16

VMEM_LIMIT = 62 * 1024 * 1024


def nn(a, b):
    return lax.dot_general(a, b, (((1,), (0,)), ((), ())), preferred_element_type=f32)


def nt(a, b):
    return lax.dot_general(a, b, (((1,), (1,)), ((), ())), preferred_element_type=f32)


def tn(a, b):
    return lax.dot_general(a, b, (((0,), (0,)), ((), ())), preferred_element_type=f32)


def norm_parts(values):
    centred = values - jnp.mean(values, axis=-1, keepdims=True)
    rate = lax.rsqrt(jnp.mean(centred * centred, axis=-1, keepdims=True) + EPSILON)
    return centred * rate, rate


def norm_back(z, rate, gain, grad):
    scaled = gain * grad
    return rate * (
        scaled
        - jnp.mean(scaled, axis=-1, keepdims=True)
        - z * jnp.mean(scaled * z, axis=-1, keepdims=True)
    )


def row_sum(values):
    return jnp.sum(values, axis=0, keepdims=True)


def spread_heads(block):
    heads = block.shape[1] // HEAD_DIM
    lanes = lax.broadcasted_iota(jnp.int32, (1, block.shape[1]), 1)
    parts = []
    for i in range(heads):
        mine = (lanes >= i * HEAD_DIM) & (lanes < (i + 1) * HEAD_DIM)
        parts.append(block * jnp.where(mine, 1.0, 0.0).astype(block.dtype))
    return jnp.concatenate(parts, axis=0)


def own_blocks(matrix):
    heads = matrix.shape[0] // HEAD_DIM
    return jnp.concatenate(
        [
            matrix[i * HEAD_DIM : (i + 1) * HEAD_DIM, i * QT : (i + 1) * QT]
            for i in range(heads)
        ],
        axis=0,
    )


def head_row(matrix):
    heads = matrix.shape[0] // HEAD_DIM
    return jnp.concatenate(
        [row_sum(matrix[i * HEAD_DIM : (i + 1) * HEAD_DIM]) for i in range(heads)], axis=1
    )


def for_heads(block, heads):
    return jnp.concatenate([block] * heads, axis=1)


def window_mask(segk_ref, segq_ref, n, halo, window, skip):
    keys = segk_ref[pl.ds(n * QT + skip, window), :]
    same = keys == segq_ref[n]
    ahead = lax.broadcasted_iota(jnp.int32, (window, QT), 0) - lax.broadcasted_iota(
        jnp.int32, (window, QT), 1
    )
    return jnp.where(same & (ahead <= halo - skip), 0.0, MASKED)


def fwd1_kernel(
    near_ref, xa_ref, g1_ref, permh_ref, permu_ref, segk_ref, segq_ref,
    a1_ref, qkv_ref, o_ref, lse_ref, vec_ref, hb_ref, ub_ref,
):
    rows = xa_ref.shape[0]
    own = segq_ref.shape[0] * QT
    halo = rows - own
    window = halo + QT
    hw = o_ref.shape[2]
    tile = 256
    heads = hw // HEAD_DIM
    small = g1_ref[0, :, 3 * hw :]
    head_rows = tn(small, permh_ref[...])
    unit_rows = tn(small, permu_ref[...])
    biases = [row_parts(head_rows, 16 + heads * w, heads) for w in range(4)]
    hb_ref[0] = jnp.concatenate(biases + [jnp.zeros((4, hw), f32)], axis=0)
    ub_ref[0] = row_parts(unit_rows, 16 + 4 * heads, heads)
    bias = jnp.concatenate([biases[0], jnp.zeros((1, hw), f32), biases[1]], axis=1)

    @pl.when(pl.program_id(0) == 0)
    def _():
        vec_ref[...] = small.astype(f32).T[0:16]

        def body(i, _):
            at = pl.ds(i * tile, tile)
            z, _ = norm_parts(xa_ref[at, :].astype(f32))
            a1_ref[at, :] = (z * vec_ref[0:1, :] + vec_ref[1:2, :]).astype(bf16)
            return 0

        lax.fori_loop(0, rows // tile, body, 0)

    w = g1_ref[0, :, : 3 * hw]

    def project(i, _):
        at = pl.ds(i * tile, tile)
        qkv_ref[0, at, :] = (nn(a1_ref[at, :], w) + bias).astype(bf16)
        return 0

    lax.fori_loop(0, rows // tile, project, 0)

    def attend_from(n, skip):
        add = window_mask(segk_ref, segq_ref, n, halo, window - skip, skip)
        block = qkv_ref[0, pl.ds(n * QT + skip, window - skip), :]
        spread = spread_heads(block[halo - skip :, :hw] * bf16(SCALE))
        scores = nt(block[:, hw : 2 * hw], spread) + for_heads(add, heads)
        top = jnp.max(scores, axis=0, keepdims=True)
        weights = jnp.exp(scores - top)
        total = jnp.sum(weights, axis=0, keepdims=True)
        mixed = own_blocks(tn(block[:, 2 * hw :], weights.astype(bf16)) / total)
        lse_ref[0, n] = top + jnp.log(total)
        o_ref[0, pl.ds(n * QT, QT), :] = mixed.T.astype(bf16)

    def attend(n, _):
        near = near_ref[n] > 0
        pl.when(near)(functools.partial(attend_from, n, halo // 2))
        pl.when(jnp.logical_not(near))(functools.partial(attend_from, n, 0))
        return 0

    lax.fori_loop(0, own // QT, attend, 0)


def fwd2_kernel(
    span_ref, g2_ref, e_ref, xo_ref, o_ref, vec_ref, hb_ref, segq_ref, count_ref,
    ckv_ref, r1_ref, a2_ref, cq_ref, co_ref, lse_ref, r2_ref, a3_ref, ep_ref, acc_ref, wide_ref, spread_ref,
):
    groups = g2_ref.shape[0]
    half = e_ref.shape[1]
    own = xo_ref.shape[0]
    hw = o_ref.shape[2]
    slots = ep_ref.shape[0]
    per_doc = slots // DOCS
    heads = hw // HEAD_DIM
    tile = 256

    def regroup(i, _):
        lane = pl.ds(pl.multiple_of(i * 128, 128), 128)
        wide_ref[i, 0:half, :] = e_ref[0, :, lane].astype(f32)
        wide_ref[i, half : 2 * half, :] = e_ref[1, :, lane].astype(f32)
        wide_ref[i, 2 * half :, :] = jnp.zeros((slots - 2 * half, 128), f32)
        for d in range(DOCS):
            ep_ref[d * per_doc : (d + 1) * per_doc, lane] = wide_ref[
                i, pl.ds(d, per_doc, stride=DOCS), :
            ].astype(bf16)
        return 0

    lax.fori_loop(0, ep_ref.shape[1] // 128, regroup, 0)

    def frame_group(t, _):
        bias = jnp.concatenate([jnp.zeros((1, hw), f32), hb_ref[t, 3:4, :]], axis=1)

        def frames(i, _, bias=bias):
            at = pl.ds(i * tile, tile)
            y = nn(ep_ref[at, :], g2_ref[t, :, 2 * hw : 4 * hw]) + bias
            ckv_ref[t, at, :] = y.astype(bf16)
            return 0

        lax.fori_loop(0, slots // tile, frames, 0)
        return 0

    lax.fori_loop(0, groups, frame_group, 0)

    def middle(i, _):
        at = pl.ds(i * tile, tile)
        r1 = xo_ref[at, :].astype(f32) + vec_ref[6:7, :]
        for t in range(groups):
            r1 = r1 + nt(o_ref[t, at, :], g2_ref[t, :, 0:hw])
        r1_ref[at, :] = r1
        z, _ = norm_parts(r1)
        a2 = (z * vec_ref[2:3, :] + vec_ref[3:4, :]).astype(bf16)
        a2_ref[at, :] = a2
        for t in range(groups):
            cq_ref[t, at, :] = (nn(a2, g2_ref[t, :, 4 * hw : 5 * hw]) + hb_ref[t, 2:3, :]).astype(bf16)
        return 0

    lax.fori_loop(0, own // tile, middle, 0)

    acc_ref[...] = jnp.zeros_like(acc_ref)
    lse_ref[...] = jnp.zeros_like(lse_ref)
    place = lax.broadcasted_iota(jnp.int32, (per_doc, QT), 0).astype(f32)

    def attend(n, _):
        segs = segq_ref[n]
        for t in range(groups):
            spread_ref[t] = spread_heads(cq_ref[t, pl.ds(n * QT, QT), :] * bf16(SCALE))

        def document(d, _):
            col = for_heads(jnp.where(segs == d.astype(f32), 1.0, 0.0), heads)
            add = for_heads(jnp.where(place < count_ref[d], 0.0, MASKED), heads)
            for t in range(groups):
                kv = ckv_ref[t, pl.ds(d * per_doc, per_doc), :]
                scores = nt(kv[:, :hw], spread_ref[t]) + add
                top = jnp.max(scores, axis=0, keepdims=True)
                weights = jnp.exp(scores - top)
                total = jnp.sum(weights, axis=0, keepdims=True)
                mixed = tn(kv[:, hw:], weights.astype(bf16)) * (col / total)
                acc_ref[n, t] += own_blocks(mixed)
                lse_ref[t, n] += col * (top + jnp.log(total))
            return 0

        lax.fori_loop(span_ref[2 * n], span_ref[2 * n + 1] + 1, document, 0)
        for t in range(groups):
            co_ref[t, pl.ds(n * QT, QT), :] = acc_ref[n, t].T.astype(bf16)
        return 0

    lax.fori_loop(0, own // QT, attend, 0)

    def final(i, _):
        at = pl.ds(i * tile, tile)
        r2 = r1_ref[at, :] + vec_ref[7:8, :]
        for t in range(groups):
            r2 = r2 + nt(co_ref[t, at, :], g2_ref[t, :, hw : 2 * hw])
        r2_ref[at, :] = r2
        z, _ = norm_parts(r2)
        a3_ref[at, :] = (z * vec_ref[4:5, :] + vec_ref[5:6, :]).astype(bf16)
        return 0

    lax.fori_loop(0, own // tile, final, 0)


def ff_kernel(
    a3_ref, r2_ref, dy_ref, g3_ref, ub_ref, vec_ref,
    out_ref, dr2_ref, gr3_ref, ubg_ref, vecg_ref,
    a3t_ref, dmt_ref, acc_ref, acd_ref, gs_ref, dus_ref,
):
    t = pl.program_id(0)
    own, width = a3_ref.shape
    units = ub_ref.shape[2]
    tile = 256

    @pl.when(t == 0)
    def _():
        def turn(i, _):
            at = pl.ds(pl.multiple_of(i * tile, tile), tile)
            a3t_ref[:, at] = a3_ref[at, :].T
            dmt_ref[:, at] = dy_ref[at, :].T
            return 0

        lax.fori_loop(0, own // tile, turn, 0)
        acc_ref[...] = jnp.zeros_like(acc_ref)
        acd_ref[...] = jnp.zeros_like(acd_ref)

    ubg_ref[...] = jnp.zeros_like(ubg_ref)
    up = g3_ref[0, :, :units]
    down = g3_ref[0, :, units:]

    def rows(i, _):
        at = pl.ds(i * tile, tile)
        u = nn(a3_ref[at, :], up) + ub_ref[0]
        phi = 0.5 + 0.5 * lax.erf(u * (1.0 / math.sqrt(2.0)))
        g = (u * phi).astype(bf16)
        gs_ref[at, :] = g
        slope = phi + u * (jnp.exp(-0.5 * u * u) * (1.0 / math.sqrt(2.0 * math.pi)))
        du = (nn(dy_ref[at, :], down) * slope).astype(bf16)
        dus_ref[at, :] = du
        ubg_ref[0] += row_sum(du.astype(f32))
        acc_ref[at, :] += nt(g, down)
        acd_ref[at, :] += nt(du, up)
        return 0

    lax.fori_loop(0, own // tile, rows, 0)

    def grads(i, _):
        at = pl.ds(i * tile, tile)
        gr3_ref[0, at, :units] = nn(a3t_ref[at, :], dus_ref[...]).astype(bf16)
        gr3_ref[0, at, units:] = nn(dmt_ref[at, :], gs_ref[...]).astype(bf16)
        return 0

    lax.fori_loop(0, width // tile, grads, 0)

    @pl.when(t == pl.num_programs(0) - 1)
    def _():
        vecg_ref[...] = jnp.zeros_like(vecg_ref)

        def finish(i, _):
            at = pl.ds(i * tile, tile)
            r2 = r2_ref[at, :]
            dy = dy_ref[at, :].astype(f32)
            out_ref[at, :] = (r2 + (acc_ref[at, :] + vec_ref[8:9, :])).astype(bf16)
            z, rate = norm_parts(r2)
            da = acd_ref[at, :]
            dr2_ref[at, :] = dy + norm_back(z, rate, vec_ref[4:5, :], da)
            vecg_ref[0:1, :] += row_sum(da * z)
            vecg_ref[1:2, :] += row_sum(da)
            vecg_ref[2:3, :] += row_sum(dy)
            return 0

        lax.fori_loop(0, own // tile, finish, 0)


def bwd2_kernel(
    span_ref, g2_ref, ep_ref, dr2_ref, cq_ref, ckv_ref, co_ref, lse_ref, a2_ref, r1_ref, o_ref,
    vec_ref, segq_ref, count_ref,
    dr1_ref, do_ref, gr2_ref, de_ref, vecg_ref, hbg_ref,
    dco_ref, dcq_ref, dkv_ref, low_ref, rowt_ref, ept_ref, acc_ref, wide_ref, qs_ref, dos_ref, delta_ref,
):
    groups, width = g2_ref.shape[0], g2_ref.shape[1]
    own = dr2_ref.shape[0]
    hw = o_ref.shape[2]
    slots = ep_ref.shape[0]
    per_doc = slots // DOCS
    heads = hw // HEAD_DIM
    tile = 256

    vecg_ref[...] = jnp.zeros_like(vecg_ref)
    hbg_ref[...] = jnp.zeros_like(hbg_ref)

    def tile_at(i):
        return pl.ds(pl.multiple_of(i * tile, tile), tile)

    def first(i, _):
        at = tile_at(i)
        dc = dr2_ref[at, :].astype(bf16)
        vecg_ref[2:3, :] += row_sum(dc.astype(f32))
        rowt_ref[:, at] = dc.T
        for t in range(groups):
            dco_ref[t, at, :] = nn(dc, g2_ref[t, :, hw : 2 * hw]).astype(bf16)
        return 0

    lax.fori_loop(0, own // tile, first, 0)

    def output_grads(t, _):
        gr2_ref[t, :, hw : 2 * hw] = nn(rowt_ref[...], co_ref[t]).astype(bf16)
        return 0

    lax.fori_loop(0, groups, output_grads, 0)

    dkv_ref[...] = jnp.zeros_like(dkv_ref)
    place = lax.broadcasted_iota(jnp.int32, (per_doc, QT), 0).astype(f32)

    def attend(n, _):
        segs = segq_ref[n]
        mine = pl.ds(n * QT, QT)
        acc_ref[...] = jnp.zeros_like(acc_ref)
        for t in range(groups):
            qs_ref[t] = spread_heads(cq_ref[t, mine, :] * bf16(SCALE))
            dos = dco_ref[t, mine, :]
            dos_ref[t] = spread_heads(dos)
            inner = (dos.astype(f32) * co_ref[t, mine, :].astype(f32)).T
            delta_ref[t] = head_row(inner)

        def document(d, _):
            keep = (segs == d.astype(f32)) & (place < count_ref[d])
            add = for_heads(jnp.where(keep, 0.0, MASKED), heads)
            at = pl.ds(d * per_doc, per_doc)
            for t in range(groups):
                kv = ckv_ref[t, at, :]
                scores = nt(kv[:, :hw], qs_ref[t]) + add
                probs = jnp.exp(scores - lse_ref[t, n])
                grad = nt(kv[:, hw:], dos_ref[t])
                ds = (probs * (grad - delta_ref[t])).astype(bf16)
                dkv_ref[t, at, :hw] += nn(ds, qs_ref[t])
                dkv_ref[t, at, hw:] += nn(probs.astype(bf16), dos_ref[t])
                acc_ref[t] += own_blocks(tn(kv[:, :hw], ds))
            return 0

        lax.fori_loop(span_ref[2 * n], span_ref[2 * n + 1] + 1, document, 0)
        for t in range(groups):
            dcq_ref[t, mine, :] = (acc_ref[t].T * SCALE).astype(bf16)
        return 0

    lax.fori_loop(0, own // QT, attend, 0)

    def queries_back(i, _):
        at = tile_at(i)
        da = jnp.zeros((tile, width), f32)
        for t in range(groups):
            da = da + nt(dcq_ref[t, at, :], g2_ref[t, :, 4 * hw : 5 * hw])
        z, rate = norm_parts(r1_ref[at, :])
        dr1 = dr2_ref[at, :] + norm_back(z, rate, vec_ref[2:3, :], da)
        dr1_ref[at, :] = dr1
        vecg_ref[0:1, :] += row_sum(da * z)
        vecg_ref[1:2, :] += row_sum(da)
        rowt_ref[:, at] = a2_ref[at, :].T
        return 0

    lax.fori_loop(0, own // tile, queries_back, 0)

    def query_grads(t, _):
        gr2_ref[t, :, 4 * hw : 5 * hw] = nn(rowt_ref[...], dcq_ref[t]).astype(bf16)
        hbg_ref[t, 0:1, :] = row_sum(dcq_ref[t].astype(f32))
        return 0

    lax.fori_loop(0, groups, query_grads, 0)

    def self_back(i, _):
        at = tile_at(i)
        ds = dr1_ref[at, :].astype(bf16)
        vecg_ref[3:4, :] += row_sum(ds.astype(f32))
        rowt_ref[:, at] = ds.T
        for t in range(groups):
            do_ref[t, at, :] = nn(ds, g2_ref[t, :, 0:hw]).astype(bf16)
        return 0

    lax.fori_loop(0, own // tile, self_back, 0)

    def self_grads(t, _):
        gr2_ref[t, :, 0:hw] = nn(rowt_ref[...], o_ref[t]).astype(bf16)
        return 0

    lax.fori_loop(0, groups, self_grads, 0)

    def turn(i, _):
        at = tile_at(i)
        ept_ref[:, at] = ep_ref[at, :].T
        for t in range(groups):
            low = dkv_ref[t, at, :].astype(bf16)
            low_ref[t, at, :] = low
            hbg_ref[t, 1:2, :] += row_sum(low[:, hw:].astype(f32))
        return 0

    lax.fori_loop(0, slots // tile, turn, 0)

    half = width // 2
    def frame_grads(i, _):
        at = pl.ds(pl.multiple_of(4 * i * per_doc, 4 * per_doc), 4 * per_doc)
        total = jnp.zeros((4 * per_doc, width), f32)
        for t in range(groups):
            total = total + nt(low_ref[t, at, :], g2_ref[t, :, 2 * hw : 4 * hw])
        for d in range(4):
            block = total[d * per_doc : (d + 1) * per_doc]
            for j in range(width // 128):
                wide_ref[j, pl.ds(4 * i + d, per_doc, stride=DOCS), :] = block[
                    :, j * 128 : (j + 1) * 128
                ]
        return 0

    lax.fori_loop(0, DOCS // 4, frame_grads, 0)
    per_half = half // 128
    for j in range(width // 128):
        lane = slice((j % per_half) * 128, (j % per_half + 1) * 128)
        held = de_ref.shape[2]
        for h in range(de_ref.shape[1]):
            at = slice(h * held, (h + 1) * held)
            de_ref[j // per_half, h, :, lane] = wide_ref[j, at, :].astype(bf16)

    def key_grads(t, _):
        gr2_ref[t, :, 2 * hw : 4 * hw] = nn(ept_ref[...], low_ref[t]).astype(bf16)
        return 0

    lax.fori_loop(0, groups, key_grads, 0)


def bwd1_kernel(
    near_ref, xa_ref, a1_ref, g1_ref, qkv_ref, o_ref, do_ref, lse_ref, segk_ref, segq_ref,
    vecg2_ref, vecg3_ref, hbg2_ref, ubg_ref, permh_ref, permu_ref,
    da_ref, dh_ref, gr1_ref, sg_ref,
    a1t_ref, acc_ref, dk_ref, dv_ref, dq_ref, low_ref, vecg_ref, hbg_ref,
):
    t = pl.program_id(0)
    rows, width = xa_ref.shape
    own = segq_ref.shape[0] * QT
    halo = rows - own
    window = halo + QT
    hw = o_ref.shape[2]
    tile = 256

    @pl.when(t == 0)
    def _():
        def turn(i, _):
            at = pl.ds(pl.multiple_of(i * tile, tile), tile)
            a1t_ref[:, at] = a1_ref[at, :].T
            return 0

        lax.fori_loop(0, rows // tile, turn, 0)
        acc_ref[...] = jnp.zeros_like(acc_ref)
        low_ref[0:halo, 0:hw] = jnp.zeros((halo, hw), bf16)

    dk_ref[...] = jnp.zeros_like(dk_ref)
    dv_ref[...] = jnp.zeros_like(dv_ref)

    def attend_from(n, skip):
        add = window_mask(segk_ref, segq_ref, n, halo, window - skip, skip)
        at = pl.ds(n * QT + skip, window - skip)
        mine = pl.ds(n * QT, QT)
        block = qkv_ref[0, at, :]
        dos = do_ref[0, mine, :]
        heads = hw // HEAD_DIM
        delta = head_row((dos.astype(f32) * o_ref[0, mine, :].astype(f32)).T)
        dos = spread_heads(dos)
        qs = spread_heads(block[halo - skip :, :hw] * bf16(SCALE))
        scores = nt(block[:, hw : 2 * hw], qs) + for_heads(add, heads)
        probs = jnp.exp(scores - lse_ref[0, n])
        grad = nt(block[:, 2 * hw :], dos)
        ds = (probs * (grad - delta)).astype(bf16)
        dv_ref[at, :] += nn(probs.astype(bf16), dos)
        dk_ref[at, :] += nn(ds, qs)
        dq = own_blocks(tn(block[:, hw : 2 * hw], ds))
        dq_ref[mine, :] = (dq.T * SCALE).astype(bf16)

    def attend(n, _):
        near = near_ref[n] > 0
        pl.when(near)(functools.partial(attend_from, n, halo // 2))
        pl.when(jnp.logical_not(near))(functools.partial(attend_from, n, 0))
        return 0

    lax.fori_loop(0, own // QT, attend, 0)
    low_ref[halo:, 0:hw] = dq_ref[...]
    low_ref[:, hw : 2 * hw] = dk_ref[...].astype(bf16)
    low_ref[:, 2 * hw : 3 * hw] = dv_ref[...].astype(bf16)
    hbg_ref[t, 0:1, :] = row_sum(dq_ref[...].astype(f32))
    hbg_ref[t, 1:2, :] = row_sum(dv_ref[...].astype(bf16).astype(f32))
    w = g1_ref[0, :, : 3 * hw]

    def back(i, _):
        at = pl.ds(i * tile, tile)
        acc_ref[at, :] += nt(low_ref[at, :], w)
        return 0

    lax.fori_loop(0, rows // tile, back, 0)

    def grads(i, _):
        at = pl.ds(i * tile, tile)
        gr1_ref[0, at, 0 : 3 * hw] = nn(a1t_ref[at, :], low_ref[...]).astype(bf16)
        return 0

    lax.fori_loop(0, width // tile, grads, 0)

    @pl.when(t == pl.num_programs(0) - 1)
    def _():
        vecg_ref[...] = jnp.zeros_like(vecg_ref)
        dh_ref[...] = acc_ref[0:halo, :].astype(bf16)
        da_ref[...] = acc_ref[halo:, :]

        def sums(i, _):
            at = pl.ds(i * tile, tile)
            z, _ = norm_parts(xa_ref[at, :].astype(f32))
            vecg_ref[0:1, :] += row_sum(acc_ref[at, :] * z)
            vecg_ref[1:2, :] += row_sum(acc_ref[at, :])
            return 0

        lax.fori_loop(0, rows // tile, sums, 0)
        heads = hw // HEAD_DIM
        vectors = jnp.concatenate(
            [
                vecg_ref[0:2, :], vecg2_ref[0:2, :], vecg3_ref[0:2, :],
                vecg2_ref[3:4, :], vecg2_ref[2:3, :], vecg3_ref[2:3, :], jnp.zeros((7, width), f32),
            ],
            axis=0,
        ).T
        def small(g, _):
            four = (hbg_ref[g, 0:1], hbg_ref[g, 1:2], hbg2_ref[g, 0:1], hbg2_ref[g, 1:2])
            by_head = [lane_parts(row, heads) for row in four]
            by_head = jnp.concatenate(by_head + [jnp.zeros((16 - 4 * heads, HEAD_DIM), f32)], axis=0)
            by_unit = lane_parts(ubg_ref[g], heads)
            edge = jnp.zeros((4 * heads, by_unit.shape[1]), f32)
            rest = jnp.zeros((16 - 5 * heads, by_unit.shape[1]), f32)
            by_unit = jnp.concatenate([edge, by_unit, rest], axis=0)
            biases = nt(permh_ref[...], by_head.astype(bf16)) + nt(permu_ref[...], by_unit.astype(bf16))
            sg_ref[g] = jnp.concatenate(
                [vectors, biases, jnp.zeros((width, 32), f32)], axis=1
            ).astype(bf16)
            return 0

        lax.fori_loop(0, hbg2_ref.shape[0], small, 0)


def whole(shape):
    return pl.BlockSpec(shape, lambda *_: (0,) * len(shape))


def step_of(shape):
    return pl.BlockSpec((1,) + shape[1:], lambda t: (t,) + (0,) * (len(shape) - 1))


def params(dims=0):
    return pltpu.CompilerParams(
        vmem_limit_bytes=VMEM_LIMIT,
        dimension_semantics=("arbitrary",) * dims if dims else None,
    )


def cost(flops, exps, size):
    return pl.CostEstimate(flops=int(flops), transcendentals=int(exps), bytes_accessed=int(size))


def sds(shape, dtype):
    return jax.ShapeDtypeStruct(shape, dtype)

MESH_ID = pl.DeviceIdType.MESH


def place_of(chips, ctx, groups):
    f, x, z = lax.axis_index("fsdp"), lax.axis_index("ctx"), lax.axis_index("tp")
    return lax.div(f, 2), lax.rem(f, 2), x, z


def greet(chips, ctx, groups, y, c, x, z):
    barrier = pltpu.get_barrier_semaphore()
    peers = [(2 * lax.rem(y + j, chips) + c, x, z) for j in range(1, chips)]
    for dc in range(2):
        for dx in range(ctx):
            for dz in range(groups):
                if dc + dx + dz > 0:
                    other = (2 * y + lax.rem(c + dc, 2), lax.rem(x + dx, ctx), lax.rem(z + dz, groups))
                    peers.append(other)
    for peer in peers:
        pl.semaphore_signal(barrier, inc=1, device_id=peer, device_id_type=MESH_ID)
    pl.semaphore_wait(barrier, len(peers))


def gather_kernel(paths, chips, ctx, groups, *refs):
    count = len(paths)
    packs, (rows_in, frames_in, seg_in) = refs[:count], refs[count : count + 3]
    refs = refs[count + 3 :]
    fulls, (rows_out, frames_out, seg_out) = refs[:count], refs[count : count + 3]
    blank, local, zs, zr, fs, fr, ss, sr, cs, cr, xs, xr, xl, es, er, el = refs[count + 3 :]
    y, c, x, z = place_of(chips, ctx, groups)
    greet(chips, ctx, groups, y, c, x, z)
    sent = []

    def sizes(a):
        return (ctx, chips) if paths[a] == "xy" else (chips, ctx)

    def spot(a, k, i, j, core):
        t = lax.rem(z + groups - k, groups)
        dx, dy = (i, j) if paths[a] == "xy" else (j, i)
        return fulls[a].at[t, lax.rem(y + chips - dy, chips), core, lax.rem(x + ctx - dx, ctx)]

    def peer(a, first, hop):
        along_x = (paths[a] == "xy") == first
        if along_x:
            return (2 * y + c, lax.rem(x + hop, ctx), z)
        return (2 * lax.rem(y + hop, chips) + c, x, z)

    def flat(a, i, j):
        return i * sizes(a)[1] + j

    def send(src, dst, ssem, rsem, device):
        copy = pltpu.make_async_remote_copy(
            src_ref=src, dst_ref=dst, send_sem=ssem, recv_sem=rsem,
            device_id=device, device_id_type=MESH_ID,
        )
        copy.start()
        sent.append(copy)

    def arrived(dst, ssem, rsem):
        pltpu.make_async_remote_copy(
            src_ref=dst, dst_ref=dst, send_sem=ssem, recv_sem=rsem,
            device_id=(2 * y + 1 - c, x, z), device_id_type=MESH_ID,
        ).wait_recv()

    def to_core(a, k, i, j, src):
        send(src, spot(a, k, i, j, c), cs.at[a, k, flat(a, i, j)], cr.at[a, k, flat(a, i, j)], (2 * y + 1 - c, x, z))

    def second(a, k, i, src):
        for j in range(1, sizes(a)[1]):
            send(src, spot(a, k, i, 0, c), ss.at[a, k, flat(a, i, j)], sr.at[a, k, flat(a, i, j)], peer(a, False, j))

    half, low = lax.div(z, 2), lax.rem(z, 2)
    me = (2 * y + c, x, z)
    core_peer = (2 * y + 1 - c, x, z)

    def remote(src, dst, ssem, rsem, device):
        return pltpu.make_async_remote_copy(
            src_ref=src, dst_ref=dst, send_sem=ssem, recv_sem=rsem,
            device_id=device, device_id_type=MESH_ID,
        )

    blank[...] = jnp.zeros_like(blank)
    next_piece = 2 * x + c + 1
    next_exists = next_piece < 2 * ctx
    next_device = (2 * y + lax.rem(next_piece, 2), lax.rem(lax.div(next_piece, 2), ctx), z)

    def stays(b):
        return (half == c) & (2 * c + b == z)

    def to_owner(b):
        return remote(
            rows_in.at[b], rows_out.at[2 + low], xs.at[b], xr.at[2 + low], (2 * y + half, x, 2 * c + b)
        )

    def to_self(b):
        return pltpu.make_async_copy(rows_in.at[b], rows_out.at[2 + low], xl.at[2])

    def to_next(s):
        return remote(rows_out.at[2 + s], rows_out.at[s], xs.at[2 + s], xr.at[s], next_device)

    first = (x == 0) & (c == 0)

    @pl.when(first)
    def _():
        for s in range(2):
            pltpu.make_async_copy(blank, rows_out.at[s], xl.at[s]).start()

    holds = half == c

    @pl.when(holds)
    def _():
        pltpu.make_async_copy(frames_in.at[low], frames_out.at[x], el.at[0]).start()
        pltpu.make_async_copy(seg_in, seg_out, el.at[1]).start()
        remote(
            frames_in.at[low], frames_out.at[x], es.at[0], er.at[0], (2 * y + c, 1 - x, z)
        ).start()
        remote(frames_in.at[low], frames_out.at[x], es.at[1], er.at[1], core_peer).start()
        remote(seg_in, seg_out, es.at[2], er.at[2], core_peer).start()

    mine = []
    for a in range(count):
        copy = pltpu.make_async_copy(packs[a], spot(a, 0, 0, 0, c), local.at[a])
        copy.start()
        mine.append(copy)
    for k in range(1, groups):
        for a in range(count):
            send(
                packs[a], spot(a, 0, 0, 0, c), zs.at[a, k], zr.at[a, k],
                (2 * y + c, x, lax.rem(z + k, groups)),
            )
    for b in range(2):
        pl.when(jnp.logical_not(stays(b)))(to_owner(b).start)
        pl.when(stays(b))(to_self(b).start)
    for step in range(groups + 2):
        for a in range(count):
            n1, n2 = sizes(a)
            k = step
            if k < groups:
                src = packs[a] if k == 0 else spot(a, k, 0, 0, c)
                if k > 0:
                    arrived(src, zs.at[a, k], zr.at[a, k])
                for i in range(1, n1):
                    send(src, spot(a, k, 0, 0, c), fs.at[a, k, i], fr.at[a, k, i], peer(a, True, i))
                second(a, k, 0, src)
                to_core(a, k, 0, 0, src)
            k = step - 1
            if 0 <= k < groups:
                for i in range(1, n1):
                    src = spot(a, k, i, 0, c)
                    arrived(src, fs.at[a, k, i], fr.at[a, k, i])
                    second(a, k, i, src)
                    to_core(a, k, i, 0, src)
            k = step - 2
            if 0 <= k < groups:
                for i in range(n1):
                    for j in range(1, n2):
                        src = spot(a, k, i, j, c)
                        arrived(src, ss.at[a, k, flat(a, i, j)], sr.at[a, k, flat(a, i, j)])
                        to_core(a, k, i, j, src)
    for s in range(2):
        pl.when(jnp.logical_not(stays(s)))(
            remote(rows_in.at[0], rows_out.at[2 + s], xs.at[0], xr.at[2 + s], core_peer).wait_recv
        )
        pl.when(stays(s))(to_self(s).wait)
    for s in range(2):
        pl.when(next_exists)(to_next(s).start)

    far = 1 - x

    @pl.when(holds)
    def _():
        remote(frames_in.at[low], frames_out.at[far], es.at[0], er.at[0], (2 * y + c, far, z)).wait_recv()
        remote(frames_out.at[far], frames_out.at[far], es.at[3], er.at[3], core_peer).start()

    for a in range(count):
        n1, n2 = sizes(a)
        for k in range(groups):
            for i in range(n1):
                for j in range(n2):
                    arrived(spot(a, k, i, j, 1 - c), cs.at[a, k, flat(a, i, j)], cr.at[a, k, flat(a, i, j)])
    @pl.when(holds)
    def _():
        relay = remote(frames_out.at[far], frames_out.at[far], es.at[3], er.at[3], core_peer)
        remote(frames_in.at[low], frames_out.at[x], es.at[0], er.at[0], (2 * y + c, far, z)).wait_send()
        remote(frames_in.at[low], frames_out.at[x], es.at[1], er.at[1], core_peer).wait_send()
        remote(seg_in, seg_out, es.at[2], er.at[2], core_peer).wait_send()
        relay.wait_send()
        pltpu.make_async_copy(frames_in.at[low], frames_out.at[x], el.at[0]).wait()
        pltpu.make_async_copy(seg_in, seg_out, el.at[1]).wait()

    @pl.when(jnp.logical_not(holds))
    def _():
        remote(frames_in.at[low], frames_out.at[x], es.at[1], er.at[1], core_peer).wait_recv()
        remote(seg_in, seg_out, es.at[2], er.at[2], core_peer).wait_recv()
        remote(frames_out.at[far], frames_out.at[far], es.at[3], er.at[3], core_peer).wait_recv()

    for b in range(2):
        pl.when(jnp.logical_not(stays(b)))(to_owner(b).wait_send)

    @pl.when(first)
    def _():
        for s in range(2):
            pltpu.make_async_copy(blank, rows_out.at[s], xl.at[s]).wait()

    for s in range(2):
        pl.when(next_exists)(to_next(s).wait_send)
        pl.when(jnp.logical_not(first))(to_next(s).wait_recv)

    for copy in sent:
        copy.wait_send()
    for copy in mine:
        copy.wait()


def gather_packs(packs, rows, frames, segs, paths, chips, ctx, groups, collective_id):
    count = len(packs)
    side = max(chips, ctx)
    dma = pltpu.SemaphoreType.DMA
    moved = sum(p.size for p in packs) * 2 * (2 * chips * ctx * groups)
    return pl.pallas_call(
        functools.partial(gather_kernel, paths, chips, ctx, groups),
        in_specs=[pl.BlockSpec(memory_space=pltpu.VMEM)] * count
        + [pl.BlockSpec(memory_space=pl.ANY)] * 3,
        out_specs=[pl.BlockSpec(memory_space=pl.ANY)] * (count + 3),
        out_shape=[sds((groups, chips, 2, ctx) + p.shape, p.dtype) for p in packs]
        + [
            sds((4,) + rows.shape[1:], bf16),
            sds((ctx,) + frames.shape[1:], bf16),
            sds(segs.shape, f32),
        ],
        scratch_shapes=[
            pltpu.VMEM(rows.shape[1:], bf16),
            dma((count,)),
            dma((count, groups)),
            dma((count, groups)),
            dma((count, groups, side)),
            dma((count, groups, side)),
            dma((count, groups, chips * ctx)),
            dma((count, groups, chips * ctx)),
            dma((count, groups, chips * ctx)),
            dma((count, groups, chips * ctx)),
            dma((4,)),
            dma((4,)),
            dma((4,)),
            dma((4,)),
            dma((4,)),
            dma((2,)),
        ],
        compiler_params=pltpu.CompilerParams(
            collective_id=collective_id, has_side_effects=True, vmem_limit_bytes=8 * 1024 * 1024
        ),
        cost_estimate=cost(0, 0, 10 * moved),
        name="gather_packs",
    )(*packs, rows, frames, segs)


def reduce_kernel(paths, chips, ctx, groups, *refs):
    count = len(paths)
    grads, (de, dh, da, dr1, xo, gain) = refs[:count], refs[count : count + 6]
    refs = refs[count + 6 :]
    outs, (gx, ge) = refs[:count], refs[count : count + 2]
    at = count + 2
    bufs = [refs[at + 8 * a : at + 8 * a + 7] for a in range(count)]
    kept = [refs[at + 8 * a + 7] for a in range(count)]
    at = at + 8 * count
    hbuf, gbuf, rce, se, rxe, qe = refs[at : at + 6]
    cs, cr, s1, r1, s2, r2, zs, zr, hs, hr, es, er, gs, gr, gl, ks = refs[at + 6 :]
    y, c, x, z = place_of(chips, ctx, groups)
    half, low = lax.div(z, 2), lax.rem(z, 2)
    core_peer = (2 * y + 1 - c, x, z)

    def keep(a, g):
        t = lax.rem(z + 1 + g, groups)
        return pltpu.make_async_copy(grads[a].at[t, :, c], kept[a].at[t], ks.at[a, g])

    for g in range(groups):
        for a in range(count):
            keep(a, g).start()
    greet(chips, ctx, groups, y, c, x, z)
    sent = []

    def sizes(a):
        return (ctx, chips) if paths[a] == "xy" else (chips, ctx)

    def mine(a):
        return (x, y) if paths[a] == "xy" else (y, x)

    def peer(a, first, index):
        if (paths[a] == "xy") == first:
            return (2 * y + c, index, z)
        return (2 * index + c, x, z)

    def send(src, dst, ssem, rsem, device):
        copy = pltpu.make_async_remote_copy(
            src_ref=src, dst_ref=dst, send_sem=ssem, recv_sem=rsem,
            device_id=device, device_id_type=MESH_ID,
        )
        copy.start()
        sent.append(copy)

    def arrived(dst, ssem, rsem):
        pltpu.make_async_remote_copy(
            src_ref=dst, dst_ref=dst, send_sem=ssem, recv_sem=rsem,
            device_id=(2 * y + 1 - c, x, z), device_id_type=MESH_ID,
        ).wait_recv()

    def group(g):
        return lax.rem(z + 1 + g, groups)

    def remote(src, dst, ssem, rsem, device):
        return pltpu.make_async_remote_copy(
            src_ref=src, dst_ref=dst, send_sem=ssem, recv_sem=rsem,
            device_id=device, device_id_type=MESH_ID,
        )

    piece = 2 * x + c
    prev = lax.rem(piece + 2 * ctx - 1, 2 * ctx)
    prev_core, prev_x = lax.rem(prev, 2), lax.div(prev, 2)
    to_prev = remote(dh, hbuf, hs, hr, (2 * y + prev_core, prev_x, z))
    pl.when(piece > 0)(to_prev.start)

    send(de.at[1 - c], rce, es.at[0], er.at[0], core_peer)

    for g in range(groups):
        for a in range(count):
            send(
                grads[a].at[group(g), :, 1 - c], bufs[a][0].at[group(g)], cs.at[a, g], cr.at[a, g],
                (2 * y + 1 - c, x, z),
            )

    def onward(a, g, i):
        n1, _ = sizes(a)
        t, index = group(g), lax.rem(mine(a)[0] + i, n1)
        p1, b1 = bufs[a][1], bufs[a][2]
        return remote(
            p1.at[t, index], b1.at[t, i - 1], s1.at[a, g, i], r1.at[a, g, i], peer(a, True, index)
        )

    def stage1(g, _):
        t = group(g)
        for a in range(count):
            rc, p1 = bufs[a][0], bufs[a][1]
            keep(a, g).wait()
            arrived(rc.at[t], cs.at[a, g], cr.at[a, g])
            for yy in range(chips):
                for xx in range(ctx):
                    i, j = (xx, yy) if paths[a] == "xy" else (yy, xx)
                    total = kept[a][t, yy, xx].astype(f32) + rc[t, yy, xx].astype(f32)
                    p1[t, i, j] = total.astype(bf16)
            for i in range(1, sizes(a)[0]):
                onward(a, g, i).start()
        return 0

    def stage2(g):
        t = group(g)
        for a in range(count):
            p1, b1, p2, b2 = bufs[a][1:5]
            n1, n2 = sizes(a)
            for i in range(1, n1):
                arrived(b1.at[t, i - 1], s1.at[a, g, i], r1.at[a, g, i])
            for j in range(n2):
                total = p1[t, mine(a)[0], j].astype(f32)
                for i in range(1, n1):
                    total = total + b1[t, i - 1, j].astype(f32)
                p2[t, j] = total.astype(bf16)
            for j in range(1, n2):
                index = lax.rem(mine(a)[1] + j, n2)
                send(
                    p2.at[t, index], b2.at[t, j - 1], s2.at[a, g, j], r2.at[a, g, j],
                    peer(a, False, index),
                )

    def stage3(g):
        t = group(g)
        for a in range(count):
            p2, b2, p3, b3 = bufs[a][3:7]
            _, n2 = sizes(a)
            for j in range(1, n2):
                arrived(b2.at[t, j - 1], s2.at[a, g, j], r2.at[a, g, j])
            total = p2[t, mine(a)[1]].astype(f32)
            for j in range(1, n2):
                total = total + b2[t, j - 1].astype(f32)
            if g == groups - 1:
                outs[a][...] = total
            else:
                p3[g] = total.astype(bf16)
                send(p3.at[g], b3.at[g], zs.at[a, g], zr.at[a, g], (2 * y + c, x, t))

    def home(src, dst, k, s):
        stays = (half == c) & (2 * c + s == z)
        away = remote(
            src.at[s], dst.at[low], gs.at[k, s], gr.at[k, low], (2 * y + half, x, 2 * c + s)
        )
        here = pltpu.make_async_copy(src.at[s], dst.at[low], gl.at[k])
        return stays, away, here

    def go_home(src, dst, k):
        for s in range(2):
            stays, away, here = home(src, dst, k, s)
            pl.when(jnp.logical_not(stays))(away.start)
            pl.when(stays)(here.start)

    def settle(src, dst, k):
        for s in range(2):
            stays, away, here = home(src, dst, k, s)
            pl.when(jnp.logical_not(stays))(away.wait_send)
            pl.when(stays)(here.wait)
        for b in range(2):
            came = jnp.logical_not((half == c) & (2 * c + b == z))
            pl.when(came)(remote(src.at[0], dst.at[b], gs.at[k, 0], gr.at[k, b], core_peer).wait_recv)

    def frames1():
        arrived(rce, es.at[0], er.at[0])
        for h in range(ctx):
            se[h] = (de[c, h].astype(f32) + rce[h].astype(f32)).astype(bf16)
        send(se.at[1 - x], rxe, es.at[1], er.at[1], (2 * y + c, 1 - x, z))

    def frames2():
        arrived(rxe, es.at[1], er.at[1])
        total = (se[x].astype(f32) + rxe[...].astype(f32)).astype(bf16)
        quarter = qe.shape[2]
        for s in range(2):
            qe[s] = total[:, s * quarter : (s + 1) * quarter]
        go_home(qe, ge, 1)

    def rows_back():
        last = piece == 2 * ctx - 1

        @pl.when(last)
        def _():
            hbuf[...] = jnp.zeros_like(hbuf)

        @pl.when(jnp.logical_not(last))
        def _():
            remote(dh, hbuf, hs, hr, core_peer).wait_recv()

        sub = gbuf.shape[1]
        for i in range(gbuf.shape[0]):
            at = slice(i * sub, (i + 1) * sub)
            zn, rate = norm_parts(xo[at, :].astype(f32))
            total = da[at, :] + hbuf[at, :].astype(f32)
            gbuf[i] = (dr1[at, :] + norm_back(zn, rate, gain[0:1, :], total)).astype(bf16)
        go_home(gbuf, gx, 0)

    lax.fori_loop(0, groups, stage1, 0)
    frames1()
    rows_back()
    for g in range(groups + 1):
        if g < groups:
            stage2(g)
        if g > 0:
            stage3(g - 1)
        if g == 1:
            frames2()
    for a in range(count):
        b3 = bufs[a][6]
        for g in range(groups - 1):
            arrived(b3.at[g], zs.at[a, g], zr.at[a, g])
            outs[a][...] += b3[g].astype(f32)
    settle(gbuf, gx, 0)
    settle(qe, ge, 1)
    pl.when(piece > 0)(to_prev.wait_send)
    for g in range(groups):
        for a in range(count):
            for i in range(1, sizes(a)[0]):
                onward(a, g, i).wait_send()
    for copy in sent:
        copy.wait_send()


def reduce_packs(grads, de, dh, da, dr1, xo, gain, paths, chips, ctx, groups, collective_id):
    count = len(grads)
    side = max(chips, ctx)
    own, width = dr1.shape
    held = de.shape[2]
    dma = pltpu.SemaphoreType.DMA
    scratch = []
    for a in range(count):
        block = grads[a].shape[4:]
        n1, n2 = (ctx, chips) if paths[a] == "xy" else (chips, ctx)
        for lead in (
            (groups, chips, ctx), (groups, n1, n2), (groups, n1 - 1, n2), (groups, n2),
            (groups, n2 - 1), (groups - 1,), (groups - 1,), (groups, chips, ctx),
        ):
            scratch.append(pltpu.VMEM(lead + block, bf16))
    return pl.pallas_call(
        functools.partial(reduce_kernel, paths, chips, ctx, groups),
        in_specs=[pl.BlockSpec(memory_space=pl.ANY)] * count
        + [pl.BlockSpec(memory_space=pltpu.VMEM)] * 6,
        out_specs=[pl.BlockSpec(memory_space=pltpu.VMEM)] * (count + 2),
        out_shape=[sds(g.shape[4:], f32) for g in grads]
        + [
            sds((2, own // 2, width), bf16),
            sds((2, held, width // 4), bf16),
        ],
        scratch_shapes=scratch
        + [
            pltpu.VMEM((own, width), bf16),
            pltpu.VMEM((2, own // 2, width), bf16),
            pltpu.VMEM((ctx, held, width // 2), bf16),
            pltpu.VMEM((ctx, held, width // 2), bf16),
            pltpu.VMEM((held, width // 2), bf16),
            pltpu.VMEM((2, held, width // 4), bf16),
            dma((count, groups)),
            dma((count, groups)),
            dma((count, groups, side)),
            dma((count, groups, side)),
            dma((count, groups, side)),
            dma((count, groups, side)),
            dma((count, groups)),
            dma((count, groups)),
            dma(()),
            dma(()),
            dma((2,)),
            dma((2,)),
            dma((2, 2)),
            dma((2, 2)),
            dma((2,)),
            dma((count, groups)),
        ],
        compiler_params=pltpu.CompilerParams(
            collective_id=collective_id, has_side_effects=True, vmem_limit_bytes=VMEM_LIMIT
        ),
        cost_estimate=cost(0, 0, 10 * sum(g.size for g in grads)),
        name="reduce_packs",
    )(*grads, de, dh, da, dr1, xo, gain)


def prep_kernel(
    vec_ref, qb_ref, vb_ref, cqb_ref, cvb_ref, ub_ref,
    sq_ref, sk_ref, sv_ref, so_ref, cq_ref, ck_ref, cv_ref, co_ref, up_ref, down_ref,
    p1_ref, p2_ref, p3_ref, permh_ref, permu_ref,
):
    part, hw = sq_ref.shape
    units = up_ref.shape[1]

    for table, size in ((permh_ref, qb_ref.shape[1]), (permu_ref, ub_ref.shape[1])):
        row = lax.broadcasted_iota(jnp.int32, table.shape, 0).astype(f32)
        column = lax.broadcasted_iota(jnp.int32, table.shape, 1).astype(f32)
        owner = jnp.floor((row + 0.5) * (1.0 / part))
        local = row - owner * part
        hit = (local < size) & (owner * size + local == column)
        table[...] = jnp.where(hit, 1.0, 0.0).astype(bf16)

    def padded(rows):
        rows = rows.astype(f32)
        return jnp.concatenate([rows, jnp.zeros((rows.shape[0], part - rows.shape[1]), f32)], axis=1)

    rows = [vec_ref[...], jnp.zeros((16 - vec_ref.shape[0], part), f32)]
    rows += [padded(r[...]) for r in (qb_ref, vb_ref, cqb_ref, cvb_ref, ub_ref)]
    rows.append(jnp.zeros((64 - sum(r.shape[0] for r in rows), part), f32))
    small = jnp.concatenate(rows, axis=0).T.astype(bf16)
    p1_ref[...] = jnp.concatenate([sq_ref[...], sk_ref[...], sv_ref[...], small], axis=1)
    p2_ref[...] = jnp.concatenate(
        [
            so_ref[...].T, co_ref[...].T, ck_ref[...], cv_ref[...], cq_ref[...],
            jnp.zeros((part, 64), bf16),
        ],
        axis=1,
    )
    p3_ref[:, :units] = up_ref[...]
    p3_ref[:, units:] = down_ref[...].T


def lane_parts(row, count):
    size = row.shape[1] // count
    return jnp.concatenate([row[:, i * size : (i + 1) * size] for i in range(count)], axis=0)


def row_parts(matrix, first, count):
    return jnp.concatenate([matrix[first + i : first + i + 1] for i in range(count)], axis=1)


def on_device(
    hidden_in, encoder_states, segment_ids, out_grad,
    norm1_gain, norm1_bias, norm2_gain, norm2_bias, norm3_gain, norm3_bias,
    self_query, self_key, self_value, self_output,
    cross_query, cross_key, cross_value, cross_output,
    fc_up, fc_down,
    self_query_bias, self_value_bias, cross_query_bias, cross_value_bias, up_bias,
    self_output_bias, cross_output_bias, down_bias,
):
    F, C, T = lax.axis_size("fsdp"), lax.axis_size("ctx"), lax.axis_size("tp")
    batches, sub, width = hidden_in.shape
    length = segment_ids.shape[1]
    frames_own = encoder_states.shape[1]
    assert T == 2 * batches and T == 4 and F % 2 == 0 and C == 2
    own = 2 * sub
    part = width // (F * C)
    hw = self_query.shape[1]
    units = fc_up.shape[1]
    heads = self_query_bias.shape[0]
    f, x, z = lax.axis_index("fsdp"), lax.axis_index("ctx"), lax.axis_index("tp")
    core = lax.rem(f, 2)
    odd = lax.rem(z, 2)
    tfc = ("tp", "fsdp", "ctx")

    def round_pairs(r):
        pairs = []
        for m in range(F // 2):
            for c in range(2):
                for zz in range(T):
                    b = (r + zz) % 2
                    pairs.append(((2 * m + c) * T + zz, (2 * m + zz // 2) * T + 2 * c + b))
        return pairs

    rounds = [round_pairs(0), round_pairs(1)]
    axes = ("fsdp", "tp")

    def pick(values, index):
        return lax.dynamic_index_in_dim(values, index, 0, keepdims=False)

    def spread(values):
        first = lax.ppermute(pick(values, odd), axes, rounds[0])
        second = lax.ppermute(pick(values, 1 - odd), axes, rounds[1])
        even = odd == 0
        return jnp.concatenate(
            [jnp.where(even, first, second), jnp.where(even, second, first)], axis=0
        )

    vecs = (
        norm1_gain, norm1_bias, norm2_gain, norm2_bias, norm3_gain, norm3_bias,
        self_output_bias, cross_output_bias, down_bias,
    )
    per, wide = self_query_bias.shape[1], up_bias.shape[1]
    vm = pl.BlockSpec(memory_space=pltpu.VMEM)
    pack1, pack2, pack3, permh, permu = pl.pallas_call(
        prep_kernel,
        in_specs=[vm] * 16,
        out_specs=[vm] * 5,
        out_shape=[
            sds((part, 3 * hw + 64), bf16),
            sds((part, 5 * hw + 64), bf16),
            sds((part, 2 * units), bf16),
            sds((width, F * C * per), bf16),
            sds((width, F * C * wide), bf16),
        ],
        compiler_params=params(),
        cost_estimate=cost(0, 0, 4 * part * (8 * hw + 2 * units)),
        name="prep",
    )(
        jnp.stack([v.astype(f32) for v in vecs]),
        self_query_bias, self_value_bias, cross_query_bias, cross_value_bias, up_bias,
        self_query, self_key, self_value, self_output,
        cross_query, cross_key, cross_value, cross_output, fc_up, fc_down,
    )

    def gather(block):
        full = lax.all_gather(block, tfc, axis=0, tiled=True)
        return full.reshape(T, width, block.shape[1])

    chips = F // 2
    g1, g2, xa, frames, seg_row = gather_packs(
        (pack1, pack2), hidden_in, encoder_states, segment_ids.astype(f32),
        ("yx", "xy"), chips, C, T, 0,
    )
    g1 = g1.reshape(T, width, pack1.shape[1])
    g2 = g2.reshape(T, width, pack2.shape[1])
    xa = xa.reshape(2 * own, width)
    xo = xa[own:]
    seg_row = pick(seg_row, odd)

    piece = x * 2 + core
    seg_own = lax.dynamic_slice_in_dim(seg_row, piece * own, own)
    seg_halo = lax.dynamic_slice_in_dim(seg_row, jnp.maximum(piece - 1, 0) * own, own)
    seg_halo = jnp.where(piece == 0, -1.0, seg_halo)
    segk = jnp.concatenate([seg_halo, seg_own]).reshape(2 * own, 1)
    segq = seg_own.reshape(own // QT, 1, QT)
    ends = seg_own.reshape(own // QT, QT)
    span = jnp.stack([ends[:, 0], ends[:, -1]], axis=1).reshape(-1).astype(jnp.int32)

    frames_all = 2 * frames_own
    per_doc = -(-frames_all // (DOCS * 32)) * 32
    slots = DOCS * per_doc
    counts = jnp.asarray([float(-(-(frames_all - d) // DOCS)) for d in range(DOCS)], f32)

    out_grad, pack3, g1 = lax.optimization_barrier((out_grad, pack3, g1))
    g3 = gather(pack3)
    dy = spread(out_grad)

    nq = own // QT
    smem = pl.BlockSpec(memory_space=pltpu.SMEM)
    seg_all = jnp.concatenate([seg_halo, seg_own])
    reach = seg_all[own // 2 - 1 : 2 * own - 1].reshape(-1)[: nq * QT].reshape(nq, QT)[:, 0]
    near = (reach != ends[:, 0]).astype(jnp.int32)
    a1, qkv, o, lse1, vec_all, hb_all, ub_all = pl.pallas_call(
        fwd1_kernel,
        grid=(T,),
        in_specs=[
            smem,
            whole((2 * own, width)),
            step_of(g1.shape),
            whole(permh.shape),
            whole(permu.shape),
            whole((2 * own, 1)),
            whole((nq, 1, QT)),
        ],
        out_specs=[
            whole((2 * own, width)),
            step_of((T, 2 * own, 3 * hw)),
            step_of((T, own, hw)),
            step_of((T, nq, 1, heads * QT)),
            whole((16, width)),
            step_of((T, 8, hw)),
            step_of((T, 1, units)),
        ],
        out_shape=[
            sds((2 * own, width), bf16),
            sds((T, 2 * own, 3 * hw), bf16),
            sds((T, own, hw), bf16),
            sds((T, nq, 1, heads * QT), f32),
            sds((16, width), f32),
            sds((T, 8, hw), f32),
            sds((T, 1, units), f32),
        ],
        compiler_params=params(1),
        cost_estimate=cost(2 * 2 * own * width * 3 * hw * T + 4 * own * (own + QT) * hw * T, own * (own + QT) * heads * T, 2 * g1.size + 12 * own * width),
        name="fwd1",
    )(near, xa, g1, permh, permu, segk, segq)

    ckv, r1, a2, cq, co, lse2, r2, a3, ep = pl.pallas_call(
        fwd2_kernel,
        in_specs=[smem] + [vm] * 7 + [smem],
        out_specs=[vm] * 9,
        out_shape=[
            sds((T, slots, 2 * hw), bf16),
            sds((own, width), f32),
            sds((own, width), bf16),
            sds((T, own, hw), bf16),
            sds((T, own, hw), bf16),
            sds((T, nq, 1, heads * QT), f32),
            sds((own, width), f32),
            sds((own, width), bf16),
            sds((slots, width), bf16),
        ],
        scratch_shapes=[
            pltpu.VMEM((nq, T, hw, QT), f32),
            pltpu.VMEM((width // 128, slots, 128), f32),
            pltpu.VMEM((T, heads * QT, hw), bf16),
        ],
        compiler_params=params(),
        cost_estimate=cost(2 * (2 * slots + 3 * own) * width * hw * T + 4 * own * slots * hw, own * per_doc * heads * T, 2 * g2.size + 20 * own * width),
        name="fwd2",
    )(
        span, g2, frames, xo, o, vec_all, hb_all, segq, counts,
    )

    out_rows, dr2, gr3, ubg, vecg3 = pl.pallas_call(
        ff_kernel,
        grid=(T,),
        in_specs=[
            whole((own, width)),
            whole((own, width)),
            whole((own, width)),
            step_of(g3.shape),
            step_of((T, 1, units)),
            whole((16, width)),
        ],
        out_specs=[
            whole((own, width)),
            whole((own, width)),
            step_of(g3.shape),
            step_of((T, 1, units)),
            whole((8, width)),
        ],
        out_shape=[
            sds((own, width), bf16),
            sds((own, width), f32),
            sds(g3.shape, bf16),
            sds((T, 1, units), f32),
            sds((8, width), f32),
        ],
        scratch_shapes=[
            pltpu.VMEM((width, own), bf16),
            pltpu.VMEM((width, own), bf16),
            pltpu.VMEM((own, width), f32),
            pltpu.VMEM((own, width), f32),
            pltpu.VMEM((own, units), bf16),
            pltpu.VMEM((own, units), bf16),
        ],
        compiler_params=params(1),
        cost_estimate=cost(12 * own * width * units * T, 2 * own * units * T, 4 * g3.size + 12 * own * width),
        name="ff",
    )(a3, r2, dy, g3, ub_all, vec_all)

    def scatter(block):
        return lax.psum_scatter(
            block.reshape(T * width, block.shape[2]), tfc, scatter_dimension=0, tiled=True
        )

    sum3 = scatter(gr3)
    backs = [[(d, s) for s, d in pairs] for pairs in rounds]
    out_rows = out_rows.reshape(2, sub, width)
    back0 = lax.ppermute(pick(out_rows, odd), axes, backs[0])
    back1 = lax.ppermute(pick(out_rows, 1 - odd), axes, backs[1])

    dr1, do, gr2, de, vecg2, hbg2 = pl.pallas_call(
        bwd2_kernel,
        in_specs=[smem] + [vm] * 12 + [smem],
        out_specs=[vm] * 6,
        out_shape=[
            sds((own, width), f32),
            sds((T, own, hw), bf16),
            sds(g2.shape, bf16),
            sds((2, C, frames_own, width // 2), bf16),
            sds((8, width), f32),
            sds((T, 8, hw), f32),
        ],
        scratch_shapes=[
            pltpu.VMEM((T, own, hw), bf16),
            pltpu.VMEM((T, own, hw), bf16),
            pltpu.VMEM((T, slots, 2 * hw), f32),
            pltpu.VMEM((T, slots, 2 * hw), bf16),
            pltpu.VMEM((width, own), bf16),
            pltpu.VMEM((width, slots), bf16),
            pltpu.VMEM((T, hw, QT), f32),
            pltpu.VMEM((width // 128, slots, 128), f32),
            pltpu.VMEM((T, heads * QT, hw), bf16),
            pltpu.VMEM((T, heads * QT, hw), bf16),
            pltpu.VMEM((T, 1, heads * QT), f32),
        ],
        compiler_params=params(),
        cost_estimate=cost(2 * (4 * slots + 6 * own) * width * hw * T + 10 * own * slots * hw, own * per_doc * heads * T, 4 * g2.size + 30 * own * width),
        name="bwd2",
    )(span, g2, ep, dr2, cq, ckv, co, lse2, a2, r1, o, vec_all, segq, counts)

    do, back0, back1 = lax.optimization_barrier((do, back0, back1))
    even = odd == 0
    out_final = jnp.stack([jnp.where(even, back0, back1), jnp.where(even, back1, back0)])

    da, dh, gr1, sg = pl.pallas_call(
        bwd1_kernel,
        grid=(T,),
        in_specs=[
            smem,
            whole((2 * own, width)),
            whole((2 * own, width)),
            step_of(g1.shape),
            step_of(qkv.shape),
            step_of(o.shape),
            step_of(do.shape),
            step_of(lse1.shape),
            whole((2 * own, 1)),
            whole((nq, 1, QT)),
            whole((8, width)),
            whole((8, width)),
            whole((T, 8, hw)),
            whole((T, 1, units)),
            whole(permh.shape),
            whole(permu.shape),
        ],
        out_specs=[
            whole((own, width)),
            whole((own, width)),
            step_of((T, width, 3 * hw)),
            whole((T, width, 64)),
        ],
        out_shape=[
            sds((own, width), f32),
            sds((own, width), bf16),
            sds((T, width, 3 * hw), bf16),
            sds((T, width, 64), bf16),
        ],
        scratch_shapes=[
            pltpu.VMEM((width, 2 * own), bf16),
            pltpu.VMEM((2 * own, width), f32),
            pltpu.VMEM((2 * own, hw), f32),
            pltpu.VMEM((2 * own, hw), f32),
            pltpu.VMEM((own, hw), bf16),
            pltpu.VMEM((2 * own, 3 * hw), bf16),
            pltpu.VMEM((8, width), f32),
            pltpu.VMEM((T, 8, hw), f32),
        ],
        compiler_params=params(1),
        cost_estimate=cost(2 * 4 * own * width * 3 * hw * T + 10 * own * (own + QT) * hw * T, own * (own + QT) * heads * T, 4 * g1.size + 30 * own * width),
        name="bwd1",
    )(
        near, xa, a1, g1, qkv, o, do, lse1, segk, segq, vecg2, vecg3, hbg2, ubg, permh, permu,
    )

    split = (T, chips, 2, C, part)
    sum1, sum2, sums, grad_hidden, grad_encoder = reduce_packs(
        tuple(g.reshape(split + g.shape[2:]) for g in (gr1, gr2, sg)),
        de, dh, da, dr1, xo, vec_all,
        ("xy", "yx", "xy"), chips, C, T, 1,
    )
    grad_hidden = grad_hidden.astype(f32)
    grad_encoder = grad_encoder.astype(f32)

    sum3 = sum3.astype(f32)
    third = part // T
    vout = lax.dynamic_slice_in_dim(sums[:, :16], z * third, third).T
    hout = sums[:per, 16 : 16 + 4 * heads].T.reshape(4, heads, per)
    uout = sums[:wide, 16 + 4 * heads : 16 + 5 * heads].T

    def cut(array, k):
        return array[:, k * hw : (k + 1) * hw]

    return (
        out_final,
        grad_hidden,
        grad_encoder,
        vout[0], vout[1], vout[2], vout[3], vout[4], vout[5],
        cut(sum1, 0), cut(sum1, 1), cut(sum1, 2), cut(sum2, 0).T,
        cut(sum2, 4), cut(sum2, 2), cut(sum2, 3), cut(sum2, 1).T,
        sum3[:, :units], sum3[:, units:].T,
        hout[0], hout[1], hout[2], hout[3], uout,
        vout[6], vout[7], vout[8],
    )


def solution(mesh):
    column = P(("fsdp", "ctx"), "tp")
    row = P("tp", ("fsdp", "ctx"))
    vector = P(("fsdp", "ctx"))
    vector_out = P(("fsdp", "ctx", "tp"))
    tokens = P("fsdp", ("ctx", "tp"), None)
    return jax.shard_map(
        on_device,
        mesh=mesh,
        in_specs=(tokens, P("fsdp", "ctx", None), P("fsdp", None), tokens)
        + (vector,) * 6
        + (column, column, column, row)
        + (column, column, column, row)
        + (column, row)
        + (row,) * 5
        + (vector,) * 3,
        out_specs=(tokens, tokens, P("fsdp", "ctx", "tp"))
        + (vector_out,) * 6
        + (column, column, column, row)
        + (column, column, column, row)
        + (column, row)
        + (row,) * 5
        + (vector_out,) * 3,
        check_vma=False,
    )
```
